256 devices in a mesh: pts: 4 (over y_hi, core), ctr: 64 (over x, z, y_lo).
Axes of the slice: x: 4, y: 4 (y_hi: 2, y_lo: 2; y = y_hi * 2 + y_lo), z: 8, core: 2. Of those that a mesh axis runs over, the one named last changes fastest.
Arguments:
- points: bfloat16 [4096, 512], P(('pts', 'ctr')), may hold values from -6 to 6
- point_class: int32 [4096], P(('pts', 'ctr')), may hold values from 0 to 7
- targets: float32 [4096, 128], P(('pts', 'ctr')), may hold values from -6 to 6
- class_weight: float32 [8], replicated, may hold values from 0.25 to 4
- inv_scale: float32 [512], replicated, may hold values from 0.003 to 0.3
- centers: bfloat16 [262144, 512], P('ctr'), may hold values from -6 to 6
- coefficients: bfloat16 [262144, 128], P('ctr'), may hold values from -2.5 to 2.5
- center_index: int32 [4096], replicated, may hold values from 0 to 262143, as said below
- factor: float32 [4096, 4096], P('ctr'), as said below
- panel_inverse: float32 [4096, 2048], P('ctr'), as said below
Outputs:
- gradient: float32 [262144, 128], P('ctr', 'pts')
- solved: float32 [4096, 128], P('ctr', 'pts')
The draws below stay inside these ranges and needn't reach their ends.
Inputs may be any that keep to these rules, and one draw needn't show every extreme that they name: `center_index`: the values are distinct; window row r lies in the center shard (index of ctr, 4096 centers each) numbered order[r mod 64] for one permutation order of the shards, so each shard holds exactly 64 window rows and the 64 rows of each aligned block of the window hold at most 1 of one shard's centers, a bound that is reached. factor is lower triangular with its diagonal between 1 and 2. `panel_inverse`: the rows of panel p hold the inverse of factor's diagonal block of rows and columns p * 2048 to (p + 1) * 2048 - 1.
All inputs are finite; a program needn't handle non-finite values.
Results may differ from the reference program's by a relative error of at most 0.0055.
Values may be sent and summed in bfloat16 or wider, within the bound.
No kernel may reach another device: no remote copies, remote signals or barrier semaphores. Data moves between devices by JAX's collectives and lax.ppermute only.
A program may use at most 64 MiB of HBM per device.

```python
import math
import jax
import jax.numpy as jnp
from jax import lax

D = 512
TARGETS = 128
CLASSES = 8
CTR_DEV = 4096
PANEL = 2048
PANELS = 2
NPTS = 4096
CENTERS = 262144
WIN = 4096
N_CTR = 64


def factor_matrix(key):
    folded = jax.random.fold_in(key, 11)
    strict_key, diagonal_key = jax.random.split(folded)
    strict = jnp.tril(jax.random.normal(strict_key, (WIN, WIN), jnp.float32), -1) * (0.6 / math.sqrt(WIN))
    diagonal = jax.random.uniform(diagonal_key, (WIN,), jnp.float32, 1.0, 2.0)
    return strict + jnp.diag(diagonal)


def draw_factor(key, part):
    return factor_matrix(key)


def draw_panel_inverse(key, part):
    matrix = factor_matrix(key)
    identity = jnp.eye(PANEL, dtype=jnp.float32)
    blocks = []
    for current in range(PANELS):
        begin = current * PANEL
        diagonal_block = matrix[begin:begin + PANEL, begin:begin + PANEL]
        blocks.append(jax.scipy.linalg.solve_triangular(diagonal_block, identity, lower=True))
    return jnp.concatenate(blocks, axis=0)


def draw_center_index(key, part):
    folded = jax.random.fold_in(key, 5)
    order_key, offset_key = jax.random.split(folded)
    shard_order = jax.random.permutation(order_key, N_CTR).astype(jnp.int32)
    rows = jnp.arange(WIN, dtype=jnp.int32)
    shard = shard_order[rows % N_CTR]
    occurrence = rows // N_CTR
    offset_keys = jax.random.split(offset_key, N_CTR)
    offsets = jax.vmap(lambda single: jax.random.permutation(single, CTR_DEV).astype(jnp.int32))(offset_keys)
    return (shard * CTR_DEV + offsets[shard, occurrence]).astype(jnp.int32)


def set_ends(drawn, key, least, top_value):
    spot = [jax.random.randint(jax.random.fold_in(key, axis), (), 0, length) for axis, length in enumerate(drawn.shape)]
    main_axis = drawn.shape.index(max(drawn.shape))
    beside = spot[:main_axis] + [(spot[main_axis] + 1) % drawn.shape[main_axis]] + spot[main_axis + 1:]
    return drawn.at[tuple(spot)].set(least).at[tuple(beside)].set(top_value)


def shard_levels(rng, dims, pieces, smallest, top_value):
    level = 1.0
    for position, parts in pieces:
        draws = jax.random.uniform(jax.random.fold_in(jax.random.fold_in(rng, 6), position), (parts,), jnp.float32, smallest / len(pieces), top_value / len(pieces))
        level = level * jnp.repeat(jnp.exp(draws), dims[position] // parts).reshape((-1,) + (1,) * (len(dims) - 1 - position))
    return level


def noise(key, shape, scale, most, pieces=(), held_as=jnp.bfloat16):
    gain = shard_levels(key, shape, pieces, -0.22, 0.18) if pieces else 1.0
    entries = jax.random.normal(key, shape, jnp.float32) * scale * gain
    return jnp.minimum(jnp.maximum(entries, -most), most).astype(held_as)


def setup_inputs(seed: int = 0) -> dict:
    streams_of = jax.random.split(jax.random.key(seed), 11)
    points = noise(streams_of[0], (NPTS, D), 1.0, 6.0, ((0, 256),))
    point_class = set_ends(jax.random.randint(streams_of[1], (NPTS,), 0, CLASSES), jax.random.fold_in(streams_of[1], 1), 0, CLASSES - 1).astype(jnp.int32)
    targets = noise(streams_of[2], (NPTS, TARGETS), 1.0, 6.0, ((0, 256),), jnp.float32)
    class_weight = jnp.clip(jnp.exp(jax.random.uniform(streams_of[3], (CLASSES,), jnp.float32, math.log(0.25), math.log(4.0))), 0.25, 4.0)
    inv_scale = jnp.clip(jnp.exp(jax.random.uniform(streams_of[4], (D,), jnp.float32, math.log(0.003), math.log(0.3))), 0.003, 0.3)
    centers = noise(streams_of[5], (CENTERS, D), 1.0, 6.0, ((0, 64),))
    coefficients = noise(streams_of[6], (CENTERS, TARGETS), 0.35, 2.5, ((0, 64),))
    center_index = draw_center_index(jax.random.fold_in(streams_of[10], 71), 0)
    factor = draw_factor(jax.random.fold_in(streams_of[10], 71), 0)
    panel_inverse = draw_panel_inverse(jax.random.fold_in(streams_of[10], 71), 0)
    return dict(points=points, point_class=point_class, targets=targets, class_weight=class_weight, inv_scale=inv_scale, centers=centers, coefficients=coefficients, center_index=center_index, factor=factor, panel_inverse=panel_inverse)


def gaussian(samples, anchors):
    products = lax.dot_general(samples.astype(jnp.float32), anchors.astype(jnp.float32), (((1,), (1,)), ((), ())), preferred_element_type=jnp.float32)
    left_norm = jnp.sum(jnp.square(samples.astype(jnp.float32)), axis=1)
    right_norm = jnp.sum(jnp.square(anchors.astype(jnp.float32)), axis=1)
    exponent = products - 0.5 * left_norm[:, None] - 0.5 * right_norm[None, :]
    return jnp.exp(exponent).astype(jnp.bfloat16)

def class_lookup(labels, table):
    classes = jnp.arange(table.shape[0], dtype=jnp.int32)
    return jnp.sum(jnp.where(labels[:, None] == classes[None, :], table[None, :], 0.0), axis=1)

def reference(points, point_class, targets, class_weight, inv_scale, centers, coefficients, center_index, factor, panel_inverse):
    scaled_points = (points.astype(jnp.float32) * inv_scale[None, :]).astype(jnp.bfloat16)
    scaled_centers = (centers.astype(jnp.float32) * inv_scale[None, :]).astype(jnp.bfloat16)
    center_blocks = scaled_centers.reshape(N_CTR, CTR_DEV, D)
    coef_blocks = coefficients.reshape(N_CTR, CTR_DEV, TARGETS)

    def accumulate(running, inputs):
        center_block, coef_block = inputs
        kernel = gaussian(scaled_points, center_block)
        return (running + jnp.dot(kernel.astype(jnp.float32), coef_block.astype(jnp.float32), preferred_element_type=jnp.float32), None)
    predicted, unused = lax.scan(accumulate, jnp.zeros((NPTS, TARGETS), jnp.float32), (center_blocks, coef_blocks))
    weight = class_lookup(point_class, class_weight)
    residual = (weight[:, None] * (predicted - targets)).astype(jnp.bfloat16)

    def backward(center_block):
        kernel = gaussian(scaled_points, center_block)
        return lax.dot_general(kernel.astype(jnp.float32), residual.astype(jnp.float32), (((0,), (0,)), ((), ())), preferred_element_type=jnp.float32)
    gradient = lax.map(backward, center_blocks).reshape(CENTERS, TARGETS)
    window = gradient[center_index]
    solved_full = jnp.zeros((WIN, TARGETS), jnp.float32)
    for current in range(PANELS):
        begin = current * PANEL
        rhs_part = window[begin:begin + PANEL]
        if current > 0:
            rhs_part = rhs_part - jnp.dot(factor[begin:begin + PANEL], solved_full, precision=lax.Precision.HIGHEST)
        panel_part = jnp.dot(panel_inverse[begin:begin + PANEL], rhs_part, precision=lax.Precision.HIGHEST)
        solved_full = solved_full.at[begin:begin + PANEL].set(panel_part)
    return (gradient, solved_full)
```

```python
import jax
import jax.numpy as jnp
from jax import lax
from jax.sharding import PartitionSpec as P

BF = jnp.bfloat16
F32 = jnp.float32
HI = lax.Precision.HIGHEST
LANES = 128


def gathered(x, axis):
    count = lax.axis_size(axis)
    return lax.all_to_all(jnp.broadcast_to(x[None], (count, *x.shape)), axis, 0, 0, tiled=True)


def half_norm(rows):
    return 0.5 * jnp.sum(jnp.square(rows.astype(F32)), axis=1)


def gaussian(samples, anchors, left, right):
    products = lax.dot_general(
        samples, anchors, (((1,), (1,)), ((), ())), preferred_element_type=F32
    )
    return jnp.exp(products - left[:, None] - right[None, :]).astype(BF)


def class_lookup(labels, table):
    classes = jnp.arange(table.shape[0], dtype=jnp.int32)
    return jnp.sum(jnp.where(labels[:, None] == classes[None, :], table[None, :], 0.0), axis=1)


def side_by_side(x, count):
    rows = x.shape[0] // count
    return jnp.concatenate([x[i * rows : (i + 1) * rows] for i in range(count)], axis=1)


def diagonal_sum(x, count):
    rows, cols = x.shape[0] // count, x.shape[1] // count
    total = x[:rows, :cols]
    for i in range(1, count):
        total = total + x[i * rows : (i + 1) * rows, i * cols : (i + 1) * cols]
    return total


def body(
    points,
    point_class,
    targets,
    class_weight,
    inv_scale,
    centers,
    coefficients,
    center_index,
    factor,
    panel_inverse,
):
    groups = lax.axis_size("pts")
    shards = lax.axis_size("ctr")
    shard = lax.axis_index("ctr")
    own_points, depth = points.shape
    shard_rows = centers.shape[0]
    target_count = targets.shape[1]
    target_slice = target_count // groups
    window_rows = center_index.shape[0]
    own_rows = window_rows // shards
    panel_rows = panel_inverse.shape[1]
    panel_shards = panel_rows // own_rows
    panel = shard // panel_shards
    fold = LANES // target_slice
    strip = own_rows // fold

    own_scaled = (points.astype(F32) * inv_scale[None, :]).astype(BF)
    group_rows = gathered(own_scaled, "ctr").reshape(shards * own_points, depth)

    scaled_centers = (centers.astype(F32) * inv_scale[None, :]).astype(BF)
    center_norm = half_norm(scaled_centers)

    blocks = center_index.reshape(own_rows, shards)
    order = blocks[0] // shard_rows
    here = order == shard
    local = jnp.sum(jnp.where(here[None, :], blocks - shard * shard_rows, 0), axis=1)
    choose = (local[:, None] == jnp.arange(shard_rows, dtype=jnp.int32)[None, :]).astype(BF)
    chosen = jnp.dot(choose, scaled_centers, preferred_element_type=F32).astype(BF)
    chosen_norm = half_norm(chosen)
    place = (order[:, None] == jnp.arange(shards, dtype=jnp.int32)[None, :]).astype(F32)

    halves = panel_rows // (strip * shards)
    inverse = panel_inverse.reshape(own_rows, halves, strip, shards)
    inverse_window = jnp.einsum("rhqj,js->hrsq", inverse, place, precision=HI)
    inverse_window = inverse_window.reshape(halves, own_rows, shards * strip)
    parts = []
    for i in range(fold):
        parts.append(jnp.where(panel == i // halves, inverse_window[i % halves], 0.0))
    inverse_window = jnp.concatenate(parts, axis=0)

    def folded(matrix):
        m = matrix.reshape(own_rows, panel_shards, fold, strip)
        return m.transpose(2, 0, 1, 3).reshape(fold * own_rows, panel_shards * strip)

    factor_rows = folded(factor[:, :panel_rows])
    inverse_rows = folded(panel_inverse)

    point_norm = half_norm(group_rows)
    kernel = gaussian(group_rows, scaled_centers, point_norm, center_norm)
    chosen_kernel = gaussian(group_rows, chosen, point_norm, chosen_norm)
    partial_value = jnp.dot(kernel, coefficients, preferred_element_type=F32).astype(BF)
    own_weight = class_lookup(point_class, class_weight)
    shares = lax.all_to_all(
        partial_value.reshape(shards, own_points, target_count), "ctr", 0, 0, tiled=True
    )
    predicted = jnp.sum(shares.astype(F32), axis=0)
    own_residual = (own_weight[:, None] * (predicted - targets)).astype(BF)
    residual = gathered(own_residual, "ctr").reshape(shards * own_points, target_count)

    window = lax.dot_general(
        chosen_kernel, residual, (((0,), (0,)), ((), ())), preferred_element_type=F32
    )
    pieces = jnp.stack(
        [
            side_by_side(window[:, i * target_slice : (i + 1) * target_slice], fold)
            for i in range(groups)
        ]
    )
    pieces = lax.all_to_all(pieces, "pts", 0, 0, tiled=True)
    window = jnp.sum(pieces, axis=0).astype(BF)
    window = gathered(window, "ctr").reshape(shards * strip, LANES)

    backward = lax.dot_general(
        residual, kernel, (((0,), (0,)), ((), ())), preferred_element_type=F32
    ).astype(BF)
    backward = lax.all_to_all(
        backward.reshape(groups, target_slice, shard_rows), "pts", 0, 0, tiled=True
    )
    gradient = jnp.sum(backward.astype(F32), axis=0).T

    base = diagonal_sum(jnp.dot(inverse_window, window.astype(F32), precision=HI), fold)
    first = gathered(side_by_side(base, fold).astype(BF), "ctr")
    first = first[:panel_shards].reshape(panel_shards * strip, LANES)
    update = diagonal_sum(jnp.dot(factor_rows, first.astype(F32), precision=HI), fold)
    second = gathered(side_by_side(update, fold).astype(BF), "ctr")
    second = second[panel_shards:].reshape(panel_shards * strip, LANES)
    change = diagonal_sum(jnp.dot(inverse_rows, second.astype(F32), precision=HI), fold)
    solved = base - jnp.where(panel == 1, change, 0.0)
    return (gradient, solved)


def solution(mesh):
    placed = (
        P(("pts", "ctr"), None),
        P(("pts", "ctr")),
        P(("pts", "ctr"), None),
        P(),
        P(),
        P("ctr", None),
        P("ctr", None),
        P(),
        P("ctr", None),
        P("ctr", None),
    )
    return jax.shard_map(
        body,
        mesh=mesh,
        in_specs=placed,
        out_specs=(P("ctr", "pts"), P("ctr", "pts")),
        check_vma=False,
    )
```

```python
import jax
import jax.numpy as jnp
from jax import lax
from jax.experimental import pallas as pl
from jax.experimental.pallas import tpu as pltpu
from jax.sharding import PartitionSpec as P

BF = jnp.bfloat16
F32 = jnp.float32
HI = lax.Precision.HIGHEST
LANES = 128


PLANES = 4
TILE = 512


def gathered(x, axis):
    count = lax.axis_size(axis)
    return lax.all_to_all(jnp.broadcast_to(x[None], (count, *x.shape)), axis, 0, 0, tiled=True)


def plane_groups(axis):
    size = lax.axis_size(axis) // PLANES
    return [[plane * size + i for i in range(size)] for plane in range(PLANES)]


def plane_exchange(pieces, axis):
    groups = plane_groups(axis)
    return lax.all_to_all(pieces, axis, 0, 0, tiled=True, axis_index_groups=groups)


def plane_gathered(x, axis):
    size = lax.axis_size(axis) // PLANES
    return plane_exchange(jnp.broadcast_to(x[None], (size, *x.shape)), axis)


def swapped(x, axis, bits):
    return lax.ppermute(x, axis, [(i, i ^ bits) for i in range(lax.axis_size(axis))])


def kernel_block(points_ref, centers_ref, norm_ref, coef_ref, kernel_ref, value_ref):
    samples = points_ref[...]
    wide = samples.astype(F32)
    left = 0.5 * jnp.sum(wide * wide, axis=1, keepdims=True)
    total = jnp.zeros(value_ref.shape, F32)
    for i in range(centers_ref.shape[0] // TILE):
        rows = pl.ds(i * TILE, TILE)
        products = lax.dot_general(
            samples, centers_ref[rows, :], (((1,), (1,)), ((), ())), preferred_element_type=F32
        )
        block = jnp.exp(products - left - norm_ref[:, rows]).astype(BF)
        kernel_ref[:, rows] = block
        total += jnp.dot(block, coef_ref[rows, :], preferred_element_type=F32)
    value_ref[...] = total.astype(value_ref.dtype)


def kernel_and_value(samples, anchors, norms, coefficients):
    count, depth = samples.shape
    total, cols = coefficients.shape
    return pl.pallas_call(
        kernel_block,
        out_shape=(
            jax.ShapeDtypeStruct((count, total), BF),
            jax.ShapeDtypeStruct((count, cols), BF),
        ),
        in_specs=[pl.BlockSpec(memory_space=pltpu.VMEM)] * 4,
        out_specs=[pl.BlockSpec(memory_space=pltpu.VMEM)] * 2,
        compiler_params=pltpu.CompilerParams(vmem_limit_bytes=16 * 1024 * 1024),
        cost_estimate=pl.CostEstimate(
            flops=2 * count * total * (depth + cols),
            bytes_accessed=2 * (count * depth + total * depth + total * cols + count * total),
            transcendentals=count * total,
        ),
    )(samples, anchors, norms, coefficients)


def half_norm(rows):
    return 0.5 * jnp.sum(jnp.square(rows.astype(F32)), axis=1)


def gaussian(samples, anchors, left, right):
    products = lax.dot_general(
        samples, anchors, (((1,), (1,)), ((), ())), preferred_element_type=F32
    )
    return jnp.exp(products - left[:, None] - right[None, :]).astype(BF)


def class_lookup(labels, table):
    classes = jnp.arange(table.shape[0], dtype=jnp.int32)
    return jnp.sum(jnp.where(labels[:, None] == classes[None, :], table[None, :], 0.0), axis=1)


def side_by_side(x, count):
    rows = x.shape[0] // count
    return jnp.concatenate([x[i * rows : (i + 1) * rows] for i in range(count)], axis=1)


def diagonal_sum(x, count):
    rows, cols = x.shape[0] // count, x.shape[1] // count
    total = x[:rows, :cols]
    for i in range(1, count):
        total = total + x[i * rows : (i + 1) * rows, i * cols : (i + 1) * cols]
    return total


def body(
    points,
    point_class,
    targets,
    class_weight,
    inv_scale,
    centers,
    coefficients,
    center_index,
    factor,
    panel_inverse,
):
    groups = lax.axis_size("pts")
    shards = lax.axis_size("ctr")
    shard = lax.axis_index("ctr")
    own_points, depth = points.shape
    shard_rows = centers.shape[0]
    target_count = targets.shape[1]
    target_slice = target_count // groups
    window_rows = center_index.shape[0]
    own_rows = window_rows // shards
    panel_rows = panel_inverse.shape[1]
    panel_shards = panel_rows // own_rows
    panel = shard // panel_shards
    fold = LANES // target_slice
    strip = own_rows // fold

    plane_bits = [shards // PLANES * k for k in range(PLANES)]
    plane_points = shards // PLANES * own_points

    own_scaled = (points.astype(F32) * inv_scale[None, :]).astype(BF)
    plane_rows = plane_gathered(own_scaled, "ctr").reshape(plane_points, depth)
    far = swapped(plane_rows, "ctr", plane_bits[2])
    chunks = [
        plane_rows,
        swapped(plane_rows, "ctr", plane_bits[1]),
        far,
        swapped(plane_rows, "ctr", plane_bits[3]),
    ]

    scaled_centers = (centers.astype(F32) * inv_scale[None, :]).astype(BF)
    center_norm = half_norm(scaled_centers)

    blocks = center_index.reshape(own_rows, shards)
    order = blocks[0] // shard_rows
    here = order == shard
    local = jnp.sum(jnp.where(here[None, :], blocks - shard * shard_rows, 0), axis=1)
    choose = (local[:, None] == jnp.arange(shard_rows, dtype=jnp.int32)[None, :]).astype(BF)
    chosen = jnp.dot(choose, scaled_centers, preferred_element_type=F32).astype(BF)
    chosen_norm = half_norm(chosen)
    place = (order[:, None] == jnp.arange(shards, dtype=jnp.int32)[None, :]).astype(F32)

    halves = panel_rows // (strip * shards)
    inverse = panel_inverse.reshape(own_rows, halves, strip, shards)
    inverse_window = jnp.einsum("rhqj,js->hrsq", inverse, place, precision=HI)
    inverse_window = inverse_window.reshape(halves, own_rows, shards * strip)
    parts = []
    for i in range(fold):
        parts.append(jnp.where(panel == i // halves, inverse_window[i % halves], 0.0))
    inverse_window = jnp.concatenate(parts, axis=0)

    def folded(matrix):
        m = matrix.reshape(own_rows, panel_shards, fold, strip)
        return m.transpose(2, 0, 1, 3).reshape(fold * own_rows, panel_shards * strip)

    factor_rows = folded(factor[:, :panel_rows])
    inverse_rows = folded(panel_inverse)

    kernels = [None] * PLANES
    arrived = None
    for k in (0, 1, 3, 2):
        kernels[k], value = kernel_and_value(
            chunks[k], scaled_centers, center_norm[None, :], coefficients
        )
        value = value if k == 0 else swapped(value, "ctr", plane_bits[k])
        value = value.astype(F32)
        arrived = value if arrived is None else arrived + value
    own_weight = class_lookup(point_class, class_weight)
    shares = plane_exchange(
        arrived.astype(BF).reshape(shards // PLANES, own_points, target_count), "ctr"
    )
    predicted = jnp.sum(shares.astype(F32), axis=0)
    own_residual = (own_weight[:, None] * (predicted - targets)).astype(BF)
    plane_residual = plane_gathered(own_residual, "ctr").reshape(plane_points, target_count)
    residuals = [plane_residual] + [
        swapped(plane_residual, "ctr", plane_bits[k]) for k in range(1, PLANES)
    ]

    window = None
    for k in range(PLANES):
        chosen_kernel = gaussian(chunks[k], chosen, half_norm(chunks[k]), chosen_norm)
        part = lax.dot_general(
            chosen_kernel, residuals[k], (((0,), (0,)), ((), ())), preferred_element_type=F32
        )
        window = part if window is None else window + part
    pieces = jnp.stack(
        [
            side_by_side(window[:, i * target_slice : (i + 1) * target_slice], fold)
            for i in range(groups)
        ]
    )
    pieces = lax.all_to_all(pieces, "pts", 0, 0, tiled=True)
    window = jnp.sum(pieces, axis=0).astype(BF)
    window = gathered(window, "ctr").reshape(shards * strip, LANES)

    backward = None
    for k in range(PLANES):
        part = lax.dot_general(
            residuals[k], kernels[k], (((0,), (0,)), ((), ())), preferred_element_type=F32
        )
        backward = part if backward is None else backward + part
    backward = backward.reshape(groups, target_slice, shard_rows)
    group = lax.axis_index("pts")
    gradient = lax.dynamic_index_in_dim(backward, group, 0, keepdims=False)
    backward = backward.astype(BF)
    for k in range(1, groups):
        piece = lax.dynamic_index_in_dim(backward, group ^ k, 0, keepdims=False)
        gradient = gradient + swapped(piece, "pts", k).astype(F32)
    gradient = gradient.T

    base = diagonal_sum(jnp.dot(inverse_window, window.astype(F32), precision=HI), fold)
    first = gathered(side_by_side(base, fold).astype(BF), "ctr")
    first = first[:panel_shards].reshape(panel_shards * strip, LANES)
    update = diagonal_sum(jnp.dot(factor_rows, first.astype(F32), precision=HI), fold)
    second = gathered(side_by_side(update, fold).astype(BF), "ctr")
    second = second[panel_shards:].reshape(panel_shards * strip, LANES)
    change = diagonal_sum(jnp.dot(inverse_rows, second.astype(F32), precision=HI), fold)
    solved = base - jnp.where(panel == 1, change, 0.0)
    return (gradient, solved)


def solution(mesh):
    placed = (
        P(("pts", "ctr"), None),
        P(("pts", "ctr")),
        P(("pts", "ctr"), None),
        P(),
        P(),
        P("ctr", None),
        P("ctr", None),
        P(),
        P("ctr", None),
        P("ctr", None),
    )
    return jax.shard_map(
        body,
        mesh=mesh,
        in_specs=placed,
        out_specs=(P("ctr", "pts"), P("ctr", "pts")),
        check_vma=False,
    )
```

```python
import jax
import jax.numpy as jnp
from jax import lax
from jax.experimental import pallas as pl
from jax.experimental.pallas import tpu as pltpu
from jax.sharding import PartitionSpec as P

BF = jnp.bfloat16
F32 = jnp.float32
HI = lax.Precision.HIGHEST
LANES = 128


PLANES = 4
TILE = 512


def gathered(x, axis):
    count = lax.axis_size(axis)
    return lax.all_to_all(jnp.broadcast_to(x[None], (count, *x.shape)), axis, 0, 0, tiled=True)


def plane_groups(axis):
    size = lax.axis_size(axis) // PLANES
    return [[plane * size + i for i in range(size)] for plane in range(PLANES)]


def plane_exchange(pieces, axis):
    groups = plane_groups(axis)
    return lax.all_to_all(pieces, axis, 0, 0, tiled=True, axis_index_groups=groups)


def plane_gathered(x, axis):
    size = lax.axis_size(axis) // PLANES
    return plane_exchange(jnp.broadcast_to(x[None], (size, *x.shape)), axis)


def swapped(x, axis, bits):
    return lax.ppermute(x, axis, [(i, i ^ bits) for i in range(lax.axis_size(axis))])


def kernel_block(
    points_ref, centers_ref, norm_ref, coef_ref, kernel_ref, value_ref, slots, total, sems
):
    step = pl.program_id(0)
    samples = points_ref[...]
    wide = samples.astype(F32)
    left = 0.5 * jnp.sum(wide * wide, axis=1, keepdims=True)
    products = lax.dot_general(
        samples, centers_ref[...], (((1,), (1,)), ((), ())), preferred_element_type=F32
    )
    block = jnp.exp(products - left - norm_ref[...]).astype(BF)
    slots[step] = block
    columns = pl.ds(pl.multiple_of(step * TILE, TILE), TILE)
    pltpu.make_async_copy(slots.at[step], kernel_ref.at[:, columns], sems.at[step]).start()
    part = jnp.dot(block, coef_ref[...], preferred_element_type=F32)

    @pl.when(step == 0)
    def _():
        total[...] = part

    @pl.when(step > 0)
    def _():
        total[...] += part

    @pl.when(step == pl.num_programs(0) - 1)
    def _():
        value_ref[...] = total[...].astype(value_ref.dtype)
        for i in range(slots.shape[0]):
            rows = pl.ds(i * TILE, TILE)
            pltpu.make_async_copy(slots.at[i], kernel_ref.at[:, rows], sems.at[i]).wait()


def kernel_and_value(samples, anchors, norms, coefficients):
    count, depth = samples.shape
    total, cols = coefficients.shape
    steps = total // TILE
    return pl.pallas_call(
        kernel_block,
        grid=(steps,),
        out_shape=(
            pltpu.HBM((count, total), BF),
            jax.ShapeDtypeStruct((count, cols), BF),
        ),
        in_specs=[
            pl.BlockSpec((count, depth), lambda i: (0, 0)),
            pl.BlockSpec((TILE, depth), lambda i: (i, 0)),
            pl.BlockSpec((1, TILE), lambda i: (0, i)),
            pl.BlockSpec((TILE, cols), lambda i: (i, 0)),
        ],
        out_specs=[
            pl.BlockSpec(memory_space=pltpu.HBM),
            pl.BlockSpec((count, cols), lambda i: (0, 0)),
        ],
        scratch_shapes=[
            pltpu.VMEM((steps, count, TILE), BF),
            pltpu.VMEM((count, cols), F32),
            pltpu.SemaphoreType.DMA((steps,)),
        ],
        compiler_params=pltpu.CompilerParams(vmem_limit_bytes=16 * 1024 * 1024),
        cost_estimate=pl.CostEstimate(
            flops=2 * count * total * (depth + cols),
            bytes_accessed=2 * (count * depth + total * depth + total * cols + count * total),
            transcendentals=count * total,
        ),
    )(
        samples,
        pltpu.with_memory_space_constraint(anchors, pltpu.HBM),
        norms,
        pltpu.with_memory_space_constraint(coefficients, pltpu.HBM),
    )


def half_norm(rows):
    return 0.5 * jnp.sum(jnp.square(rows.astype(F32)), axis=1)


def gaussian(samples, anchors, left, right):
    products = lax.dot_general(
        samples, anchors, (((1,), (1,)), ((), ())), preferred_element_type=F32
    )
    return jnp.exp(products - left[:, None] - right[None, :]).astype(BF)


def class_lookup(labels, table):
    classes = jnp.arange(table.shape[0], dtype=jnp.int32)
    return jnp.sum(jnp.where(labels[:, None] == classes[None, :], table[None, :], 0.0), axis=1)


def side_by_side(x, count):
    rows = x.shape[0] // count
    return jnp.concatenate([x[i * rows : (i + 1) * rows] for i in range(count)], axis=1)


def diagonal_sum(x, count):
    rows, cols = x.shape[0] // count, x.shape[1] // count
    total = x[:rows, :cols]
    for i in range(1, count):
        total = total + x[i * rows : (i + 1) * rows, i * cols : (i + 1) * cols]
    return total


def body(
    points,
    point_class,
    targets,
    class_weight,
    inv_scale,
    centers,
    coefficients,
    center_index,
    factor,
    panel_inverse,
):
    groups = lax.axis_size("pts")
    shards = lax.axis_size("ctr")
    shard = lax.axis_index("ctr")
    own_points, depth = points.shape
    shard_rows = centers.shape[0]
    target_count = targets.shape[1]
    target_slice = target_count // groups
    window_rows = center_index.shape[0]
    own_rows = window_rows // shards
    panel_rows = panel_inverse.shape[1]
    panel_shards = panel_rows // own_rows
    panel = shard // panel_shards
    fold = LANES // target_slice
    strip = own_rows // fold

    plane_bits = [shards // PLANES * k for k in range(PLANES)]
    plane_points = shards // PLANES * own_points

    own_scaled = (points.astype(F32) * inv_scale[None, :]).astype(BF)
    plane_rows = plane_gathered(own_scaled, "ctr").reshape(plane_points, depth)
    far = swapped(plane_rows, "ctr", plane_bits[2])
    chunks = [
        plane_rows,
        swapped(plane_rows, "ctr", plane_bits[1]),
        far,
        swapped(plane_rows, "ctr", plane_bits[3]),
    ]

    scaled_centers = (centers.astype(F32) * inv_scale[None, :]).astype(BF)
    center_norm = half_norm(scaled_centers)

    kernels = [None] * PLANES
    arrived = None
    for k in (0, 1, 3, 2):
        kernels[k], value = kernel_and_value(
            chunks[k], scaled_centers, center_norm[None, :], coefficients
        )
        value = value if k == 0 else swapped(value, "ctr", plane_bits[k])
        value = value.astype(F32)
        arrived = value if arrived is None else arrived + value
    arrived, panel_inverse, center_index, scaled_centers = lax.optimization_barrier(
        (arrived, panel_inverse, center_index, scaled_centers)
    )
    blocks = center_index.reshape(own_rows, shards)
    order = blocks[0] // shard_rows
    here = order == shard
    local = jnp.sum(jnp.where(here[None, :], blocks - shard * shard_rows, 0), axis=1)
    choose = (local[:, None] == jnp.arange(shard_rows, dtype=jnp.int32)[None, :]).astype(BF)
    chosen = jnp.dot(choose, scaled_centers, preferred_element_type=F32).astype(BF)
    chosen_norm = half_norm(chosen)
    place = (order[:, None] == jnp.arange(shards, dtype=jnp.int32)[None, :]).astype(F32)

    halves = panel_rows // (strip * shards)
    inverse = panel_inverse.reshape(own_rows, halves, strip, shards)
    inverse_window = jnp.einsum("rhqj,js->hrsq", inverse, place, precision=HI)
    inverse_window = inverse_window.reshape(halves, own_rows, shards * strip)
    parts = []
    for i in range(fold):
        parts.append(jnp.where(panel == i // halves, inverse_window[i % halves], 0.0))
    inverse_window = jnp.concatenate(parts, axis=0)

    own_weight = class_lookup(point_class, class_weight)
    shares = plane_exchange(
        arrived.astype(BF).reshape(shards // PLANES, own_points, target_count), "ctr"
    )
    predicted = jnp.sum(shares.astype(F32), axis=0)
    own_residual = (own_weight[:, None] * (predicted - targets)).astype(BF)
    own_residual, factor = lax.optimization_barrier((own_residual, factor[:, :panel_rows]))
    def folded(matrix):
        m = matrix.reshape(own_rows, panel_shards, fold, strip)
        return m.transpose(2, 0, 1, 3).reshape(fold * own_rows, panel_shards * strip)

    factor_rows = folded(factor)
    plane_residual = plane_gathered(own_residual, "ctr").reshape(plane_points, target_count)
    residuals = [plane_residual] + [
        swapped(plane_residual, "ctr", plane_bits[k]) for k in range(1, PLANES)
    ]

    window = None
    for k in range(PLANES):
        chosen_kernel = gaussian(chunks[k], chosen, half_norm(chunks[k]), chosen_norm)
        part = lax.dot_general(
            chosen_kernel, residuals[k], (((0,), (0,)), ((), ())), preferred_element_type=F32
        )
        window = part if window is None else window + part
    pieces = jnp.stack(
        [
            side_by_side(window[:, i * target_slice : (i + 1) * target_slice], fold)
            for i in range(groups)
        ]
    )
    pieces = lax.all_to_all(pieces, "pts", 0, 0, tiled=True)
    window = jnp.sum(pieces, axis=0).astype(BF)
    window, panel_inverse = lax.optimization_barrier((window, panel_inverse))
    inverse_rows = folded(panel_inverse)
    window = gathered(window, "ctr").reshape(shards * strip, LANES)

    backward = None
    for k in range(PLANES):
        part = lax.dot_general(
            residuals[k], kernels[k], (((0,), (0,)), ((), ())), preferred_element_type=F32
        )
        backward = part if backward is None else backward + part
    backward = backward.reshape(groups, target_slice, shard_rows)
    group = lax.axis_index("pts")
    gradient = lax.dynamic_index_in_dim(backward, group, 0, keepdims=False)
    backward = backward.astype(BF)
    for k in range(1, groups):
        piece = lax.dynamic_index_in_dim(backward, group ^ k, 0, keepdims=False)
        gradient = gradient + swapped(piece, "pts", k).astype(F32)
    gradient = gradient.T

    base = diagonal_sum(jnp.dot(inverse_window, window.astype(F32), precision=HI), fold)
    first = gathered(side_by_side(base, fold).astype(BF), "ctr")
    first = first[:panel_shards].reshape(panel_shards * strip, LANES)
    update = diagonal_sum(jnp.dot(factor_rows, first.astype(F32), precision=HI), fold)
    second = gathered(side_by_side(update, fold).astype(BF), "ctr")
    second = second[panel_shards:].reshape(panel_shards * strip, LANES)
    change = diagonal_sum(jnp.dot(inverse_rows, second.astype(F32), precision=HI), fold)
    solved = base - jnp.where(panel == 1, change, 0.0)
    return (gradient, solved)


def solution(mesh):
    placed = (
        P(("pts", "ctr"), None),
        P(("pts", "ctr")),
        P(("pts", "ctr"), None),
        P(),
        P(),
        P("ctr", None),
        P("ctr", None),
        P(),
        P("ctr", None),
        P("ctr", None),
    )
    return jax.shard_map(
        body,
        mesh=mesh,
        in_specs=placed,
        out_specs=(P("ctr", "pts"), P("ctr", "pts")),
        check_vma=False,
    )
```

```python
import jax
import jax.numpy as jnp
from jax import lax
from jax.experimental import pallas as pl
from jax.experimental.pallas import tpu as pltpu
from jax.sharding import PartitionSpec as P

BF = jnp.bfloat16
F32 = jnp.float32
LANES = 128
PLANES = 4
HALVES = 2
TILE = 512
VMEM = pl.BlockSpec(memory_space=pltpu.VMEM)


def exchanged(pieces, axis, parts=1):
    size = lax.axis_size(axis) // parts
    groups = [[part * size + i for i in range(size)] for part in range(parts)]
    return lax.all_to_all(
        pieces, axis, 0, 0, tiled=True, axis_index_groups=groups if parts > 1 else None
    )


def copies(x, count):
    return jnp.broadcast_to(x[None], (count, *x.shape))


def swapped(x, axis, bits):
    return lax.ppermute(x, axis, [(i, i ^ bits) for i in range(lax.axis_size(axis))])


def pick(x, index):
    return lax.dynamic_index_in_dim(x, index, 0, keepdims=False)


def kernel_block(points_ref, centers_ref, norm_ref, coef_ref, kernel_ref, value_ref, slots, sems):
    samples = points_ref[...]
    wide = samples.astype(F32)
    left = 0.5 * jnp.sum(wide * wide, axis=1, keepdims=True)
    total = jnp.zeros(value_ref.shape, F32)
    saves = []
    for i in range(centers_ref.shape[0] // TILE):
        rows = pl.ds(i * TILE, TILE)
        products = lax.dot_general(
            samples, centers_ref[rows, :], (((1,), (1,)), ((), ())), preferred_element_type=F32
        )
        block = jnp.exp(products - left - norm_ref[:, rows]).astype(BF)
        slots[i] = block
        saves.append(pltpu.make_async_copy(slots.at[i], kernel_ref.at[:, rows], sems.at[i]))
        saves[-1].start()
        total += jnp.dot(block, coef_ref[rows, :], preferred_element_type=F32)
    value_ref[...] = total.astype(value_ref.dtype)
    for save in saves:
        save.wait()


def kernel_and_value(samples, anchors, norms, coefficients):
    count, depth = samples.shape
    total, cols = coefficients.shape
    steps = total // TILE
    return pl.pallas_call(
        kernel_block,
        out_shape=(pltpu.HBM((count, total), BF), jax.ShapeDtypeStruct((count, cols), BF)),
        in_specs=[VMEM] * 4,
        out_specs=[pl.BlockSpec(memory_space=pltpu.HBM), VMEM],
        scratch_shapes=[pltpu.VMEM((steps, count, TILE), BF), pltpu.SemaphoreType.DMA((steps,))],
        compiler_params=pltpu.CompilerParams(vmem_limit_bytes=24 * 1024 * 1024),
        cost_estimate=pl.CostEstimate(
            flops=2 * count * total * (depth + cols),
            bytes_accessed=2 * count * total,
            transcendentals=count * total,
        ),
    )(samples, pltpu.with_memory_space_constraint(anchors, pltpu.VMEM), norms, coefficients)


def lane_block(shape, width, index):
    lane = lax.broadcasted_iota(jnp.int32, shape, len(shape) - 1)
    return (lane >= index * width) & (lane < (index + 1) * width)


def turned(x, lanes):
    lanes = lanes % LANES
    return pltpu.roll(x, lanes, 1) if lanes else x


def folded_sum(product, fold, strip, blocks):
    width = LANES // fold
    out = None
    for f in range(fold):
        total = None
        for r in blocks:
            row = (r * fold + f) * strip
            part = turned(product[row : row + strip, :], (f - r) * width)
            total = part if total is None else total + part
        out = total if out is None else jnp.where(lane_block(total.shape, width, f), total, out)
    return out


def first_step(matrix_ref, window_ref, sent_ref, low_ref, high_ref):
    strip = sent_ref.shape[1]
    fold = int(round((matrix_ref.shape[0] // strip) ** 0.5))
    product = jnp.dot(matrix_ref[...], window_ref[...], preferred_element_type=F32)
    low = folded_sum(product, fold, strip, range(fold // HALVES))
    high = folded_sum(product, fold, strip, range(fold // HALVES, fold))
    low_ref[...] = low
    high_ref[...] = high
    sent_ref[...] = jnp.broadcast_to(low.astype(BF)[None], sent_ref.shape)


def middle_step(matrix_ref, solved_ref, sent_ref):
    strip = sent_ref.shape[1]
    fold = int(round((matrix_ref.shape[0] // strip) ** 0.5))
    product = jnp.dot(matrix_ref[...], solved_ref[...], preferred_element_type=F32)
    total = folded_sum(product, fold, strip, range(fold))
    sent_ref[...] = jnp.broadcast_to(total.astype(BF)[None], sent_ref.shape)


def last_step(matrix_ref, update_ref, high_ref, out_ref):
    strip = out_ref.shape[0]
    fold = int(round((matrix_ref.shape[0] // strip) ** 0.5))
    product = jnp.dot(matrix_ref[...], update_ref[...], preferred_element_type=F32)
    out_ref[...] = high_ref[...] - folded_sum(product, fold, strip, range(fold))


def window_step(chosen_ref, residual_ref, pieces_ref):
    window = lax.dot_general(
        chosen_ref[...], residual_ref[...], (((0,), (0,)), ((), ())), preferred_element_type=F32
    )
    groups, strip, _ = pieces_ref.shape
    width = LANES // groups
    for p in range(groups):
        out = None
        for r in range(window.shape[0] // strip):
            part = turned(window[r * strip : (r + 1) * strip, :], (r - p) * width)
            out = part if out is None else jnp.where(lane_block(part.shape, width, r), part, out)
        pieces_ref[p] = out


def whole(body, shapes, *args):
    return pl.pallas_call(
        body,
        out_shape=shapes,
        in_specs=[VMEM] * len(args),
        out_specs=jax.tree.map(lambda _: VMEM, shapes),
        compiler_params=pltpu.CompilerParams(vmem_limit_bytes=16 * 1024 * 1024),
    )(*args)


def half_norm(rows):
    return 0.5 * jnp.sum(jnp.square(rows.astype(F32)), axis=-1)


def class_lookup(labels, table):
    classes = jnp.arange(table.shape[0], dtype=jnp.int32)
    return jnp.sum(jnp.where(labels[:, None] == classes[None, :], table[None, :], 0.0), axis=1)


def body(
    points,
    point_class,
    targets,
    class_weight,
    inv_scale,
    centers,
    coefficients,
    center_index,
    factor,
    panel_inverse,
):
    groups = lax.axis_size("pts")
    shards = lax.axis_size("ctr")
    shard = lax.axis_index("ctr")
    group = lax.axis_index("pts")
    own_points, depth = points.shape
    shard_rows = centers.shape[0]
    target_count = targets.shape[1]
    target_slice = target_count // groups
    own_rows = center_index.shape[0] // shards
    panel_rows = panel_inverse.shape[1]
    panel_shards = panel_rows // own_rows
    panel = shard // panel_shards
    fold = LANES // target_slice
    strip = own_rows // fold
    plane_size = shards // PLANES
    plane = shard // plane_size
    plane_points = plane_size * own_points

    own_scaled = (points.astype(F32) * inv_scale[None, :]).astype(BF)
    plane_rows = exchanged(copies(own_scaled, plane_size), "ctr", PLANES)
    plane_rows = plane_rows.reshape(plane_points, depth)
    chunks = [plane_rows] + [None] * (PLANES - 1)
    for k in (2, 1, 3):
        chunks[k] = swapped(plane_rows, "ctr", k * plane_size)

    scaled_centers = (centers.astype(F32) * inv_scale[None, :]).astype(BF)
    center_norm = half_norm(scaled_centers)

    blocks = center_index.reshape(own_rows, shards)
    order = blocks[0] // shard_rows
    here = order == shard
    local = jnp.sum(jnp.where(here[None, :], blocks - shard * shard_rows, 0), axis=1)
    choose = (local[:, None] == jnp.arange(shard_rows, dtype=jnp.int32)[None, :]).astype(BF)
    chosen = jnp.dot(choose, scaled_centers, preferred_element_type=F32).astype(BF)
    chosen_norm = half_norm(chosen)
    place = (order[:, None] == jnp.arange(shards, dtype=jnp.int32)[None, :]).astype(BF)

    inverse = panel_inverse.astype(BF)
    count = panel_rows // (strip * shards)
    turned_inverse = jnp.einsum(
        "rhqj,js->hrsq", inverse.reshape(own_rows, count, strip, shards), place
    ).reshape(count * own_rows, shards * strip)
    other_inverse = swapped(turned_inverse, "ctr", panel_shards)

    kernels = [None] * PLANES
    arrived = None
    for k in (0, 1, 3, 2):
        kernels[k], value = kernel_and_value(
            chunks[k], scaled_centers, center_norm[None, :], coefficients
        )
        value = value if k == 0 else swapped(value, "ctr", k * plane_size)
        value = value.astype(F32)
        arrived = value if arrived is None else arrived + value
    arrived, inverse, factor, chosen = lax.optimization_barrier(
        (arrived, inverse, factor[:, :panel_rows].astype(BF), chosen)
    )

    def folded(matrix):
        m = matrix.reshape(own_rows, panel_shards, fold, strip)
        return m.transpose(2, 0, 1, 3).reshape(fold * own_rows, panel_shards * strip)

    factor_rows = folded(factor)
    inverse_rows = folded(inverse)
    solve_rows = jnp.concatenate(
        [
            jnp.where(panel == 0, turned_inverse, other_inverse),
            jnp.where(panel == 0, other_inverse, turned_inverse),
        ],
        axis=0,
    )
    near = jnp.stack(chunks)
    products = lax.dot_general(
        near, chosen, (((2,), (1,)), ((), ())), preferred_element_type=F32
    )
    chosen_kernel = jnp.exp(products - half_norm(near)[:, :, None] - chosen_norm).astype(BF)
    chosen_kernel = jnp.concatenate([pick(chosen_kernel, plane ^ k) for k in range(PLANES)], axis=0)

    own_weight = class_lookup(point_class, class_weight)
    shares = exchanged(
        arrived.astype(BF).reshape(plane_size, own_points, target_count), "ctr", PLANES
    )
    predicted = jnp.sum(shares.astype(F32), axis=0)
    own_residual = (own_weight[:, None] * (predicted - targets)).astype(BF)
    residual = exchanged(copies(own_residual, shards), "ctr")
    residual = residual.reshape(shards * own_points, target_count)

    pieces = whole(
        window_step, jax.ShapeDtypeStruct((groups, strip, LANES), F32), chosen_kernel, residual
    )
    pieces = exchanged(pieces, "pts")
    window = jnp.sum(pieces, axis=0).astype(BF)
    window = exchanged(copies(window, shards), "ctr").reshape(shards * strip, LANES)

    planes = residual.reshape(PLANES, plane_points, target_count)
    backward = None
    for k in range(PLANES):
        part = lax.dot_general(
            pick(planes, plane ^ k), kernels[k], (((0,), (0,)), ((), ())), preferred_element_type=F32
        )
        backward = part if backward is None else backward + part
    backward = backward.reshape(groups, target_slice, shard_rows)
    near_pair = jnp.stack([pick(backward, group), pick(backward, group ^ 2)])
    far_pair = jnp.stack([pick(backward, group ^ 1), pick(backward, group ^ 3)]).astype(BF)
    near_pair = near_pair + swapped(far_pair, "pts", 1).astype(F32)
    gradient = near_pair[0] + swapped(near_pair[1].astype(BF), "pts", 2).astype(F32)
    gradient = gradient.T

    half = shards // HALVES
    sent = jax.ShapeDtypeStruct((half, strip, LANES), BF)
    packed = jax.ShapeDtypeStruct((strip, LANES), F32)
    first, low, high = whole(first_step, (sent, packed, packed), solve_rows, window)
    first = exchanged(first, "ctr", HALVES).reshape(half * strip, LANES)
    update = whole(middle_step, sent, factor_rows, first)
    update = exchanged(update, "ctr", HALVES).reshape(half * strip, LANES)
    changed = whole(last_step, packed, inverse_rows, update, high)
    solved = jnp.where(panel == 0, low, changed)
    solved = solved.reshape(strip, fold, target_slice).transpose(1, 0, 2)
    return (gradient, solved.reshape(own_rows, target_slice))


def solution(mesh):
    placed = (
        P(("pts", "ctr"), None),
        P(("pts", "ctr")),
        P(("pts", "ctr"), None),
        P(),
        P(),
        P("ctr", None),
        P("ctr", None),
        P(),
        P("ctr", None),
        P("ctr", None),
    )
    return jax.shard_map(
        body,
        mesh=mesh,
        in_specs=placed,
        out_specs=(P("ctr", "pts"), P("ctr", "pts")),
        check_vma=False,
    )
```

```python
import jax
import jax.numpy as jnp
from jax import lax
from jax.experimental import pallas as pl
from jax.experimental.pallas import tpu as pltpu
from jax.sharding import PartitionSpec as P

BF = jnp.bfloat16
F32 = jnp.float32
LANES = 128
PLANES = 4
HALVES = 2
TILE = 512
VMEM = pl.BlockSpec(memory_space=pltpu.VMEM)


def exchanged(pieces, axis, parts=1):
    size = lax.axis_size(axis) // parts
    groups = [[part * size + i for i in range(size)] for part in range(parts)]
    return lax.all_to_all(
        pieces, axis, 0, 0, tiled=True, axis_index_groups=groups if parts > 1 else None
    )


def copies(x, count):
    return jnp.broadcast_to(x[None], (count, *x.shape))


def swapped(x, axis, bits):
    return lax.ppermute(x, axis, [(i, i ^ bits) for i in range(lax.axis_size(axis))])


def pick(x, index):
    return lax.dynamic_index_in_dim(x, index, 0, keepdims=False)


def scale_step(centers_ref, scale_ref, scaled_ref, norm_ref, slots, sems):
    loads = []
    for i in range(slots.shape[0]):
        rows = pl.ds(i * TILE, TILE)
        loads.append(pltpu.make_async_copy(centers_ref.at[rows, :], slots.at[i], sems.at[i]))
        loads[-1].start()
    for i, load in enumerate(loads):
        rows = pl.ds(i * TILE, TILE)
        load.wait()
        scaled = (slots[i].astype(F32) * scale_ref[...]).astype(BF)
        scaled_ref[rows, :] = scaled
        wide = scaled.astype(F32)
        norm = 0.5 * jnp.sum(wide * wide, axis=1, keepdims=True)
        norm_ref[:, rows] = jnp.broadcast_to(norm, (TILE, LANES)).T[0:1, :]


def scaled_and_norm(centers, scale):
    total, depth = centers.shape
    steps = total // TILE
    return pl.pallas_call(
        scale_step,
        out_shape=(pltpu.VMEM((total, depth), BF), jax.ShapeDtypeStruct((1, total), F32)),
        in_specs=[pl.BlockSpec(memory_space=pltpu.HBM), VMEM],
        out_specs=[VMEM, VMEM],
        scratch_shapes=[pltpu.VMEM((steps, TILE, depth), BF), pltpu.SemaphoreType.DMA((steps,))],
        compiler_params=pltpu.CompilerParams(vmem_limit_bytes=24 * 1024 * 1024),
        cost_estimate=pl.CostEstimate(
            flops=4 * total * depth, bytes_accessed=2 * total * depth, transcendentals=0
        ),
    )(pltpu.with_memory_space_constraint(centers, pltpu.HBM), scale)


def kernel_block(
    slot_ref, points_ref, scale_ref, centers_ref, norm_ref, coef_ref, *refs
):
    scaled_ref, kernel_ref, value_ref = refs[-3:]
    samples = (points_ref[...].astype(F32) * scale_ref[...]).astype(BF)
    scaled_ref[...] = samples
    wide = samples.astype(F32)
    left = 0.5 * jnp.sum(wide * wide, axis=1, keepdims=True)
    total = jnp.zeros(value_ref.shape[1:], F32)
    for i in range(centers_ref.shape[0] // TILE):
        rows = pl.ds(i * TILE, TILE)
        products = lax.dot_general(
            samples, centers_ref[rows, :], (((1,), (1,)), ((), ())), preferred_element_type=F32
        )
        block = jnp.exp(products - left - norm_ref[:, rows]).astype(BF)
        kernel_ref[:, rows] = block
        total += jnp.dot(block, coef_ref[rows, :], preferred_element_type=F32)
    if len(refs) > 3:
        value_ref[...] = refs[0][...]
    value_ref[slot_ref[0]] = total.astype(value_ref.dtype)


def kernel_and_value(slot, samples, scale, anchors, norms, coefficients, values=None):
    count, depth = samples.shape
    total, cols = coefficients.shape
    args = [samples, scale, pltpu.with_memory_space_constraint(anchors, pltpu.VMEM)]
    args += [norms, coefficients] + ([] if values is None else [values])
    return pl.pallas_call(
        kernel_block,
        out_shape=(
            jax.ShapeDtypeStruct((count, depth), BF),
            pltpu.VMEM((count, total), BF),
            jax.ShapeDtypeStruct((PLANES, count, cols), BF),
        ),
        in_specs=[pl.BlockSpec(memory_space=pltpu.SMEM)] + [VMEM] * len(args),
        out_specs=[VMEM] * 3,
        compiler_params=pltpu.CompilerParams(vmem_limit_bytes=24 * 1024 * 1024),
        cost_estimate=pl.CostEstimate(
            flops=2 * count * total * (depth + cols),
            bytes_accessed=2 * count * total,
            transcendentals=count * total,
        ),
    )(slot, *args)


def lane_block(shape, width, index):
    lane = lax.broadcasted_iota(jnp.int32, shape, len(shape) - 1)
    return (lane >= index * width) & (lane < (index + 1) * width)


def turned(x, lanes):
    lanes = lanes % LANES
    return pltpu.roll(x, lanes, 1) if lanes else x


def folded_sum(product, fold, strip, blocks):
    width = LANES // fold
    out = None
    for f in range(fold):
        total = None
        for r in blocks:
            row = (r * fold + f) * strip
            part = turned(product[row : row + strip, :], (f - r) * width)
            total = part if total is None else total + part
        out = total if out is None else jnp.where(lane_block(total.shape, width, f), total, out)
    return out


def first_step(matrix_ref, window_ref, sent_ref, low_ref, high_ref):
    strip = sent_ref.shape[1]
    fold = int(round((matrix_ref.shape[0] // strip) ** 0.5))
    product = jnp.dot(matrix_ref[...], window_ref[...], preferred_element_type=F32)
    low = folded_sum(product, fold, strip, range(fold // HALVES))
    high = folded_sum(product, fold, strip, range(fold // HALVES, fold))
    low_ref[...] = low
    high_ref[...] = high
    sent_ref[...] = jnp.broadcast_to(low.astype(BF)[None], sent_ref.shape)


def middle_step(matrix_ref, solved_ref, sent_ref):
    strip = sent_ref.shape[1]
    fold = int(round((matrix_ref.shape[0] // strip) ** 0.5))
    product = jnp.dot(matrix_ref[...], solved_ref[...], preferred_element_type=F32)
    total = folded_sum(product, fold, strip, range(fold))
    sent_ref[...] = jnp.broadcast_to(total.astype(BF)[None], sent_ref.shape)


def last_step(panel_ref, matrix_ref, update_ref, low_ref, high_ref, out_ref):
    strip = low_ref.shape[0]
    fold = int(round((matrix_ref.shape[0] // strip) ** 0.5))
    width = LANES // fold
    product = jnp.dot(matrix_ref[...], update_ref[...], preferred_element_type=F32)
    changed = high_ref[...] - folded_sum(product, fold, strip, range(fold))
    solved = jnp.where(panel_ref[0] == 0, low_ref[...], changed)
    rows = jnp.concatenate([turned(solved, -f * width) for f in range(fold)], axis=0)
    out_ref[...] = rows.T[:width, :]


def window_step(chosen_ref, residual_ref, window_ref):
    window_ref[...] = lax.dot_general(
        chosen_ref[...], residual_ref[...], (((0,), (0,)), ((), ())), preferred_element_type=F32
    )


def fold_step(group_ref, parts_ref, sent_ref):
    groups = parts_ref.shape[0]
    strip = sent_ref.shape[1]
    width = LANES // groups
    window = jnp.sum(parts_ref[...].astype(F32), axis=0)
    result = None
    for p in range(groups):
        out = None
        for r in range(window.shape[0] // strip):
            part = turned(window[r * strip : (r + 1) * strip, :], (r - p) * width)
            out = part if out is None else jnp.where(lane_block(part.shape, width, r), part, out)
        result = out if result is None else jnp.where(group_ref[0] == p, out, result)
    sent_ref[...] = jnp.broadcast_to(result.astype(BF)[None], sent_ref.shape)


def whole(body, shapes, *args, scalars=0):
    return pl.pallas_call(
        body,
        out_shape=shapes,
        in_specs=[pl.BlockSpec(memory_space=pltpu.SMEM)] * scalars + [VMEM] * (len(args) - scalars),
        out_specs=jax.tree.map(lambda _: VMEM, shapes),
        compiler_params=pltpu.CompilerParams(vmem_limit_bytes=16 * 1024 * 1024),
    )(*args)


def half_norm(rows):
    return 0.5 * jnp.sum(jnp.square(rows.astype(F32)), axis=-1)


def class_lookup(labels, table):
    classes = jnp.arange(table.shape[0], dtype=jnp.int32)
    return jnp.sum(jnp.where(labels[:, None] == classes[None, :], table[None, :], 0.0), axis=1)


def body(
    points,
    point_class,
    targets,
    class_weight,
    inv_scale,
    centers,
    coefficients,
    center_index,
    factor,
    panel_inverse,
):
    groups = lax.axis_size("pts")
    shards = lax.axis_size("ctr")
    shard = lax.axis_index("ctr")
    group = lax.axis_index("pts")
    own_points, depth = points.shape
    shard_rows = centers.shape[0]
    target_count = targets.shape[1]
    target_slice = target_count // groups
    own_rows = center_index.shape[0] // shards
    panel_rows = panel_inverse.shape[1]
    panel_shards = panel_rows // own_rows
    panel = shard // panel_shards
    fold = LANES // target_slice
    strip = own_rows // fold
    plane_size = shards // PLANES
    plane = shard // plane_size
    plane_points = plane_size * own_points

    plane_rows = exchanged(copies(points, plane_size), "ctr", PLANES)
    plane_rows = plane_rows.reshape(plane_points, depth)
    scale = inv_scale[None, :]
    scaled_centers, center_norm = scaled_and_norm(centers, scale)
    blocks = center_index.reshape(own_rows, shards)
    order = blocks[0] // shard_rows
    here = order == shard
    local = jnp.sum(jnp.where(here[None, :], blocks - shard * shard_rows, 0), axis=1)
    choose = (local[:, None] == jnp.arange(shard_rows, dtype=jnp.int32)[None, :]).astype(BF)
    chosen = jnp.dot(choose, scaled_centers, preferred_element_type=F32).astype(BF)
    chosen_norm = half_norm(chosen)
    plane_rows, scaled_centers, chosen, order = lax.optimization_barrier(
        (plane_rows, scaled_centers, chosen, order)
    )
    chunks = [plane_rows] + [None] * (PLANES - 1)
    for k in (2, 1, 3):
        chunks[k] = swapped(plane_rows, "ctr", k * plane_size)
    values = None
    kernels = [None] * PLANES
    for k in (0, 1, 3, 2):
        slot = (plane ^ k).astype(jnp.int32).reshape(1)
        chunks[k], kernels[k], values = kernel_and_value(
            slot, chunks[k], scale, scaled_centers, center_norm, coefficients, values
        )
    values, panel_inverse = lax.optimization_barrier((values, panel_inverse))

    place = (order[:, None] == jnp.arange(shards, dtype=jnp.int32)[None, :]).astype(BF)

    inverse = panel_inverse.astype(BF)
    count = panel_rows // (strip * shards)
    turned_inverse = jnp.einsum(
        "rhqj,js->hrsq", inverse.reshape(own_rows, count, strip, shards), place
    ).reshape(count * own_rows, shards * strip)

    def folded(matrix):
        m = matrix.reshape(own_rows, panel_shards, fold, strip)
        return m.transpose(2, 0, 1, 3).reshape(fold * own_rows, panel_shards * strip)

    near = jnp.stack(chunks)
    products = lax.dot_general(
        near, chosen, (((2,), (1,)), ((), ())), preferred_element_type=F32
    )
    chosen_kernel = jnp.exp(products - half_norm(near)[:, :, None] - chosen_norm).astype(BF)
    chosen_kernel = jnp.concatenate([pick(chosen_kernel, plane ^ k) for k in range(PLANES)], axis=0)

    own_weight = class_lookup(point_class, class_weight)
    shares = exchanged(values.reshape(shards, own_points, target_count), "ctr")
    predicted = jnp.sum(shares.astype(F32), axis=0)
    own_residual = (own_weight[:, None] * (predicted - targets)).astype(BF)
    own_residual, factor, inverse = lax.optimization_barrier(
        (own_residual, factor[:, :panel_rows], inverse)
    )
    factor_rows = folded(factor.astype(BF))
    inverse_rows = folded(inverse)
    residual = exchanged(copies(own_residual, shards), "ctr")
    residual = residual.reshape(shards * own_points, target_count)

    index = group.astype(jnp.int32).reshape(1)
    window = whole(
        window_step, jax.ShapeDtypeStruct((own_rows, target_count), F32), chosen_kernel, residual
    )
    parts = lax.all_gather(window, "pts")
    sent = jax.ShapeDtypeStruct((shards, strip, LANES), BF)
    window = whole(fold_step, sent, index, parts, scalars=1)
    window, turned_inverse = lax.optimization_barrier((window, turned_inverse))
    other_inverse = swapped(turned_inverse, "ctr", panel_shards)
    other_inverse, residual = lax.optimization_barrier((other_inverse, residual))
    solve_rows = jnp.concatenate(
        [
            jnp.where(panel == 0, turned_inverse, other_inverse),
            jnp.where(panel == 0, other_inverse, turned_inverse),
        ],
        axis=0,
    )
    window = exchanged(window, "ctr")
    window = window.reshape(shards * strip, LANES)

    planes = residual.reshape(PLANES, plane_points, target_count)
    backward = None
    for k in range(PLANES):
        part = lax.dot_general(
            pick(planes, plane ^ k), kernels[k], (((0,), (0,)), ((), ())), preferred_element_type=F32
        )
        backward = part if backward is None else backward + part
    backward = backward.reshape(groups, target_slice, shard_rows)
    near_pair = jnp.stack([pick(backward, group), pick(backward, group ^ 2)])
    far_pair = jnp.stack([pick(backward, group ^ 1), pick(backward, group ^ 3)]).astype(BF)
    near_pair = near_pair + swapped(far_pair, "pts", 1).astype(F32)
    gradient = near_pair[0] + swapped(near_pair[1].astype(BF), "pts", 2).astype(F32)
    gradient = gradient.T

    half = shards // HALVES
    sent = jax.ShapeDtypeStruct((half, strip, LANES), BF)
    packed = jax.ShapeDtypeStruct((strip, LANES), F32)
    first, low, high = whole(first_step, (sent, packed, packed), solve_rows, window)
    first = exchanged(first, "ctr", HALVES).reshape(half * strip, LANES)
    update = whole(middle_step, sent, factor_rows, first)
    update = exchanged(update, "ctr", HALVES).reshape(half * strip, LANES)
    solved = whole(
        last_step,
        jax.ShapeDtypeStruct((target_slice, own_rows), F32),
        panel.astype(jnp.int32).reshape(1),
        inverse_rows,
        update,
        low,
        high,
        scalars=1,
    )
    return (gradient, solved.T)


def solution(mesh):
    placed = (
        P(("pts", "ctr"), None),
        P(("pts", "ctr")),
        P(("pts", "ctr"), None),
        P(),
        P(),
        P("ctr", None),
        P("ctr", None),
        P(),
        P("ctr", None),
        P("ctr", None),
    )
    return jax.shard_map(
        body,
        mesh=mesh,
        in_specs=placed,
        out_specs=(P("ctr", "pts"), P("ctr", "pts")),
        check_vma=False,
    )
```

```python
import functools

import jax
import jax.numpy as jnp
from jax import lax
from jax.experimental import pallas as pl
from jax.experimental.pallas import tpu as pltpu
from jax.sharding import PartitionSpec as P

BF = jnp.bfloat16
F32 = jnp.float32
LANES = 128
PLANES = 4
HALVES = 2
TILE = 512
VMEM = pl.BlockSpec(memory_space=pltpu.VMEM)


def exchanged(pieces, axis, parts=1):
    size = lax.axis_size(axis) // parts
    groups = [[part * size + i for i in range(size)] for part in range(parts)]
    return lax.all_to_all(
        pieces, axis, 0, 0, tiled=True, axis_index_groups=groups if parts > 1 else None
    )


def copies(x, count):
    return jnp.broadcast_to(x[None], (count, *x.shape))


def swapped(x, axis, bits):
    return lax.ppermute(x, axis, [(i, i ^ bits) for i in range(lax.axis_size(axis))])


def pick(x, index):
    return lax.dynamic_index_in_dim(x, index, 0, keepdims=False)


def scale_step(
    centers_ref, scale_ref, local_ref, scaled_ref, norm_ref, chosen_ref, extra_ref, slots, sems, outs
):
    loads = []
    for i in range(slots.shape[0]):
        rows = pl.ds(i * TILE, TILE)
        loads.append(pltpu.make_async_copy(centers_ref.at[rows, :], slots.at[i], sems.at[i]))
        loads[-1].start()
    count = chosen_ref.shape[0]
    chosen = jnp.zeros(chosen_ref.shape, F32)
    lane = lax.broadcasted_iota(jnp.int32, (count, TILE), 1)
    saves = []
    for i, load in enumerate(loads):
        rows = pl.ds(i * TILE, TILE)
        load.wait()
        scaled = (slots[i].astype(F32) * scale_ref[...]).astype(BF)
        slots[i] = scaled
        saves.append(pltpu.make_async_copy(slots.at[i], scaled_ref.at[rows, :], outs.at[i]))
        saves[-1].start()
        wide = scaled.astype(F32)
        norm = 0.5 * jnp.sum(wide * wide, axis=1, keepdims=True)
        norm_ref[:, rows] = jnp.broadcast_to(norm, (TILE, LANES)).T[0:1, :]
        pick_rows = (lane + i * TILE == local_ref[...]).astype(F32).astype(BF)
        chosen += jnp.dot(pick_rows, scaled, preferred_element_type=F32)
    chosen_ref[...] = chosen.astype(BF)
    norm = 0.5 * jnp.sum(chosen * chosen, axis=1, keepdims=True)
    extra_ref[...] = jnp.broadcast_to(norm, (count, LANES)).T[0:1, :]
    for save in saves:
        save.wait()


def scaled_and_norm(centers, scale, local):
    total, depth = centers.shape
    count = local.shape[0]
    steps = total // TILE
    return pl.pallas_call(
        scale_step,
        out_shape=(
            pltpu.HBM((total, depth), BF),
            jax.ShapeDtypeStruct((1, total), F32),
            jax.ShapeDtypeStruct((count, depth), BF),
            jax.ShapeDtypeStruct((1, count), F32),
        ),
        in_specs=[pl.BlockSpec(memory_space=pltpu.HBM), VMEM, VMEM],
        out_specs=[pl.BlockSpec(memory_space=pltpu.HBM)] + [VMEM] * 3,
        scratch_shapes=[pltpu.VMEM((steps, TILE, depth), BF)]
        + [pltpu.SemaphoreType.DMA((steps,))] * 2,
        compiler_params=pltpu.CompilerParams(vmem_limit_bytes=24 * 1024 * 1024),
        cost_estimate=pl.CostEstimate(
            flops=4 * total * depth, bytes_accessed=2 * total * depth, transcendentals=0
        ),
    )(pltpu.with_memory_space_constraint(centers, pltpu.HBM), scale, local)


def kernel_block(
    held, slot_ref, points_ref, scale_ref, centers_ref, norm_ref, coef_ref, chosen_ref, extra_ref, *refs
):
    kernel_ref, value_ref, picked_ref, slots, sems, *stream = refs[2 * held :]
    steps = centers_ref.shape[0] // TILE
    loads = []
    if stream:
        for i in range(steps):
            rows = pl.ds(i * TILE, TILE)
            loads.append(
                pltpu.make_async_copy(centers_ref.at[rows, :], stream[0].at[i], stream[1].at[i])
            )
            loads[-1].start()
    samples = (points_ref[...].astype(F32) * scale_ref[...]).astype(BF)
    wide = samples.astype(F32)
    left = 0.5 * jnp.sum(wide * wide, axis=1, keepdims=True)

    def block(anchors, norm):
        products = lax.dot_general(
            samples, anchors, (((1,), (1,)), ((), ())), preferred_element_type=F32
        )
        return jnp.exp(products - left - norm).astype(BF)

    if held:
        value_ref[...] = refs[0][...]
        picked_ref[...] = refs[1][...]
    total = jnp.zeros(value_ref.shape[1:], F32)
    saves = []
    before = None
    for i in range(steps):
        rows = pl.ds(i * TILE, TILE)
        if stream:
            loads[i].wait()
        anchors = stream[0][i] if stream else centers_ref[rows, :]
        current = block(anchors, norm_ref[:, rows])
        slots[i] = current
        saves.append(pltpu.make_async_copy(slots.at[i], kernel_ref.at[:, rows], sems.at[i]))
        saves[-1].start()
        if before is not None:
            coef = coef_ref[pl.ds((i - 1) * TILE, TILE), :]
            total += jnp.dot(before, coef, preferred_element_type=F32)
        before = current
    coef = coef_ref[pl.ds((steps - 1) * TILE, TILE), :]
    total += jnp.dot(before, coef, preferred_element_type=F32)
    value_ref[slot_ref[0]] = total.astype(value_ref.dtype)
    picked_ref[slot_ref[0]] = block(chosen_ref[...], extra_ref[...])
    for save in saves:
        save.wait()


def kernel_and_value(slot, samples, scale, anchors, norms, coefficients, chosen, extra, *held):
    count, depth = samples.shape
    total, cols = coefficients.shape
    steps = total // TILE
    space = VMEM if held else pl.BlockSpec(memory_space=pltpu.HBM)
    loaded = [pltpu.VMEM((steps, TILE, depth), BF), pltpu.SemaphoreType.DMA((steps,))]
    args = [samples, scale, anchors if held else pltpu.with_memory_space_constraint(anchors, pltpu.HBM)]
    args += [norms, coefficients, chosen, extra, *held]
    return pl.pallas_call(
        functools.partial(kernel_block, bool(held)),
        out_shape=(
            pltpu.HBM((count, total), BF),
            jax.ShapeDtypeStruct((PLANES, count, cols), BF),
            jax.ShapeDtypeStruct((PLANES, count, chosen.shape[0]), BF),
        ),
        in_specs=[pl.BlockSpec(memory_space=pltpu.SMEM), VMEM, VMEM, space]
        + [VMEM] * (len(args) - 3),
        out_specs=[pl.BlockSpec(memory_space=pltpu.HBM), VMEM, VMEM],
        scratch_shapes=[pltpu.VMEM((steps, count, TILE), BF), pltpu.SemaphoreType.DMA((steps,))]
        + ([] if held else loaded),
        compiler_params=pltpu.CompilerParams(vmem_limit_bytes=24 * 1024 * 1024),
        cost_estimate=pl.CostEstimate(
            flops=2 * count * total * (depth + cols),
            bytes_accessed=2 * count * total,
            transcendentals=count * total,
        ),
    )(slot, *args)


def lane_block(shape, width, index):
    lane = lax.broadcasted_iota(jnp.int32, shape, len(shape) - 1)
    return (lane >= index * width) & (lane < (index + 1) * width)


def turned(x, lanes):
    lanes = lanes % LANES
    return pltpu.roll(x, lanes, 1) if lanes else x


def folded_sum(product, fold, strip, blocks):
    width = LANES // fold
    out = None
    for f in range(fold):
        total = None
        for r in blocks:
            row = (r * fold + f) * strip
            part = turned(product[row : row + strip, :], (f - r) * width)
            total = part if total is None else total + part
        out = total if out is None else jnp.where(lane_block(total.shape, width, f), total, out)
    return out


def first_step(matrix_ref, window_ref, sent_ref, low_ref, high_ref):
    strip = sent_ref.shape[1]
    fold = int(round((matrix_ref.shape[0] // strip) ** 0.5))
    product = jnp.dot(matrix_ref[...], window_ref[...], preferred_element_type=F32)
    low = folded_sum(product, fold, strip, range(fold // HALVES))
    high = folded_sum(product, fold, strip, range(fold // HALVES, fold))
    low_ref[...] = low
    high_ref[...] = high
    sent_ref[...] = jnp.broadcast_to(low.astype(BF)[None], sent_ref.shape)


def natural_product(matrix_ref, data_ref, rows_ref):
    parts, fold, strip, _ = rows_ref.shape
    data = data_ref[...].astype(F32).reshape(parts * strip, LANES)
    for f in range(fold):
        piece = turned(data, -f * (LANES // fold)).astype(BF)
        rows_ref[:, f] = piece.reshape(parts, strip, LANES)
    right = rows_ref[...].reshape(parts * fold * strip, LANES)
    return jnp.dot(matrix_ref[...].astype(BF), right, preferred_element_type=F32)


def middle_step(matrix_ref, data_ref, sent_ref, rows_ref):
    product = natural_product(matrix_ref, data_ref, rows_ref)
    _, fold, strip, _ = rows_ref.shape
    width = LANES // fold
    out = None
    for f in range(fold):
        part = turned(product[f * strip : (f + 1) * strip, :], f * width)
        out = part if out is None else jnp.where(lane_block(part.shape, width, f), part, out)
    sent_ref[...] = jnp.broadcast_to(out.astype(BF)[None], sent_ref.shape)


def last_step(panel_ref, matrix_ref, data_ref, low_ref, high_ref, out_ref, rows_ref):
    product = natural_product(matrix_ref, data_ref, rows_ref)
    _, fold, strip, _ = rows_ref.shape
    width = LANES // fold
    low = jnp.concatenate([turned(low_ref[...], -f * width) for f in range(fold)], axis=0)
    high = jnp.concatenate([turned(high_ref[...], -f * width) for f in range(fold)], axis=0)
    solved = jnp.where(panel_ref[0] == 0, low, high - product)
    out_ref[...] = solved.T[:width, :]


def panel_call(body, shape, matrix, parts, fold, data, *more, scalars=()):
    rows, depth = matrix.shape[0], parts * data.shape[0] // parts * fold
    strip = data.shape[0] // parts
    return pl.pallas_call(
        body,
        grid=(1,),
        out_shape=shape,
        in_specs=[pl.BlockSpec(memory_space=pltpu.SMEM)] * len(scalars)
        + [pl.BlockSpec((rows, depth), lambda i: (0, 0))]
        + [VMEM] * (1 + len(more)),
        out_specs=VMEM,
        scratch_shapes=[pltpu.VMEM((parts, fold, strip, LANES), BF)],
        compiler_params=pltpu.CompilerParams(vmem_limit_bytes=16 * 1024 * 1024),
    )(*scalars, matrix, data, *more)


def window_step(chosen_ref, residual_ref, window_ref):
    window_ref[...] = lax.dot_general(
        chosen_ref[...], residual_ref[...], (((0,), (0,)), ((), ())), preferred_element_type=F32
    )


def fold_step(group_ref, parts_ref, sent_ref):
    groups = parts_ref.shape[0]
    strip = sent_ref.shape[1]
    width = LANES // groups
    window = jnp.sum(parts_ref[...].astype(F32), axis=0)
    result = None
    for p in range(groups):
        out = None
        for r in range(window.shape[0] // strip):
            part = turned(window[r * strip : (r + 1) * strip, :], (r - p) * width)
            out = part if out is None else jnp.where(lane_block(part.shape, width, r), part, out)
        result = out if result is None else jnp.where(group_ref[0] == p, out, result)
    sent_ref[...] = jnp.broadcast_to(result.astype(BF)[None], sent_ref.shape)


def whole(body, shapes, *args, scalars=0):
    return pl.pallas_call(
        body,
        out_shape=shapes,
        in_specs=[pl.BlockSpec(memory_space=pltpu.SMEM)] * scalars + [VMEM] * (len(args) - scalars),
        out_specs=jax.tree.map(lambda _: VMEM, shapes),
        compiler_params=pltpu.CompilerParams(vmem_limit_bytes=16 * 1024 * 1024),
    )(*args)


def half_norm(rows):
    return 0.5 * jnp.sum(jnp.square(rows.astype(F32)), axis=-1)


def class_lookup(labels, table):
    classes = jnp.arange(table.shape[0], dtype=jnp.int32)
    return jnp.sum(jnp.where(labels[:, None] == classes[None, :], table[None, :], 0.0), axis=1)


def body(
    points,
    point_class,
    targets,
    class_weight,
    inv_scale,
    centers,
    coefficients,
    center_index,
    factor,
    panel_inverse,
):
    groups = lax.axis_size("pts")
    shards = lax.axis_size("ctr")
    shard = lax.axis_index("ctr")
    group = lax.axis_index("pts")
    own_points, depth = points.shape
    shard_rows = centers.shape[0]
    target_count = targets.shape[1]
    target_slice = target_count // groups
    own_rows = center_index.shape[0] // shards
    panel_rows = panel_inverse.shape[1]
    panel_shards = panel_rows // own_rows
    panel = shard // panel_shards
    fold = LANES // target_slice
    strip = own_rows // fold
    plane_size = shards // PLANES
    plane = shard // plane_size
    plane_points = plane_size * own_points

    plane_rows = exchanged(copies(points, plane_size), "ctr", PLANES)
    plane_rows = plane_rows.reshape(plane_points, depth)
    blocks = center_index.reshape(own_rows, shards)
    order = blocks[0] // shard_rows
    here = order == shard
    local = jnp.sum(jnp.where(here[None, :], blocks - shard * shard_rows, 0), axis=1)
    scale = inv_scale[None, :]
    scaled_centers, center_norm, chosen, extra = scaled_and_norm(centers, scale, local[:, None])
    plane_rows, extra = lax.optimization_barrier((plane_rows, extra))
    chunks = [plane_rows] + [None] * (PLANES - 1)
    for k in (2, 1, 3):
        chunks[k] = swapped(plane_rows, "ctr", k * plane_size)
    held = ()
    kernels = [None] * PLANES
    for k in (0, 1, 3, 2):
        slot = (plane ^ k).astype(jnp.int32).reshape(1)
        kernels[k], *held = kernel_and_value(
            slot, chunks[k], scale, scaled_centers, center_norm, coefficients, chosen, extra, *held
        )
    values, picked = held
    values, panel_inverse = lax.optimization_barrier((values, panel_inverse))

    place = (order[:, None] == jnp.arange(shards, dtype=jnp.int32)[None, :]).astype(BF)

    inverse = panel_inverse.astype(BF)
    count = panel_rows // (strip * shards)
    turned_inverse = jnp.einsum(
        "rhqj,js->hrsq", inverse.reshape(own_rows, count, strip, shards), place
    ).reshape(count * own_rows, shards * strip)

    own_weight = class_lookup(point_class, class_weight)
    shares = exchanged(values.reshape(shards, own_points, target_count), "ctr")
    predicted = jnp.sum(shares.astype(F32), axis=0)
    own_residual = (own_weight[:, None] * (predicted - targets)).astype(BF)
    residual = exchanged(copies(own_residual, shards), "ctr")
    residual = residual.reshape(shards * own_points, target_count)

    index = group.astype(jnp.int32).reshape(1)
    window = whole(
        window_step,
        jax.ShapeDtypeStruct((own_rows, target_count), F32),
        picked.reshape(shards * own_points, own_rows),
        residual,
    )
    parts = lax.all_gather(window, "pts")
    sent = jax.ShapeDtypeStruct((shards, strip, LANES), BF)
    window = whole(fold_step, sent, index, parts, scalars=1)
    window, turned_inverse = lax.optimization_barrier((window, turned_inverse))
    other_inverse = swapped(turned_inverse, "ctr", panel_shards)
    other_inverse, residual = lax.optimization_barrier((other_inverse, residual))
    solve_rows = jnp.concatenate(
        [
            jnp.where(panel == 0, turned_inverse, other_inverse),
            jnp.where(panel == 0, other_inverse, turned_inverse),
        ],
        axis=0,
    )
    window = exchanged(window, "ctr")
    window = window.reshape(shards * strip, LANES)

    planes = residual.reshape(PLANES, plane_points, target_count)
    backward = None
    for k in range(PLANES):
        part = lax.dot_general(
            pick(planes, plane ^ k), kernels[k], (((0,), (0,)), ((), ())), preferred_element_type=F32
        )
        backward = part if backward is None else backward + part
    backward = backward.reshape(groups, target_slice, shard_rows)
    near_pair = jnp.stack([pick(backward, group), pick(backward, group ^ 2)])
    far_pair = jnp.stack([pick(backward, group ^ 1), pick(backward, group ^ 3)]).astype(BF)
    near_pair = near_pair + swapped(far_pair, "pts", 1).astype(F32)
    gradient = near_pair[0] + swapped(near_pair[1].astype(BF), "pts", 2).astype(F32)
    gradient = gradient.T

    half = shards // HALVES
    sent = jax.ShapeDtypeStruct((half, strip, LANES), BF)
    packed = jax.ShapeDtypeStruct((strip, LANES), F32)
    first, low, high = whole(first_step, (sent, packed, packed), solve_rows, window)
    first = exchanged(first, "ctr", HALVES).reshape(half * strip, LANES)
    update = panel_call(middle_step, sent, factor, half, fold, first)
    update = exchanged(update, "ctr", HALVES).reshape(half * strip, LANES)
    solved = panel_call(
        last_step,
        jax.ShapeDtypeStruct((target_slice, own_rows), F32),
        panel_inverse,
        half,
        fold,
        update,
        low,
        high,
        scalars=(panel.astype(jnp.int32).reshape(1),),
    )
    return (gradient, solved.T)


def solution(mesh):
    placed = (
        P(("pts", "ctr"), None),
        P(("pts", "ctr")),
        P(("pts", "ctr"), None),
        P(),
        P(),
        P("ctr", None),
        P("ctr", None),
        P(),
        P("ctr", None),
        P("ctr", None),
    )
    return jax.shard_map(
        body,
        mesh=mesh,
        in_specs=placed,
        out_specs=(P("ctr", "pts"), P("ctr", "pts")),
        check_vma=False,
    )
```

```python
import functools

import jax
import jax.numpy as jnp
from jax import lax
from jax.experimental import pallas as pl
from jax.experimental.pallas import tpu as pltpu
from jax.sharding import PartitionSpec as P

BF = jnp.bfloat16
F32 = jnp.float32
LANES = 128
PLANES = 4
HALVES = 2
TILE = 512
VMEM = pl.BlockSpec(memory_space=pltpu.VMEM)


def exchanged(pieces, axis, parts=1):
    size = lax.axis_size(axis) // parts
    groups = [[part * size + i for i in range(size)] for part in range(parts)]
    return lax.all_to_all(
        pieces, axis, 0, 0, tiled=True, axis_index_groups=groups if parts > 1 else None
    )


def copies(x, count):
    return jnp.broadcast_to(x[None], (count, *x.shape))


def swapped(x, axis, bits):
    return lax.ppermute(x, axis, [(i, i ^ bits) for i in range(lax.axis_size(axis))])


def pick(x, index):
    return lax.dynamic_index_in_dim(x, index, 0, keepdims=False)


def scale_step(
    centers_ref, scale_ref, local_ref, scaled_ref, norm_ref, chosen_ref, extra_ref, slots, sems, outs
):
    loads = []
    for i in range(slots.shape[0]):
        rows = pl.ds(i * TILE, TILE)
        loads.append(pltpu.make_async_copy(centers_ref.at[rows, :], slots.at[i], sems.at[i]))
        loads[-1].start()
    count = chosen_ref.shape[0]
    chosen = jnp.zeros(chosen_ref.shape, F32)
    lane = lax.broadcasted_iota(jnp.int32, (count, TILE), 1)
    saves = []
    for i, load in enumerate(loads):
        rows = pl.ds(i * TILE, TILE)
        load.wait()
        scaled = (slots[i].astype(F32) * scale_ref[...]).astype(BF)
        slots[i] = scaled
        saves.append(pltpu.make_async_copy(slots.at[i], scaled_ref.at[rows, :], outs.at[i]))
        saves[-1].start()
        wide = scaled.astype(F32)
        norm = 0.5 * jnp.sum(wide * wide, axis=1, keepdims=True)
        norm_ref[:, rows] = jnp.broadcast_to(norm, (TILE, LANES)).T[0:1, :]
        pick_rows = (lane + i * TILE == local_ref[...]).astype(F32).astype(BF)
        chosen += jnp.dot(pick_rows, scaled, preferred_element_type=F32)
    chosen_ref[...] = chosen.astype(BF)
    norm = 0.5 * jnp.sum(chosen * chosen, axis=1, keepdims=True)
    extra_ref[...] = jnp.broadcast_to(norm, (count, LANES)).T[0:1, :]
    for save in saves:
        save.wait()


def scaled_and_norm(centers, scale, local):
    total, depth = centers.shape
    count = local.shape[0]
    steps = total // TILE
    return pl.pallas_call(
        scale_step,
        out_shape=(
            pltpu.HBM((total, depth), BF),
            jax.ShapeDtypeStruct((1, total), F32),
            jax.ShapeDtypeStruct((count, depth), BF),
            jax.ShapeDtypeStruct((1, count), F32),
        ),
        in_specs=[pl.BlockSpec(memory_space=pltpu.HBM), VMEM, VMEM],
        out_specs=[pl.BlockSpec(memory_space=pltpu.HBM)] + [VMEM] * 3,
        scratch_shapes=[pltpu.VMEM((steps, TILE, depth), BF)]
        + [pltpu.SemaphoreType.DMA((steps,))] * 2,
        compiler_params=pltpu.CompilerParams(vmem_limit_bytes=24 * 1024 * 1024),
        cost_estimate=pl.CostEstimate(
            flops=4 * total * depth, bytes_accessed=2 * total * depth, transcendentals=0
        ),
    )(pltpu.with_memory_space_constraint(centers, pltpu.HBM), scale, local)


def kernel_block(
    held, slot_ref, points_ref, scale_ref, centers_ref, norm_ref, coef_ref, chosen_ref, extra_ref, *refs
):
    kernel_ref, value_ref, picked_ref, *rest = refs[2 * held :]
    stream = [] if held else [rest[0], rest[-1]]
    slots, sems = rest[-2:] if held else rest[1:3]
    steps = centers_ref.shape[0] // TILE
    loads = []
    if stream:
        for i in range(steps):
            rows = pl.ds(i * TILE, TILE)
            loads.append(
                pltpu.make_async_copy(centers_ref.at[rows, :], stream[0].at[rows, :], stream[1].at[i])
            )
            loads[-1].start()
    samples = (points_ref[...].astype(F32) * scale_ref[...]).astype(BF)
    wide = samples.astype(F32)
    left = 0.5 * jnp.sum(wide * wide, axis=1, keepdims=True)

    def block(anchors, norm):
        products = lax.dot_general(
            samples, anchors, (((1,), (1,)), ((), ())), preferred_element_type=F32
        )
        return jnp.exp(products - left - norm).astype(BF)

    if held:
        value_ref[...] = refs[0][...]
        picked_ref[...] = refs[1][...]
    total = jnp.zeros(value_ref.shape[1:], F32)
    saves = []
    before = None
    for i in range(steps):
        rows = pl.ds(i * TILE, TILE)
        if stream:
            loads[i].wait()
        anchors = stream[0][rows, :] if stream else centers_ref[rows, :]
        current = block(anchors, norm_ref[:, rows])
        slots[i] = current
        saves.append(pltpu.make_async_copy(slots.at[i], kernel_ref.at[:, rows], sems.at[i]))
        saves[-1].start()
        if before is not None:
            coef = coef_ref[pl.ds((i - 1) * TILE, TILE), :]
            total += jnp.dot(before, coef, preferred_element_type=F32)
        before = current
    coef = coef_ref[pl.ds((steps - 1) * TILE, TILE), :]
    total += jnp.dot(before, coef, preferred_element_type=F32)
    value_ref[slot_ref[0]] = total.astype(value_ref.dtype)
    picked_ref[slot_ref[0]] = block(chosen_ref[...], extra_ref[...])
    for save in saves:
        save.wait()


def kernel_and_value(slot, samples, scale, anchors, norms, coefficients, chosen, extra, *held):
    count, depth = samples.shape
    total, cols = coefficients.shape
    steps = total // TILE
    space = VMEM if held else pl.BlockSpec(memory_space=pltpu.HBM)
    args = [samples, scale, anchors if held else pltpu.with_memory_space_constraint(anchors, pltpu.HBM)]
    args += [norms, coefficients, chosen, extra, *held]
    return pl.pallas_call(
        functools.partial(kernel_block, bool(held)),
        out_shape=(
            pltpu.HBM((count, total), BF),
            jax.ShapeDtypeStruct((PLANES, count, cols), BF),
            jax.ShapeDtypeStruct((PLANES, count, chosen.shape[0]), BF),
        )
        + (() if held else (pltpu.VMEM((total, depth), BF),)),
        in_specs=[pl.BlockSpec(memory_space=pltpu.SMEM), VMEM, VMEM, space]
        + [VMEM] * (len(args) - 3),
        out_specs=[pl.BlockSpec(memory_space=pltpu.HBM)] + [VMEM] * (2 if held else 3),
        scratch_shapes=[pltpu.VMEM((steps, count, TILE), BF)]
        + [pltpu.SemaphoreType.DMA((steps,))] * (1 if held else 2),
        compiler_params=pltpu.CompilerParams(vmem_limit_bytes=24 * 1024 * 1024),
        cost_estimate=pl.CostEstimate(
            flops=2 * count * total * (depth + cols),
            bytes_accessed=2 * count * total,
            transcendentals=count * total,
        ),
    )(slot, *args)


def lane_block(shape, width, index):
    lane = lax.broadcasted_iota(jnp.int32, shape, len(shape) - 1)
    return (lane >= index * width) & (lane < (index + 1) * width)


def turned(x, lanes):
    lanes = lanes % LANES
    return pltpu.roll(x, lanes, 1) if lanes else x


def folded_sum(product, fold, strip, blocks):
    width = LANES // fold
    out = None
    for f in range(fold):
        total = None
        for r in blocks:
            row = (r * fold + f) * strip
            part = turned(product[row : row + strip, :], (f - r) * width)
            total = part if total is None else total + part
        out = total if out is None else jnp.where(lane_block(total.shape, width, f), total, out)
    return out


def first_step(matrix_ref, window_ref, sent_ref, low_ref, high_ref):
    strip = sent_ref.shape[1]
    fold = int(round((matrix_ref.shape[0] // strip) ** 0.5))
    product = jnp.dot(matrix_ref[...], window_ref[...], preferred_element_type=F32)
    low = folded_sum(product, fold, strip, range(fold // HALVES))
    high = folded_sum(product, fold, strip, range(fold // HALVES, fold))
    low_ref[...] = low
    high_ref[...] = high
    sent_ref[...] = jnp.broadcast_to(low.astype(BF)[None], sent_ref.shape)


def natural_product(matrix_ref, data_ref, rows_ref):
    parts, fold, strip, _ = rows_ref.shape
    data = data_ref[...].astype(F32).reshape(parts * strip, LANES)
    for f in range(fold):
        piece = turned(data, -f * (LANES // fold)).astype(BF)
        rows_ref[:, f] = piece.reshape(parts, strip, LANES)
    right = rows_ref[...].reshape(parts * fold * strip, LANES)
    return jnp.dot(matrix_ref[...].astype(BF), right, preferred_element_type=F32)


def middle_step(matrix_ref, data_ref, sent_ref, rows_ref):
    product = natural_product(matrix_ref, data_ref, rows_ref)
    _, fold, strip, _ = rows_ref.shape
    width = LANES // fold
    out = None
    for f in range(fold):
        part = turned(product[f * strip : (f + 1) * strip, :], f * width)
        out = part if out is None else jnp.where(lane_block(part.shape, width, f), part, out)
    sent_ref[...] = jnp.broadcast_to(out.astype(BF)[None], sent_ref.shape)


def last_step(panel_ref, matrix_ref, data_ref, low_ref, high_ref, out_ref, rows_ref):
    product = natural_product(matrix_ref, data_ref, rows_ref)
    _, fold, strip, _ = rows_ref.shape
    width = LANES // fold
    low = jnp.concatenate([turned(low_ref[...], -f * width) for f in range(fold)], axis=0)
    high = jnp.concatenate([turned(high_ref[...], -f * width) for f in range(fold)], axis=0)
    solved = jnp.where(panel_ref[0] == 0, low, high - product)
    out_ref[...] = solved.T[:width, :]


def panel_call(body, shape, matrix, parts, fold, data, *more, scalars=()):
    rows, depth = matrix.shape[0], parts * data.shape[0] // parts * fold
    strip = data.shape[0] // parts
    return pl.pallas_call(
        body,
        grid=(1,),
        out_shape=shape,
        in_specs=[pl.BlockSpec(memory_space=pltpu.SMEM)] * len(scalars)
        + [pl.BlockSpec((rows, depth), lambda i: (0, 0))]
        + [VMEM] * (1 + len(more)),
        out_specs=VMEM,
        scratch_shapes=[pltpu.VMEM((parts, fold, strip, LANES), BF)],
        compiler_params=pltpu.CompilerParams(vmem_limit_bytes=16 * 1024 * 1024),
    )(*scalars, matrix, data, *more)


def residual_step(shares_ref, targets_ref, weight_ref, sent_ref):
    predicted = jnp.sum(shares_ref[...].astype(F32), axis=0)
    residual = (weight_ref[...] * (predicted - targets_ref[...])).astype(BF)
    sent_ref[...] = jnp.broadcast_to(residual[None], sent_ref.shape)


def window_step(chosen_ref, residual_ref, window_ref):
    window_ref[...] = lax.dot_general(
        chosen_ref[...], residual_ref[...], (((0,), (0,)), ((), ())), preferred_element_type=F32
    )


def fold_step(group_ref, parts_ref, sent_ref):
    groups = parts_ref.shape[0]
    strip = sent_ref.shape[1]
    width = LANES // groups
    window = jnp.sum(parts_ref[...].astype(F32), axis=0)
    result = None
    for p in range(groups):
        out = None
        for r in range(window.shape[0] // strip):
            part = turned(window[r * strip : (r + 1) * strip, :], (r - p) * width)
            out = part if out is None else jnp.where(lane_block(part.shape, width, r), part, out)
        result = out if result is None else jnp.where(group_ref[0] == p, out, result)
    sent_ref[...] = jnp.broadcast_to(result.astype(BF)[None], sent_ref.shape)


def whole(body, shapes, *args, scalars=0):
    return pl.pallas_call(
        body,
        out_shape=shapes,
        in_specs=[pl.BlockSpec(memory_space=pltpu.SMEM)] * scalars + [VMEM] * (len(args) - scalars),
        out_specs=jax.tree.map(lambda _: VMEM, shapes),
        compiler_params=pltpu.CompilerParams(vmem_limit_bytes=16 * 1024 * 1024),
    )(*args)


def class_lookup(labels, table):
    classes = jnp.arange(table.shape[0], dtype=jnp.int32)
    return jnp.sum(jnp.where(labels[:, None] == classes[None, :], table[None, :], 0.0), axis=1)


def body(
    points,
    point_class,
    targets,
    class_weight,
    inv_scale,
    centers,
    coefficients,
    center_index,
    factor,
    panel_inverse,
):
    groups = lax.axis_size("pts")
    shards = lax.axis_size("ctr")
    shard = lax.axis_index("ctr")
    group = lax.axis_index("pts")
    own_points, depth = points.shape
    shard_rows = centers.shape[0]
    target_count = targets.shape[1]
    target_slice = target_count // groups
    own_rows = center_index.shape[0] // shards
    panel_rows = panel_inverse.shape[1]
    panel_shards = panel_rows // own_rows
    panel = shard // panel_shards
    fold = LANES // target_slice
    strip = own_rows // fold
    plane_size = shards // PLANES
    plane = shard // plane_size
    plane_points = plane_size * own_points

    plane_rows = exchanged(copies(points, plane_size), "ctr", PLANES)
    plane_rows = plane_rows.reshape(plane_points, depth)
    blocks = center_index.reshape(own_rows, shards)
    order = blocks[0] // shard_rows
    here = order == shard
    local = jnp.sum(jnp.where(here[None, :], blocks - shard * shard_rows, 0), axis=1)
    scale = inv_scale[None, :]
    scaled_centers, center_norm, chosen, extra = scaled_and_norm(centers, scale, local[:, None])
    place = (order[:, None] == jnp.arange(shards, dtype=jnp.int32)[None, :]).astype(BF)

    inverse = panel_inverse.astype(BF)
    count = panel_rows // (strip * shards)
    turned_inverse = jnp.einsum(
        "rhqj,js->hrsq", inverse.reshape(own_rows, count, strip, shards), place
    ).reshape(count * own_rows, shards * strip)
    weight = class_lookup(point_class, class_weight)[:, None]
    plane_rows, extra, turned_inverse, weight = lax.optimization_barrier(
        (plane_rows, extra, turned_inverse, weight)
    )
    chunks = [plane_rows] + [None] * (PLANES - 1)
    for k in (2, 1, 3):
        chunks[k] = swapped(plane_rows, "ctr", k * plane_size)
    held = ()
    kernels = [None] * PLANES
    for k in (0, 1, 3, 2):
        slot = (plane ^ k).astype(jnp.int32).reshape(1)
        kernels[k], *held = kernel_and_value(
            slot, chunks[k], scale, scaled_centers, center_norm, coefficients, chosen, extra, *held
        )
        if k == 0:
            scaled_centers = held.pop()
    values, picked = held

    shares = exchanged(values.reshape(shards, own_points, target_count), "ctr")
    residual = whole(
        residual_step,
        jax.ShapeDtypeStruct((shards, own_points, target_count), BF),
        shares,
        targets,
        weight,
    )
    residual = exchanged(residual, "ctr").reshape(shards * own_points, target_count)

    index = group.astype(jnp.int32).reshape(1)
    window = whole(
        window_step,
        jax.ShapeDtypeStruct((own_rows, target_count), F32),
        picked.reshape(shards * own_points, own_rows),
        residual,
    )
    parts = lax.all_gather(window, "pts")
    sent = jax.ShapeDtypeStruct((shards, strip, LANES), BF)
    window = whole(fold_step, sent, index, parts, scalars=1)
    window, turned_inverse = lax.optimization_barrier((window, turned_inverse))
    other_inverse = swapped(turned_inverse, "ctr", panel_shards)
    other_inverse, residual = lax.optimization_barrier((other_inverse, residual))
    solve_rows = jnp.concatenate(
        [
            jnp.where(panel == 0, turned_inverse, other_inverse),
            jnp.where(panel == 0, other_inverse, turned_inverse),
        ],
        axis=0,
    )
    window = exchanged(window, "ctr")
    window = window.reshape(shards * strip, LANES)

    planes = residual.reshape(PLANES, plane_points, target_count)
    backward = None
    for k in range(PLANES):
        part = lax.dot_general(
            pick(planes, plane ^ k), kernels[k], (((0,), (0,)), ((), ())), preferred_element_type=F32
        )
        backward = part if backward is None else backward + part
    backward = backward.reshape(groups, target_slice, shard_rows)
    near_pair = jnp.stack([pick(backward, group), pick(backward, group ^ 2)])
    far_pair = jnp.stack([pick(backward, group ^ 1), pick(backward, group ^ 3)]).astype(BF)
    near_pair = near_pair + swapped(far_pair, "pts", 1).astype(F32)
    gradient = near_pair[0] + swapped(near_pair[1].astype(BF), "pts", 2).astype(F32)
    gradient = gradient.T

    half = shards // HALVES
    sent = jax.ShapeDtypeStruct((half, strip, LANES), BF)
    packed = jax.ShapeDtypeStruct((strip, LANES), F32)
    first, low, high = whole(first_step, (sent, packed, packed), solve_rows, window)
    first = exchanged(first, "ctr", HALVES).reshape(half * strip, LANES)
    update = panel_call(middle_step, sent, factor, half, fold, first)
    update = exchanged(update, "ctr", HALVES).reshape(half * strip, LANES)
    solved = panel_call(
        last_step,
        jax.ShapeDtypeStruct((target_slice, own_rows), F32),
        panel_inverse,
        half,
        fold,
        update,
        low,
        high,
        scalars=(panel.astype(jnp.int32).reshape(1),),
    )
    return (gradient, solved.T)


def solution(mesh):
    placed = (
        P(("pts", "ctr"), None),
        P(("pts", "ctr")),
        P(("pts", "ctr"), None),
        P(),
        P(),
        P("ctr", None),
        P("ctr", None),
        P(),
        P("ctr", None),
        P("ctr", None),
    )
    return jax.shard_map(
        body,
        mesh=mesh,
        in_specs=placed,
        out_specs=(P("ctr", "pts"), P("ctr", "pts")),
        check_vma=False,
    )
```

```python
import functools

import jax
import jax.numpy as jnp
from jax import lax
from jax.experimental import pallas as pl
from jax.experimental.pallas import tpu as pltpu
from jax.sharding import PartitionSpec as P

BF = jnp.bfloat16
F32 = jnp.float32
LANES = 128
PLANES = 4
HALVES = 2
TILE = 512
EARLY = 2
VMEM = pl.BlockSpec(memory_space=pltpu.VMEM)


def exchanged(pieces, axis, parts=1):
    size = lax.axis_size(axis) // parts
    groups = [[part * size + i for i in range(size)] for part in range(parts)]
    return lax.all_to_all(
        pieces, axis, 0, 0, tiled=True, axis_index_groups=groups if parts > 1 else None
    )


def copies(x, count):
    return jnp.broadcast_to(x[None], (count, *x.shape))


def swapped(x, axis, bits):
    return lax.ppermute(x, axis, [(i, i ^ bits) for i in range(lax.axis_size(axis))])


def scale_step(
    centers_ref, scale_ref, local_ref, scaled_ref, norm_ref, chosen_ref, extra_ref, slots, sems, outs
):
    loads = []
    for i in range(slots.shape[0]):
        rows = pl.ds(i * TILE, TILE)
        loads.append(pltpu.make_async_copy(centers_ref.at[rows, :], slots.at[i], sems.at[i]))
        loads[-1].start()
    count = chosen_ref.shape[0]
    chosen = jnp.zeros(chosen_ref.shape, F32)
    lane = lax.broadcasted_iota(jnp.int32, (count, TILE), 1)
    saves = []
    for i, load in enumerate(loads):
        rows = pl.ds(i * TILE, TILE)
        load.wait()
        scaled = (slots[i].astype(F32) * scale_ref[...]).astype(BF)
        slots[i] = scaled
        saves.append(pltpu.make_async_copy(slots.at[i], scaled_ref.at[rows, :], outs.at[i]))
        saves[-1].start()
        wide = scaled.astype(F32)
        norm = 0.5 * jnp.sum(wide * wide, axis=1, keepdims=True)
        norm_ref[:, rows] = jnp.broadcast_to(norm, (TILE, LANES)).T[0:1, :]
        pick_rows = (lane + i * TILE == local_ref[...]).astype(F32).astype(BF)
        chosen += jnp.dot(pick_rows, scaled, preferred_element_type=F32)
    chosen_ref[...] = chosen.astype(BF)
    norm = 0.5 * jnp.sum(chosen * chosen, axis=1, keepdims=True)
    extra_ref[...] = jnp.broadcast_to(norm, (count, LANES)).T[0:1, :]
    for save in saves:
        save.wait()


def scaled_and_norm(centers, scale, local):
    total, depth = centers.shape
    count = local.shape[0]
    steps = total // TILE
    return pl.pallas_call(
        scale_step,
        out_shape=(
            pltpu.HBM((total, depth), BF),
            jax.ShapeDtypeStruct((1, total), F32),
            jax.ShapeDtypeStruct((count, depth), BF),
            jax.ShapeDtypeStruct((1, count), F32),
        ),
        in_specs=[pl.BlockSpec(memory_space=pltpu.HBM), VMEM, VMEM],
        out_specs=[pl.BlockSpec(memory_space=pltpu.HBM)] + [VMEM] * 3,
        scratch_shapes=[pltpu.VMEM((steps, TILE, depth), BF)]
        + [pltpu.SemaphoreType.DMA((steps,))] * 2,
        compiler_params=pltpu.CompilerParams(vmem_limit_bytes=24 * 1024 * 1024),
        cost_estimate=pl.CostEstimate(
            flops=4 * total * depth, bytes_accessed=2 * total * depth, transcendentals=0
        ),
    )(pltpu.with_memory_space_constraint(centers, pltpu.HBM), scale, local)


def kernel_block(
    held, slot_ref, points_ref, scale_ref, centers_ref, norm_ref, coef_ref, chosen_ref, extra_ref, *refs
):
    kernel_ref, value_ref, picked_ref, *rest = refs[2 * held :]
    stream = [] if held else [rest[0], rest[-1]]
    slots, sems = rest[-2:] if held else rest[1:3]
    steps = centers_ref.shape[0] // TILE
    loads = []
    if stream:
        for i in range(steps):
            rows = pl.ds(i * TILE, TILE)
            loads.append(
                pltpu.make_async_copy(centers_ref.at[rows, :], stream[0].at[rows, :], stream[1].at[i])
            )
            loads[-1].start()
    samples = (points_ref[...].astype(F32) * scale_ref[...]).astype(BF)
    wide = samples.astype(F32)
    left = 0.5 * jnp.sum(wide * wide, axis=1, keepdims=True)

    def block(anchors, norm):
        products = lax.dot_general(
            samples, anchors, (((1,), (1,)), ((), ())), preferred_element_type=F32
        )
        return jnp.exp(products - left - norm).astype(BF)

    if held:
        value_ref[...] = refs[0][...]
        picked_ref[...] = refs[1][...]
    total = jnp.zeros(value_ref.shape[1:], F32)
    saves = []
    before = None
    for i in range(steps):
        rows = pl.ds(i * TILE, TILE)
        if stream and i in (0, EARLY):
            for load in loads[i : EARLY if i == 0 else steps]:
                load.wait()
        anchors = stream[0][rows, :] if stream else centers_ref[rows, :]
        current = block(anchors, norm_ref[:, rows])
        slots[i] = current
        saves.append(pltpu.make_async_copy(slots.at[i], kernel_ref.at[:, rows], sems.at[i]))
        saves[-1].start()
        if before is not None:
            coef = coef_ref[pl.ds((i - 1) * TILE, TILE), :]
            total += jnp.dot(before, coef, preferred_element_type=F32)
        before = current
    coef = coef_ref[pl.ds((steps - 1) * TILE, TILE), :]
    total += jnp.dot(before, coef, preferred_element_type=F32)
    value_ref[slot_ref[0]] = total.astype(value_ref.dtype)
    picked_ref[slot_ref[0]] = block(chosen_ref[...], extra_ref[...])
    for save in saves:
        save.wait()


def kernel_and_value(slot, samples, scale, anchors, norms, coefficients, chosen, extra, *held):
    count, depth = samples.shape
    total, cols = coefficients.shape
    steps = total // TILE
    space = VMEM if held else pl.BlockSpec(memory_space=pltpu.HBM)
    args = [samples, scale, anchors if held else pltpu.with_memory_space_constraint(anchors, pltpu.HBM)]
    args += [norms, coefficients, chosen, extra, *held]
    return pl.pallas_call(
        functools.partial(kernel_block, bool(held)),
        out_shape=(
            pltpu.HBM((count, total), BF),
            jax.ShapeDtypeStruct((PLANES, count, cols), BF),
            jax.ShapeDtypeStruct((PLANES, count, chosen.shape[0]), BF),
        )
        + (() if held else (pltpu.VMEM((total, depth), BF),)),
        in_specs=[pl.BlockSpec(memory_space=pltpu.SMEM), VMEM, VMEM, space]
        + [VMEM] * (len(args) - 3),
        out_specs=[pl.BlockSpec(memory_space=pltpu.HBM)] + [VMEM] * (2 if held else 3),
        scratch_shapes=[pltpu.VMEM((steps, count, TILE), BF)]
        + [pltpu.SemaphoreType.DMA((steps,))] * (1 if held else 2),
        compiler_params=pltpu.CompilerParams(vmem_limit_bytes=24 * 1024 * 1024),
        cost_estimate=pl.CostEstimate(
            flops=2 * count * total * (depth + cols),
            bytes_accessed=2 * count * total,
            transcendentals=count * total,
        ),
    )(slot, *args)


def lane_block(shape, width, index):
    lane = lax.broadcasted_iota(jnp.int32, shape, len(shape) - 1)
    return (lane >= index * width) & (lane < (index + 1) * width)


def turned(x, lanes):
    lanes = lanes % LANES
    return pltpu.roll(x, lanes, 1) if lanes else x


def folded_sum(product, fold, strip, blocks):
    width = LANES // fold
    out = None
    for f in range(fold):
        total = None
        for r in blocks:
            row = (r * fold + f) * strip
            part = turned(product[row : row + strip, :], (f - r) * width)
            total = part if total is None else total + part
        out = total if out is None else jnp.where(lane_block(total.shape, width, f), total, out)
    return out


def first_step(matrix_ref, window_ref, sent_ref, low_ref, high_ref):
    strip = sent_ref.shape[1]
    fold = int(round((matrix_ref.shape[0] // strip) ** 0.5))
    product = jnp.dot(matrix_ref[...], window_ref[...], preferred_element_type=F32)
    low = folded_sum(product, fold, strip, range(fold // HALVES))
    high = folded_sum(product, fold, strip, range(fold // HALVES, fold))
    low_ref[...] = low
    high_ref[...] = high
    sent_ref[...] = jnp.broadcast_to(low.astype(BF)[None], sent_ref.shape)


def natural_product(matrix_ref, data_ref, rows_ref):
    parts, fold, strip, _ = rows_ref.shape
    data = data_ref[...].astype(F32).reshape(parts * strip, LANES)
    for f in range(fold):
        piece = turned(data, -f * (LANES // fold)).astype(BF)
        rows_ref[:, f] = piece.reshape(parts, strip, LANES)
    right = rows_ref[...].reshape(parts * fold * strip, LANES)
    return jnp.dot(matrix_ref[...].astype(BF), right, preferred_element_type=F32)


def middle_step(matrix_ref, data_ref, sent_ref, rows_ref):
    product = natural_product(matrix_ref, data_ref, rows_ref)
    _, fold, strip, _ = rows_ref.shape
    width = LANES // fold
    out = None
    for f in range(fold):
        part = turned(product[f * strip : (f + 1) * strip, :], f * width)
        out = part if out is None else jnp.where(lane_block(part.shape, width, f), part, out)
    sent_ref[...] = jnp.broadcast_to(out.astype(BF)[None], sent_ref.shape)


def last_step(panel_ref, matrix_ref, data_ref, low_ref, high_ref, out_ref, rows_ref):
    product = natural_product(matrix_ref, data_ref, rows_ref)
    _, fold, strip, _ = rows_ref.shape
    width = LANES // fold
    low = jnp.concatenate([turned(low_ref[...], -f * width) for f in range(fold)], axis=0)
    high = jnp.concatenate([turned(high_ref[...], -f * width) for f in range(fold)], axis=0)
    solved = jnp.where(panel_ref[0] == 0, low, high - product)
    out_ref[...] = solved.T[:width, :]


def panel_call(body, shape, matrix, parts, fold, data, *more, scalars=()):
    rows, depth = matrix.shape[0], parts * data.shape[0] // parts * fold
    strip = data.shape[0] // parts
    return pl.pallas_call(
        body,
        grid=(1,),
        out_shape=shape,
        in_specs=[pl.BlockSpec(memory_space=pltpu.SMEM)] * len(scalars)
        + [pl.BlockSpec((rows, depth), lambda i: (0, 0))]
        + [VMEM] * (1 + len(more)),
        out_specs=VMEM,
        scratch_shapes=[pltpu.VMEM((parts, fold, strip, LANES), BF)],
        compiler_params=pltpu.CompilerParams(vmem_limit_bytes=16 * 1024 * 1024),
    )(*scalars, matrix, data, *more)


def residual_step(shares_ref, targets_ref, weight_ref, sent_ref):
    predicted = jnp.sum(shares_ref[...].astype(F32), axis=0)
    residual = (weight_ref[...] * (predicted - targets_ref[...])).astype(BF)
    sent_ref[...] = jnp.broadcast_to(residual[None], sent_ref.shape)


def window_step(chosen_ref, residual_ref, window_ref):
    window_ref[...] = lax.dot_general(
        chosen_ref[...], residual_ref[...], (((0,), (0,)), ((), ())), preferred_element_type=F32
    )


def fold_step(group_ref, parts_ref, sent_ref):
    groups = parts_ref.shape[0]
    strip = sent_ref.shape[1]
    width = LANES // groups
    window = jnp.sum(parts_ref[...].astype(F32), axis=0)
    result = None
    for p in range(groups):
        out = None
        for r in range(window.shape[0] // strip):
            part = turned(window[r * strip : (r + 1) * strip, :], (r - p) * width)
            out = part if out is None else jnp.where(lane_block(part.shape, width, r), part, out)
        result = out if result is None else jnp.where(group_ref[0] == p, out, result)
    sent_ref[...] = jnp.broadcast_to(result.astype(BF)[None], sent_ref.shape)


def gradient_step(index_ref, residual_ref, token_ref, *refs):
    blocks, (*parts, turned_ref, stage_ref) = refs[:PLANES], refs[PLANES:]
    count = residual_ref.shape[1]
    plane, group = index_ref[0], index_ref[1]

    @pl.when(pl.program_id(0) == 0)
    def _():
        for k in range(PLANES):
            piece = residual_ref[plane ^ k].astype(F32)
            turned_ref[:, k * count : (k + 1) * count] = piece.T.astype(BF)

    total = None
    for k in range(PLANES):
        left = turned_ref[:, k * count : (k + 1) * count]
        part = jnp.dot(left, blocks[k][...], preferred_element_type=F32)
        total = part if total is None else total + part
    stage_ref[...] = total.reshape(stage_ref.shape)
    for k, part_ref in enumerate(parts):
        part_ref[...] = stage_ref[group ^ k].astype(part_ref.dtype)


def gradient_parts(plane, group, residual, token, kernels, groups):
    _, count, cols = residual.shape
    total = kernels[0].shape[1]
    shape = (cols // groups, total)
    part = pl.BlockSpec((cols // groups, TILE), lambda i: (0, i))
    return pl.pallas_call(
        gradient_step,
        grid=(total // TILE,),
        out_shape=tuple(jax.ShapeDtypeStruct(shape, t) for t in (F32, BF, F32, BF)),
        in_specs=[
            pl.BlockSpec(memory_space=pltpu.SMEM),
            pl.BlockSpec(residual.shape, lambda i: (0, 0, 0)),
            pl.BlockSpec(token.shape, lambda i: (0, 0)),
        ]
        + [pl.BlockSpec((count, TILE), lambda i: (0, i))] * PLANES,
        out_specs=[part] * groups,
        scratch_shapes=[
            pltpu.VMEM((cols, PLANES * count), BF),
            pltpu.VMEM((groups, cols // groups, TILE), F32),
        ],
        compiler_params=pltpu.CompilerParams(vmem_limit_bytes=16 * 1024 * 1024),
        cost_estimate=pl.CostEstimate(
            flops=2 * PLANES * count * cols * total,
            bytes_accessed=2 * PLANES * count * total,
            transcendentals=0,
        ),
    )(
        jnp.stack([plane, group]).astype(jnp.int32),
        residual,
        token,
        *[pltpu.with_memory_space_constraint(kernel, pltpu.HBM) for kernel in kernels],
    )


def whole(body, shapes, *args, scalars=0):
    return pl.pallas_call(
        body,
        out_shape=shapes,
        in_specs=[pl.BlockSpec(memory_space=pltpu.SMEM)] * scalars + [VMEM] * (len(args) - scalars),
        out_specs=jax.tree.map(lambda _: VMEM, shapes),
        compiler_params=pltpu.CompilerParams(vmem_limit_bytes=16 * 1024 * 1024),
    )(*args)


def class_lookup(labels, table):
    classes = jnp.arange(table.shape[0], dtype=jnp.int32)
    return jnp.sum(jnp.where(labels[:, None] == classes[None, :], table[None, :], 0.0), axis=1)


def body(
    points,
    point_class,
    targets,
    class_weight,
    inv_scale,
    centers,
    coefficients,
    center_index,
    factor,
    panel_inverse,
):
    groups = lax.axis_size("pts")
    shards = lax.axis_size("ctr")
    shard = lax.axis_index("ctr")
    group = lax.axis_index("pts")
    own_points, depth = points.shape
    shard_rows = centers.shape[0]
    target_count = targets.shape[1]
    target_slice = target_count // groups
    own_rows = center_index.shape[0] // shards
    panel_rows = panel_inverse.shape[1]
    panel_shards = panel_rows // own_rows
    panel = shard // panel_shards
    fold = LANES // target_slice
    strip = own_rows // fold
    plane_size = shards // PLANES
    plane = shard // plane_size
    plane_points = plane_size * own_points

    plane_rows = exchanged(copies(points, plane_size), "ctr", PLANES)
    plane_rows = plane_rows.reshape(plane_points, depth)
    blocks = center_index.reshape(own_rows, shards)
    order = blocks[0] // shard_rows
    here = order == shard
    local = jnp.sum(jnp.where(here[None, :], blocks - shard * shard_rows, 0), axis=1)
    scale = inv_scale[None, :]
    scaled_centers, center_norm, chosen, extra = scaled_and_norm(centers, scale, local[:, None])
    place = (order[:, None] == jnp.arange(shards, dtype=jnp.int32)[None, :]).astype(BF)

    inverse = panel_inverse.astype(BF)
    count = panel_rows // (strip * shards)
    turned_inverse = jnp.einsum(
        "rhqj,js->hrsq", inverse.reshape(own_rows, count, strip, shards), place
    ).reshape(count * own_rows, shards * strip)
    weight = class_lookup(point_class, class_weight)[:, None]
    plane_rows, extra, turned_inverse, weight = lax.optimization_barrier(
        (plane_rows, extra, turned_inverse, weight)
    )
    chunks = [plane_rows] + [None] * (PLANES - 1)
    for k in (2, 1, 3):
        chunks[k] = swapped(plane_rows, "ctr", k * plane_size)
    held = ()
    kernels = [None] * PLANES
    for k in (0, 1, 3, 2):
        slot = (plane ^ k).astype(jnp.int32).reshape(1)
        kernels[k], *held = kernel_and_value(
            slot, chunks[k], scale, scaled_centers, center_norm, coefficients, chosen, extra, *held
        )
        if k == 0:
            scaled_centers = held.pop()
    values, picked = held

    shares = exchanged(values.reshape(shards, own_points, target_count), "ctr")
    residual = whole(
        residual_step,
        jax.ShapeDtypeStruct((shards, own_points, target_count), BF),
        shares,
        targets,
        weight,
    )
    residual, turned_inverse = lax.optimization_barrier((residual, turned_inverse))
    other_inverse = swapped(turned_inverse, "ctr", panel_shards)
    residual = exchanged(residual, "ctr").reshape(shards * own_points, target_count)
    residual, other_inverse = lax.optimization_barrier((residual, other_inverse))

    index = group.astype(jnp.int32).reshape(1)
    window = whole(
        window_step,
        jax.ShapeDtypeStruct((own_rows, target_count), F32),
        picked.reshape(shards * own_points, own_rows),
        residual,
    )
    parts = lax.all_gather(window, "pts")
    sent = jax.ShapeDtypeStruct((shards, strip, LANES), BF)
    window = whole(fold_step, sent, index, parts, scalars=1)
    token = window[0]
    solve_rows = jnp.concatenate(
        [
            jnp.where(panel == 0, turned_inverse, other_inverse),
            jnp.where(panel == 0, other_inverse, turned_inverse),
        ],
        axis=0,
    )
    window = exchanged(window, "ctr")
    window = window.reshape(shards * strip, LANES)

    planes = residual.reshape(PLANES, plane_points, target_count)
    near, far, near_other, far_other = gradient_parts(plane, group, planes, token, kernels, groups)
    far_other = swapped(far_other, "pts", 1)
    far = swapped(far, "pts", 1)

    half = shards // HALVES
    sent = jax.ShapeDtypeStruct((half, strip, LANES), BF)
    packed = jax.ShapeDtypeStruct((strip, LANES), F32)
    first, low, high = whole(first_step, (sent, packed, packed), solve_rows, window)
    first = exchanged(first, "ctr", HALVES).reshape(half * strip, LANES)
    first, near_other = lax.optimization_barrier((first, near_other))
    other = swapped((near_other + far_other.astype(F32)).astype(BF), "pts", 2)
    gradient = (near + far.astype(F32) + other.astype(F32)).T
    update = panel_call(middle_step, sent, factor, half, fold, first)
    update = exchanged(update, "ctr", HALVES).reshape(half * strip, LANES)
    solved = panel_call(
        last_step,
        jax.ShapeDtypeStruct((target_slice, own_rows), F32),
        panel_inverse,
        half,
        fold,
        update,
        low,
        high,
        scalars=(panel.astype(jnp.int32).reshape(1),),
    )
    return (gradient, solved.T)


def solution(mesh):
    placed = (
        P(("pts", "ctr"), None),
        P(("pts", "ctr")),
        P(("pts", "ctr"), None),
        P(),
        P(),
        P("ctr", None),
        P("ctr", None),
        P(),
        P("ctr", None),
        P("ctr", None),
    )
    return jax.shard_map(
        body,
        mesh=mesh,
        in_specs=placed,
        out_specs=(P("ctr", "pts"), P("ctr", "pts")),
        check_vma=False,
    )
```

```python
import functools

import jax
import jax.numpy as jnp
from jax import lax
from jax.experimental import pallas as pl
from jax.experimental.pallas import tpu as pltpu
from jax.sharding import PartitionSpec as P

BF = jnp.bfloat16
F32 = jnp.float32
LANES = 128
PLANES = 4
HALVES = 2
TILE = 512
EARLY = 2
VMEM = pl.BlockSpec(memory_space=pltpu.VMEM)


def exchanged(pieces, axis, parts=1):
    size = lax.axis_size(axis) // parts
    groups = [[part * size + i for i in range(size)] for part in range(parts)]
    return lax.all_to_all(
        pieces, axis, 0, 0, tiled=True, axis_index_groups=groups if parts > 1 else None
    )


def copies(x, count):
    return jnp.broadcast_to(x[None], (count, *x.shape))


def swapped(x, axis, bits):
    return lax.ppermute(x, axis, [(i, i ^ bits) for i in range(lax.axis_size(axis))])


def pick(x, index):
    return lax.dynamic_index_in_dim(x, index, 0, keepdims=False)


def scale_step(
    centers_ref, scale_ref, local_ref, scaled_ref, norm_ref, chosen_ref, extra_ref, slots, sems, outs
):
    loads = []
    for i in range(slots.shape[0]):
        rows = pl.ds(i * TILE, TILE)
        loads.append(pltpu.make_async_copy(centers_ref.at[rows, :], slots.at[i], sems.at[i]))
        loads[-1].start()
    count = chosen_ref.shape[0]
    chosen = jnp.zeros(chosen_ref.shape, F32)
    lane = lax.broadcasted_iota(jnp.int32, (count, TILE), 1)
    saves = []
    for i, load in enumerate(loads):
        rows = pl.ds(i * TILE, TILE)
        load.wait()
        scaled = (slots[i].astype(F32) * scale_ref[...]).astype(BF)
        slots[i] = scaled
        saves.append(pltpu.make_async_copy(slots.at[i], scaled_ref.at[rows, :], outs.at[i]))
        saves[-1].start()
        wide = scaled.astype(F32)
        norm = 0.5 * jnp.sum(wide * wide, axis=1, keepdims=True)
        norm_ref[:, rows] = jnp.broadcast_to(norm, (TILE, LANES)).T[0:1, :]
        pick_rows = (lane + i * TILE == local_ref[...]).astype(F32).astype(BF)
        chosen += jnp.dot(pick_rows, scaled, preferred_element_type=F32)
    chosen_ref[...] = chosen.astype(BF)
    norm = 0.5 * jnp.sum(chosen * chosen, axis=1, keepdims=True)
    extra_ref[...] = jnp.broadcast_to(norm, (count, LANES)).T[0:1, :]
    for save in saves:
        save.wait()


def scaled_and_norm(centers, scale, local):
    total, depth = centers.shape
    count = local.shape[0]
    steps = total // TILE
    return pl.pallas_call(
        scale_step,
        out_shape=(
            pltpu.HBM((total, depth), BF),
            jax.ShapeDtypeStruct((1, total), F32),
            jax.ShapeDtypeStruct((count, depth), BF),
            jax.ShapeDtypeStruct((1, count), F32),
        ),
        in_specs=[pl.BlockSpec(memory_space=pltpu.HBM), VMEM, VMEM],
        out_specs=[pl.BlockSpec(memory_space=pltpu.HBM)] + [VMEM] * 3,
        scratch_shapes=[pltpu.VMEM((steps, TILE, depth), BF)]
        + [pltpu.SemaphoreType.DMA((steps,))] * 2,
        compiler_params=pltpu.CompilerParams(vmem_limit_bytes=24 * 1024 * 1024),
        cost_estimate=pl.CostEstimate(
            flops=4 * total * depth, bytes_accessed=2 * total * depth, transcendentals=0
        ),
    )(pltpu.with_memory_space_constraint(centers, pltpu.HBM), scale, local)


def kernel_block(
    held, slot_ref, points_ref, scale_ref, centers_ref, norm_ref, coef_ref, chosen_ref, extra_ref, *refs
):
    kernel_ref, value_ref, picked_ref, slots, sems, *stream = refs[2 * held :]
    steps = centers_ref.shape[0] // TILE
    loads = []
    if stream:
        for i in range(steps):
            rows = pl.ds(i * TILE, TILE)
            loads.append(
                pltpu.make_async_copy(centers_ref.at[rows, :], stream[0].at[i], stream[1].at[i])
            )
            loads[-1].start()
    samples = (points_ref[...].astype(F32) * scale_ref[...]).astype(BF)
    wide = samples.astype(F32)
    left = 0.5 * jnp.sum(wide * wide, axis=1, keepdims=True)

    def block(anchors, norm):
        products = lax.dot_general(
            samples, anchors, (((1,), (1,)), ((), ())), preferred_element_type=F32
        )
        return jnp.exp(products - left - norm).astype(BF)

    if held:
        value_ref[...] = refs[0][...]
        picked_ref[...] = refs[1][...]
    total = jnp.zeros(value_ref.shape[1:], F32)
    saves = []
    before = None
    for i in range(steps):
        rows = pl.ds(i * TILE, TILE)
        if stream and i in (0, EARLY):
            for load in loads[i : EARLY if i == 0 else steps]:
                load.wait()
        anchors = stream[0][i] if stream else centers_ref[rows, :]
        current = block(anchors, norm_ref[:, rows])
        slots[i] = current
        saves.append(pltpu.make_async_copy(slots.at[i], kernel_ref.at[:, rows], sems.at[i]))
        saves[-1].start()
        if before is not None:
            coef = coef_ref[pl.ds((i - 1) * TILE, TILE), :]
            total += jnp.dot(before, coef, preferred_element_type=F32)
        before = current
    coef = coef_ref[pl.ds((steps - 1) * TILE, TILE), :]
    total += jnp.dot(before, coef, preferred_element_type=F32)
    value_ref[slot_ref[0]] = total.astype(value_ref.dtype)
    picked_ref[slot_ref[0]] = block(chosen_ref[...], extra_ref[...])
    for save in saves:
        save.wait()


def kernel_and_value(slot, samples, scale, anchors, norms, coefficients, chosen, extra, *held):
    count, depth = samples.shape
    total, cols = coefficients.shape
    steps = total // TILE
    space = VMEM if held else pl.BlockSpec(memory_space=pltpu.HBM)
    loaded = [pltpu.VMEM((steps, TILE, depth), BF), pltpu.SemaphoreType.DMA((steps,))]
    args = [samples, scale, anchors if held else pltpu.with_memory_space_constraint(anchors, pltpu.HBM)]
    args += [norms, coefficients, chosen, extra, *held]
    return pl.pallas_call(
        functools.partial(kernel_block, bool(held)),
        out_shape=(
            pltpu.HBM((count, total), BF),
            jax.ShapeDtypeStruct((PLANES, count, cols), BF),
            jax.ShapeDtypeStruct((PLANES, count, chosen.shape[0]), BF),
        ),
        in_specs=[pl.BlockSpec(memory_space=pltpu.SMEM), VMEM, VMEM, space]
        + [VMEM] * (len(args) - 3),
        out_specs=[pl.BlockSpec(memory_space=pltpu.HBM), VMEM, VMEM],
        scratch_shapes=[pltpu.VMEM((steps, count, TILE), BF), pltpu.SemaphoreType.DMA((steps,))]
        + ([] if held else loaded),
        compiler_params=pltpu.CompilerParams(vmem_limit_bytes=24 * 1024 * 1024),
        cost_estimate=pl.CostEstimate(
            flops=2 * count * total * (depth + cols),
            bytes_accessed=2 * count * total,
            transcendentals=count * total,
        ),
    )(slot, *args)


def lane_block(shape, width, index):
    lane = lax.broadcasted_iota(jnp.int32, shape, len(shape) - 1)
    return (lane >= index * width) & (lane < (index + 1) * width)


def turned(x, lanes):
    lanes = lanes % LANES
    return pltpu.roll(x, lanes, 1) if lanes else x


def folded_sum(product, fold, strip, blocks):
    width = LANES // fold
    out = None
    for f in range(fold):
        total = None
        for r in blocks:
            row = (r * fold + f) * strip
            part = turned(product[row : row + strip, :], (f - r) * width)
            total = part if total is None else total + part
        out = total if out is None else jnp.where(lane_block(total.shape, width, f), total, out)
    return out


def first_step(matrix_ref, window_ref, sent_ref, low_ref, high_ref):
    strip = sent_ref.shape[1]
    fold = int(round((matrix_ref.shape[0] // strip) ** 0.5))
    product = jnp.dot(matrix_ref[...], window_ref[...], preferred_element_type=F32)
    low = folded_sum(product, fold, strip, range(fold // HALVES))
    high = folded_sum(product, fold, strip, range(fold // HALVES, fold))
    low_ref[...] = low
    high_ref[...] = high
    sent_ref[...] = jnp.broadcast_to(low.astype(BF)[None], sent_ref.shape)


def natural_product(matrix_ref, data_ref, rows_ref):
    parts, fold, strip, _ = rows_ref.shape
    data = data_ref[...].astype(F32).reshape(parts * strip, LANES)
    for f in range(fold):
        piece = turned(data, -f * (LANES // fold)).astype(BF)
        rows_ref[:, f] = piece.reshape(parts, strip, LANES)
    right = rows_ref[...].reshape(parts * fold * strip, LANES)
    return jnp.dot(matrix_ref[...].astype(BF), right, preferred_element_type=F32)


def middle_step(matrix_ref, data_ref, sent_ref, rows_ref):
    product = natural_product(matrix_ref, data_ref, rows_ref)
    _, fold, strip, _ = rows_ref.shape
    width = LANES // fold
    out = None
    for f in range(fold):
        part = turned(product[f * strip : (f + 1) * strip, :], f * width)
        out = part if out is None else jnp.where(lane_block(part.shape, width, f), part, out)
    sent_ref[...] = jnp.broadcast_to(out.astype(BF)[None], sent_ref.shape)


def last_step(panel_ref, matrix_ref, data_ref, low_ref, high_ref, out_ref, rows_ref):
    product = natural_product(matrix_ref, data_ref, rows_ref)
    _, fold, strip, _ = rows_ref.shape
    width = LANES // fold
    low = jnp.concatenate([turned(low_ref[...], -f * width) for f in range(fold)], axis=0)
    high = jnp.concatenate([turned(high_ref[...], -f * width) for f in range(fold)], axis=0)
    solved = jnp.where(panel_ref[0] == 0, low, high - product)
    out_ref[...] = solved.T[:width, :]


def panel_call(body, shape, matrix, parts, fold, data, *more, scalars=()):
    rows, depth = matrix.shape[0], parts * data.shape[0] // parts * fold
    strip = data.shape[0] // parts
    return pl.pallas_call(
        body,
        grid=(1,),
        out_shape=shape,
        in_specs=[pl.BlockSpec(memory_space=pltpu.SMEM)] * len(scalars)
        + [pl.BlockSpec((rows, depth), lambda i: (0, 0))]
        + [VMEM] * (1 + len(more)),
        out_specs=VMEM,
        scratch_shapes=[pltpu.VMEM((parts, fold, strip, LANES), BF)],
        compiler_params=pltpu.CompilerParams(vmem_limit_bytes=16 * 1024 * 1024),
    )(*scalars, matrix, data, *more)


def residual_step(shares_ref, targets_ref, weight_ref, sent_ref):
    predicted = jnp.sum(shares_ref[...].astype(F32), axis=0)
    residual = (weight_ref[...] * (predicted - targets_ref[...])).astype(BF)
    sent_ref[...] = jnp.broadcast_to(residual[None], sent_ref.shape)


def window_step(chosen_ref, residual_ref, window_ref):
    window_ref[...] = lax.dot_general(
        chosen_ref[...], residual_ref[...], (((0,), (0,)), ((), ())), preferred_element_type=F32
    )


def fold_step(group_ref, parts_ref, sent_ref):
    groups = parts_ref.shape[0]
    strip = sent_ref.shape[1]
    width = LANES // groups
    window = jnp.sum(parts_ref[...].astype(F32), axis=0)
    result = None
    for p in range(groups):
        out = None
        for r in range(window.shape[0] // strip):
            part = turned(window[r * strip : (r + 1) * strip, :], (r - p) * width)
            out = part if out is None else jnp.where(lane_block(part.shape, width, r), part, out)
        result = out if result is None else jnp.where(group_ref[0] == p, out, result)
    sent_ref[...] = jnp.broadcast_to(result.astype(BF)[None], sent_ref.shape)


def whole(body, shapes, *args, scalars=0):
    return pl.pallas_call(
        body,
        out_shape=shapes,
        in_specs=[pl.BlockSpec(memory_space=pltpu.SMEM)] * scalars + [VMEM] * (len(args) - scalars),
        out_specs=jax.tree.map(lambda _: VMEM, shapes),
        compiler_params=pltpu.CompilerParams(vmem_limit_bytes=16 * 1024 * 1024),
    )(*args)


def half_norm(rows):
    return 0.5 * jnp.sum(jnp.square(rows.astype(F32)), axis=-1)


def class_lookup(labels, table):
    classes = jnp.arange(table.shape[0], dtype=jnp.int32)
    return jnp.sum(jnp.where(labels[:, None] == classes[None, :], table[None, :], 0.0), axis=1)


def body(
    points,
    point_class,
    targets,
    class_weight,
    inv_scale,
    centers,
    coefficients,
    center_index,
    factor,
    panel_inverse,
):
    groups = lax.axis_size("pts")
    shards = lax.axis_size("ctr")
    shard = lax.axis_index("ctr")
    group = lax.axis_index("pts")
    own_points, depth = points.shape
    shard_rows = centers.shape[0]
    target_count = targets.shape[1]
    target_slice = target_count // groups
    own_rows = center_index.shape[0] // shards
    panel_rows = panel_inverse.shape[1]
    panel_shards = panel_rows // own_rows
    panel = shard // panel_shards
    fold = LANES // target_slice
    strip = own_rows // fold
    plane_size = shards // PLANES
    plane = shard // plane_size
    plane_points = plane_size * own_points

    plane_rows = exchanged(copies(points, plane_size), "ctr", PLANES)
    plane_rows = plane_rows.reshape(plane_points, depth)
    blocks = center_index.reshape(own_rows, shards)
    order = blocks[0] // shard_rows
    here = order == shard
    local = jnp.sum(jnp.where(here[None, :], blocks - shard * shard_rows, 0), axis=1)
    scale = inv_scale[None, :]
    scaled_centers, center_norm, chosen, extra = scaled_and_norm(centers, scale, local[:, None])
    plane_rows, extra = lax.optimization_barrier((plane_rows, extra))
    chunks = [plane_rows] + [None] * (PLANES - 1)
    for k in (2, 1, 3):
        chunks[k] = swapped(plane_rows, "ctr", k * plane_size)
    held = ()
    kernels = [None] * PLANES
    for k in (0, 1, 3, 2):
        slot = (plane ^ k).astype(jnp.int32).reshape(1)
        kernels[k], *held = kernel_and_value(
            slot, chunks[k], scale, scaled_centers, center_norm, coefficients, chosen, extra, *held
        )
    values, picked = held
    values, panel_inverse = lax.optimization_barrier((values, panel_inverse))

    place = (order[:, None] == jnp.arange(shards, dtype=jnp.int32)[None, :]).astype(BF)

    inverse = panel_inverse.astype(BF)
    count = panel_rows // (strip * shards)
    turned_inverse = jnp.einsum(
        "rhqj,js->hrsq", inverse.reshape(own_rows, count, strip, shards), place
    ).reshape(count * own_rows, shards * strip)

    weight = class_lookup(point_class, class_weight)[:, None]
    shares = exchanged(values.reshape(shards, own_points, target_count), "ctr")
    residual = whole(
        residual_step,
        jax.ShapeDtypeStruct((shards, own_points, target_count), BF),
        shares,
        targets,
        weight,
    )
    residual = exchanged(residual, "ctr").reshape(shards * own_points, target_count)

    index = group.astype(jnp.int32).reshape(1)
    window = whole(
        window_step,
        jax.ShapeDtypeStruct((own_rows, target_count), F32),
        picked.reshape(shards * own_points, own_rows),
        residual,
    )
    parts = lax.all_gather(window, "pts")
    sent = jax.ShapeDtypeStruct((shards, strip, LANES), BF)
    window = whole(fold_step, sent, index, parts, scalars=1)
    window, turned_inverse = lax.optimization_barrier((window, turned_inverse))
    other_inverse = swapped(turned_inverse, "ctr", panel_shards)
    other_inverse, residual = lax.optimization_barrier((other_inverse, residual))
    solve_rows = jnp.concatenate(
        [
            jnp.where(panel == 0, turned_inverse, other_inverse),
            jnp.where(panel == 0, other_inverse, turned_inverse),
        ],
        axis=0,
    )
    window = exchanged(window, "ctr")
    window = window.reshape(shards * strip, LANES)

    planes = residual.reshape(PLANES, plane_points, target_count)
    backward = None
    for k in range(PLANES):
        part = lax.dot_general(
            pick(planes, plane ^ k), kernels[k], (((0,), (0,)), ((), ())), preferred_element_type=F32
        )
        backward = part if backward is None else backward + part
    backward = backward.reshape(groups, target_slice, shard_rows)
    near_pair = jnp.stack([pick(backward, group), pick(backward, group ^ 2)])
    far_pair = jnp.stack([pick(backward, group ^ 1), pick(backward, group ^ 3)]).astype(BF)
    near_pair = near_pair + swapped(far_pair, "pts", 1).astype(F32)
    gradient = near_pair[0] + swapped(near_pair[1].astype(BF), "pts", 2).astype(F32)
    gradient = gradient.T

    half = shards // HALVES
    sent = jax.ShapeDtypeStruct((half, strip, LANES), BF)
    packed = jax.ShapeDtypeStruct((strip, LANES), F32)
    first, low, high = whole(first_step, (sent, packed, packed), solve_rows, window)
    first = exchanged(first, "ctr", HALVES).reshape(half * strip, LANES)
    update = panel_call(middle_step, sent, factor, half, fold, first)
    update = exchanged(update, "ctr", HALVES).reshape(half * strip, LANES)
    solved = panel_call(
        last_step,
        jax.ShapeDtypeStruct((target_slice, own_rows), F32),
        panel_inverse,
        half,
        fold,
        update,
        low,
        high,
        scalars=(panel.astype(jnp.int32).reshape(1),),
    )
    return (gradient, solved.T)


def solution(mesh):
    placed = (
        P(("pts", "ctr"), None),
        P(("pts", "ctr")),
        P(("pts", "ctr"), None),
        P(),
        P(),
        P("ctr", None),
        P("ctr", None),
        P(),
        P("ctr", None),
        P("ctr", None),
    )
    return jax.shard_map(
        body,
        mesh=mesh,
        in_specs=placed,
        out_specs=(P("ctr", "pts"), P("ctr", "pts")),
        check_vma=False,
    )
```

```python
import functools

import jax
import jax.numpy as jnp
from jax import lax
from jax.experimental import pallas as pl
from jax.experimental.pallas import tpu as pltpu
from jax.sharding import PartitionSpec as P

BF = jnp.bfloat16
F32 = jnp.float32
LANES = 128
PLANES = 4
HALVES = 2
TILE = 512
EARLY = 2
VMEM = pl.BlockSpec(memory_space=pltpu.VMEM)


def exchanged(pieces, axis, parts=1):
    size = lax.axis_size(axis) // parts
    groups = [[part * size + i for i in range(size)] for part in range(parts)]
    return lax.all_to_all(
        pieces, axis, 0, 0, tiled=True, axis_index_groups=groups if parts > 1 else None
    )


def copies(x, count):
    return jnp.broadcast_to(x[None], (count, *x.shape))


def swapped(x, axis, bits):
    return lax.ppermute(x, axis, [(i, i ^ bits) for i in range(lax.axis_size(axis))])


def pick(x, index):
    return lax.dynamic_index_in_dim(x, index, 0, keepdims=False)


def scale_step(
    centers_ref, scale_ref, local_ref, scaled_ref, norm_ref, chosen_ref, extra_ref, slots, sems, outs
):
    loads = []
    for i in range(slots.shape[0]):
        rows = pl.ds(i * TILE, TILE)
        loads.append(pltpu.make_async_copy(centers_ref.at[rows, :], slots.at[i], sems.at[i]))
        loads[-1].start()
    count = chosen_ref.shape[0]
    chosen = jnp.zeros(chosen_ref.shape, F32)
    lane = lax.broadcasted_iota(jnp.int32, (count, TILE), 1)
    saves = []
    for i, load in enumerate(loads):
        rows = pl.ds(i * TILE, TILE)
        load.wait()
        scaled = (slots[i].astype(F32) * scale_ref[...]).astype(BF)
        slots[i] = scaled
        saves.append(pltpu.make_async_copy(slots.at[i], scaled_ref.at[rows, :], outs.at[i]))
        saves[-1].start()
        wide = scaled.astype(F32)
        norm = 0.5 * jnp.sum(wide * wide, axis=1, keepdims=True)
        norm_ref[:, rows] = jnp.broadcast_to(norm, (TILE, LANES)).T[0:1, :]
        pick_rows = (lane + i * TILE == local_ref[...]).astype(F32).astype(BF)
        chosen += jnp.dot(pick_rows, scaled, preferred_element_type=F32)
    chosen_ref[...] = chosen.astype(BF)
    norm = 0.5 * jnp.sum(chosen * chosen, axis=1, keepdims=True)
    extra_ref[...] = jnp.broadcast_to(norm, (count, LANES)).T[0:1, :]
    for save in saves:
        save.wait()


def scaled_and_norm(centers, scale, local):
    total, depth = centers.shape
    count = local.shape[0]
    steps = total // TILE
    return pl.pallas_call(
        scale_step,
        out_shape=(
            pltpu.HBM((total, depth), BF),
            jax.ShapeDtypeStruct((1, total), F32),
            jax.ShapeDtypeStruct((count, depth), BF),
            jax.ShapeDtypeStruct((1, count), F32),
        ),
        in_specs=[pl.BlockSpec(memory_space=pltpu.HBM), VMEM, VMEM],
        out_specs=[pl.BlockSpec(memory_space=pltpu.HBM)] + [VMEM] * 3,
        scratch_shapes=[pltpu.VMEM((steps, TILE, depth), BF)]
        + [pltpu.SemaphoreType.DMA((steps,))] * 2,
        compiler_params=pltpu.CompilerParams(vmem_limit_bytes=24 * 1024 * 1024),
        cost_estimate=pl.CostEstimate(
            flops=4 * total * depth, bytes_accessed=2 * total * depth, transcendentals=0
        ),
    )(pltpu.with_memory_space_constraint(centers, pltpu.HBM), scale, local)


def kernel_block(
    held, slot_ref, points_ref, scale_ref, centers_ref, norm_ref, coef_ref, chosen_ref, extra_ref, *refs
):
    kernel_ref, value_ref, picked_ref, slots, sems, *stream = refs[2 * held :]
    steps = centers_ref.shape[0] // TILE
    loads = []
    if stream:
        for i in range(steps):
            rows = pl.ds(i * TILE, TILE)
            loads.append(
                pltpu.make_async_copy(centers_ref.at[rows, :], stream[0].at[i], stream[1].at[i])
            )
            loads[-1].start()
    samples = (points_ref[...].astype(F32) * scale_ref[...]).astype(BF)
    wide = samples.astype(F32)
    left = 0.5 * jnp.sum(wide * wide, axis=1, keepdims=True)

    def block(anchors, norm):
        products = lax.dot_general(
            samples, anchors, (((1,), (1,)), ((), ())), preferred_element_type=F32
        )
        return jnp.exp(products - left - norm).astype(BF)

    if held:
        value_ref[...] = refs[0][...]
        picked_ref[...] = refs[1][...]
    total = jnp.zeros(value_ref.shape[1:], F32)
    saves = []
    before = None
    for i in range(steps):
        rows = pl.ds(i * TILE, TILE)
        if stream and i in (0, EARLY):
            for load in loads[i : EARLY if i == 0 else steps]:
                load.wait()
        anchors = stream[0][i] if stream else centers_ref[rows, :]
        current = block(anchors, norm_ref[:, rows])
        slots[i] = current
        saves.append(pltpu.make_async_copy(slots.at[i], kernel_ref.at[:, rows], sems.at[i]))
        saves[-1].start()
        if before is not None:
            coef = coef_ref[pl.ds((i - 1) * TILE, TILE), :]
            total += jnp.dot(before, coef, preferred_element_type=F32)
        before = current
    coef = coef_ref[pl.ds((steps - 1) * TILE, TILE), :]
    total += jnp.dot(before, coef, preferred_element_type=F32)
    value_ref[slot_ref[0]] = total.astype(value_ref.dtype)
    picked_ref[slot_ref[0]] = block(chosen_ref[...], extra_ref[...])
    for save in saves:
        save.wait()


def kernel_and_value(slot, samples, scale, anchors, norms, coefficients, chosen, extra, *held):
    count, depth = samples.shape
    total, cols = coefficients.shape
    steps = total // TILE
    space = VMEM if held else pl.BlockSpec(memory_space=pltpu.HBM)
    loaded = [pltpu.VMEM((steps, TILE, depth), BF), pltpu.SemaphoreType.DMA((steps,))]
    args = [samples, scale, anchors if held else pltpu.with_memory_space_constraint(anchors, pltpu.HBM)]
    args += [norms, coefficients, chosen, extra, *held]
    return pl.pallas_call(
        functools.partial(kernel_block, bool(held)),
        out_shape=(
            pltpu.HBM((count, total), BF),
            jax.ShapeDtypeStruct((PLANES, count, cols), BF),
            jax.ShapeDtypeStruct((PLANES, count, chosen.shape[0]), BF),
        ),
        in_specs=[pl.BlockSpec(memory_space=pltpu.SMEM), VMEM, VMEM, space]
        + [VMEM] * (len(args) - 3),
        out_specs=[pl.BlockSpec(memory_space=pltpu.HBM), VMEM, VMEM],
        scratch_shapes=[pltpu.VMEM((steps, count, TILE), BF), pltpu.SemaphoreType.DMA((steps,))]
        + ([] if held else loaded),
        compiler_params=pltpu.CompilerParams(vmem_limit_bytes=24 * 1024 * 1024),
        cost_estimate=pl.CostEstimate(
            flops=2 * count * total * (depth + cols),
            bytes_accessed=2 * count * total,
            transcendentals=count * total,
        ),
    )(slot, *args)


def lane_block(shape, width, index):
    lane = lax.broadcasted_iota(jnp.int32, shape, len(shape) - 1)
    return (lane >= index * width) & (lane < (index + 1) * width)


def turned(x, lanes):
    lanes = lanes % LANES
    return pltpu.roll(x, lanes, 1) if lanes else x


def folded_sum(product, fold, strip, blocks):
    width = LANES // fold
    out = None
    for f in range(fold):
        total = None
        for r in blocks:
            row = (r * fold + f) * strip
            part = turned(product[row : row + strip, :], (f - r) * width)
            total = part if total is None else total + part
        out = total if out is None else jnp.where(lane_block(total.shape, width, f), total, out)
    return out


def first_step(matrix_ref, window_ref, sent_ref, low_ref, high_ref):
    strip = sent_ref.shape[1]
    fold = int(round((matrix_ref.shape[0] // strip) ** 0.5))
    product = jnp.dot(matrix_ref[...], window_ref[...], preferred_element_type=F32)
    low = folded_sum(product, fold, strip, range(fold // HALVES))
    high = folded_sum(product, fold, strip, range(fold // HALVES, fold))
    low_ref[...] = low
    high_ref[...] = high
    sent_ref[...] = jnp.broadcast_to(low.astype(BF)[None], sent_ref.shape)


def natural_product(matrix_ref, data_ref, rows_ref):
    parts, fold, strip, _ = rows_ref.shape
    data = data_ref[...].astype(F32).reshape(parts * strip, LANES)
    for f in range(fold):
        piece = turned(data, -f * (LANES // fold)).astype(BF)
        rows_ref[:, f] = piece.reshape(parts, strip, LANES)
    right = rows_ref[...].reshape(parts * fold * strip, LANES)
    return jnp.dot(matrix_ref[...].astype(BF), right, preferred_element_type=F32)


def middle_step(matrix_ref, data_ref, sent_ref, rows_ref):
    product = natural_product(matrix_ref, data_ref, rows_ref)
    _, fold, strip, _ = rows_ref.shape
    width = LANES // fold
    out = None
    for f in range(fold):
        part = turned(product[f * strip : (f + 1) * strip, :], f * width)
        out = part if out is None else jnp.where(lane_block(part.shape, width, f), part, out)
    sent_ref[...] = jnp.broadcast_to(out.astype(BF)[None], sent_ref.shape)


def last_step(panel_ref, matrix_ref, data_ref, low_ref, high_ref, out_ref, rows_ref):
    product = natural_product(matrix_ref, data_ref, rows_ref)
    _, fold, strip, _ = rows_ref.shape
    width = LANES // fold
    low = jnp.concatenate([turned(low_ref[...], -f * width) for f in range(fold)], axis=0)
    high = jnp.concatenate([turned(high_ref[...], -f * width) for f in range(fold)], axis=0)
    solved = jnp.where(panel_ref[0] == 0, low, high - product)
    out_ref[...] = solved.T[:width, :]


def panel_call(body, shape, matrix, parts, fold, data, *more, scalars=()):
    rows, depth = matrix.shape[0], parts * data.shape[0] // parts * fold
    strip = data.shape[0] // parts
    return pl.pallas_call(
        body,
        grid=(1,),
        out_shape=shape,
        in_specs=[pl.BlockSpec(memory_space=pltpu.SMEM)] * len(scalars)
        + [pl.BlockSpec((rows, depth), lambda i: (0, 0))]
        + [VMEM] * (1 + len(more)),
        out_specs=VMEM,
        scratch_shapes=[pltpu.VMEM((parts, fold, strip, LANES), BF)],
        compiler_params=pltpu.CompilerParams(vmem_limit_bytes=16 * 1024 * 1024),
    )(*scalars, matrix, data, *more)


def residual_step(shares_ref, targets_ref, weight_ref, sent_ref):
    predicted = jnp.sum(shares_ref[...].astype(F32), axis=0)
    residual = (weight_ref[...] * (predicted - targets_ref[...])).astype(BF)
    sent_ref[...] = jnp.broadcast_to(residual[None], sent_ref.shape)


def window_step(chosen_ref, residual_ref, window_ref):
    window = lax.dot_general(
        chosen_ref[...], residual_ref[...], (((0,), (0,)), ((), ())), preferred_element_type=F32
    )
    window_ref[...] = window.astype(window_ref.dtype)


def fold_step(group_ref, parts_ref, sent_ref):
    groups = parts_ref.shape[0]
    strip = sent_ref.shape[1]
    width = LANES // groups
    window = jnp.sum(parts_ref[...].astype(F32), axis=0)
    result = None
    for p in range(groups):
        out = None
        for r in range(window.shape[0] // strip):
            part = turned(window[r * strip : (r + 1) * strip, :], (r - p) * width)
            out = part if out is None else jnp.where(lane_block(part.shape, width, r), part, out)
        result = out if result is None else jnp.where(group_ref[0] == p, out, result)
    sent_ref[...] = jnp.broadcast_to(result.astype(BF)[None], sent_ref.shape)


def whole(body, shapes, *args, scalars=0):
    return pl.pallas_call(
        body,
        out_shape=shapes,
        in_specs=[pl.BlockSpec(memory_space=pltpu.SMEM)] * scalars + [VMEM] * (len(args) - scalars),
        out_specs=jax.tree.map(lambda _: VMEM, shapes),
        compiler_params=pltpu.CompilerParams(vmem_limit_bytes=16 * 1024 * 1024),
    )(*args)


def half_norm(rows):
    return 0.5 * jnp.sum(jnp.square(rows.astype(F32)), axis=-1)


def class_lookup(labels, table):
    classes = jnp.arange(table.shape[0], dtype=jnp.int32)
    return jnp.sum(jnp.where(labels[:, None] == classes[None, :], table[None, :], 0.0), axis=1)


def body(
    points,
    point_class,
    targets,
    class_weight,
    inv_scale,
    centers,
    coefficients,
    center_index,
    factor,
    panel_inverse,
):
    groups = lax.axis_size("pts")
    shards = lax.axis_size("ctr")
    shard = lax.axis_index("ctr")
    group = lax.axis_index("pts")
    own_points, depth = points.shape
    shard_rows = centers.shape[0]
    target_count = targets.shape[1]
    target_slice = target_count // groups
    own_rows = center_index.shape[0] // shards
    panel_rows = panel_inverse.shape[1]
    panel_shards = panel_rows // own_rows
    panel = shard // panel_shards
    fold = LANES // target_slice
    strip = own_rows // fold
    plane_size = shards // PLANES
    plane = shard // plane_size
    plane_points = plane_size * own_points

    plane_rows = exchanged(copies(points, plane_size), "ctr", PLANES)
    plane_rows = plane_rows.reshape(plane_points, depth)
    blocks = center_index.reshape(own_rows, shards)
    order = blocks[0] // shard_rows
    here = order == shard
    local = jnp.sum(jnp.where(here[None, :], blocks - shard * shard_rows, 0), axis=1)
    scale = inv_scale[None, :]
    scaled_centers, center_norm, chosen, extra = scaled_and_norm(centers, scale, local[:, None])
    plane_rows, extra = lax.optimization_barrier((plane_rows, extra))
    chunks = [plane_rows] + [None] * (PLANES - 1)
    for k in (2, 1, 3):
        chunks[k] = swapped(plane_rows, "ctr", k * plane_size)
    held = ()
    kernels = [None] * PLANES
    for k in (0, 1, 3, 2):
        slot = (plane ^ k).astype(jnp.int32).reshape(1)
        kernels[k], *held = kernel_and_value(
            slot, chunks[k], scale, scaled_centers, center_norm, coefficients, chosen, extra, *held
        )
    values, picked = held
    values, panel_inverse = lax.optimization_barrier((values, panel_inverse))

    place = (order[:, None] == jnp.arange(shards, dtype=jnp.int32)[None, :]).astype(BF)

    inverse = panel_inverse.astype(BF)
    count = panel_rows // (strip * shards)
    turned_inverse = jnp.einsum(
        "rhqj,js->hrsq", inverse.reshape(own_rows, count, strip, shards), place
    ).reshape(count * own_rows, shards * strip)

    weight = class_lookup(point_class, class_weight)[:, None]
    shares = exchanged(values.reshape(shards, own_points, target_count), "ctr")
    residual = whole(
        residual_step,
        jax.ShapeDtypeStruct((shards, own_points, target_count), BF),
        shares,
        targets,
        weight,
    )
    residual = exchanged(residual, "ctr").reshape(shards * own_points, target_count)

    index = group.astype(jnp.int32).reshape(1)
    window = whole(
        window_step,
        jax.ShapeDtypeStruct((own_rows, target_count), BF),
        picked.reshape(shards * own_points, own_rows),
        residual,
    )
    parts = lax.all_gather(window, "pts")
    sent = jax.ShapeDtypeStruct((shards, strip, LANES), BF)
    window = whole(fold_step, sent, index, parts, scalars=1)
    window, turned_inverse = lax.optimization_barrier((window, turned_inverse))
    other_inverse = swapped(turned_inverse, "ctr", panel_shards)
    other_inverse, residual = lax.optimization_barrier((other_inverse, residual))
    solve_rows = jnp.concatenate(
        [
            jnp.where(panel == 0, turned_inverse, other_inverse),
            jnp.where(panel == 0, other_inverse, turned_inverse),
        ],
        axis=0,
    )
    window = exchanged(window, "ctr")
    window = window.reshape(shards * strip, LANES)

    planes = residual.reshape(PLANES, plane_points, target_count)
    backward = None
    for k in range(PLANES):
        part = lax.dot_general(
            pick(planes, plane ^ k), kernels[k], (((0,), (0,)), ((), ())), preferred_element_type=F32
        )
        backward = part if backward is None else backward + part
    backward = backward.reshape(groups, target_slice, shard_rows)
    near_pair = jnp.stack([pick(backward, group), pick(backward, group ^ 2)])
    far_pair = jnp.stack([pick(backward, group ^ 1), pick(backward, group ^ 3)]).astype(BF)
    near_pair = near_pair + swapped(far_pair, "pts", 1).astype(F32)
    gradient = near_pair[0] + swapped(near_pair[1].astype(BF), "pts", 2).astype(F32)
    gradient = gradient.T

    half = shards // HALVES
    sent = jax.ShapeDtypeStruct((half, strip, LANES), BF)
    packed = jax.ShapeDtypeStruct((strip, LANES), F32)
    first, low, high = whole(first_step, (sent, packed, packed), solve_rows, window)
    first = exchanged(first, "ctr", HALVES).reshape(half * strip, LANES)
    update = panel_call(middle_step, sent, factor, half, fold, first)
    update = exchanged(update, "ctr", HALVES).reshape(half * strip, LANES)
    solved = panel_call(
        last_step,
        jax.ShapeDtypeStruct((target_slice, own_rows), F32),
        panel_inverse,
        half,
        fold,
        update,
        low,
        high,
        scalars=(panel.astype(jnp.int32).reshape(1),),
    )
    return (gradient, solved.T)


def solution(mesh):
    placed = (
        P(("pts", "ctr"), None),
        P(("pts", "ctr")),
        P(("pts", "ctr"), None),
        P(),
        P(),
        P("ctr", None),
        P("ctr", None),
        P(),
        P("ctr", None),
        P("ctr", None),
    )
    return jax.shard_map(
        body,
        mesh=mesh,
        in_specs=placed,
        out_specs=(P("ctr", "pts"), P("ctr", "pts")),
        check_vma=False,
    )
```

```python
import functools

import jax
import jax.numpy as jnp
from jax import lax
from jax.experimental import pallas as pl
from jax.experimental.pallas import tpu as pltpu
from jax.sharding import PartitionSpec as P

BF = jnp.bfloat16
F32 = jnp.float32
LANES = 128
PLANES = 4
HALVES = 2
TILE = 512
EARLY = 2
VMEM = pl.BlockSpec(memory_space=pltpu.VMEM)


def exchanged(pieces, axis, parts=1):
    size = lax.axis_size(axis) // parts
    groups = [[part * size + i for i in range(size)] for part in range(parts)]
    return lax.all_to_all(
        pieces, axis, 0, 0, tiled=True, axis_index_groups=groups if parts > 1 else None
    )


def copies(x, count):
    return jnp.broadcast_to(x[None], (count, *x.shape))


def swapped(x, axis, bits):
    return lax.ppermute(x, axis, [(i, i ^ bits) for i in range(lax.axis_size(axis))])


def pick(x, index):
    return lax.dynamic_index_in_dim(x, index, 0, keepdims=False)


def scale_step(
    centers_ref, scale_ref, local_ref, scaled_ref, norm_ref, chosen_ref, extra_ref, slots, sems, outs
):
    loads = []
    for i in range(slots.shape[0]):
        rows = pl.ds(i * TILE, TILE)
        loads.append(pltpu.make_async_copy(centers_ref.at[rows, :], slots.at[i], sems.at[i]))
        loads[-1].start()
    count = chosen_ref.shape[0]
    chosen = jnp.zeros(chosen_ref.shape, F32)
    lane = lax.broadcasted_iota(jnp.int32, (count, TILE), 1)
    saves = []
    for i, load in enumerate(loads):
        rows = pl.ds(i * TILE, TILE)
        load.wait()
        scaled = (slots[i].astype(F32) * scale_ref[...]).astype(BF)
        slots[i] = scaled
        saves.append(pltpu.make_async_copy(slots.at[i], scaled_ref.at[rows, :], outs.at[i]))
        saves[-1].start()
        wide = scaled.astype(F32)
        norm = 0.5 * jnp.sum(wide * wide, axis=1, keepdims=True)
        norm_ref[:, rows] = jnp.broadcast_to(norm, (TILE, LANES)).T[0:1, :]
        pick_rows = (lane + i * TILE == local_ref[...]).astype(F32).astype(BF)
        chosen += jnp.dot(pick_rows, scaled, preferred_element_type=F32)
    chosen_ref[...] = chosen.astype(BF)
    norm = 0.5 * jnp.sum(chosen * chosen, axis=1, keepdims=True)
    extra_ref[...] = jnp.broadcast_to(norm, (count, LANES)).T[0:1, :]
    for save in saves:
        save.wait()


def scaled_and_norm(centers, scale, local):
    total, depth = centers.shape
    count = local.shape[0]
    steps = total // TILE
    return pl.pallas_call(
        scale_step,
        out_shape=(
            pltpu.HBM((total, depth), BF),
            jax.ShapeDtypeStruct((1, total), F32),
            jax.ShapeDtypeStruct((count, depth), BF),
            jax.ShapeDtypeStruct((1, count), F32),
        ),
        in_specs=[pl.BlockSpec(memory_space=pltpu.HBM), VMEM, VMEM],
        out_specs=[pl.BlockSpec(memory_space=pltpu.HBM)] + [VMEM] * 3,
        scratch_shapes=[pltpu.VMEM((steps, TILE, depth), BF)]
        + [pltpu.SemaphoreType.DMA((steps,))] * 2,
        compiler_params=pltpu.CompilerParams(vmem_limit_bytes=24 * 1024 * 1024),
        cost_estimate=pl.CostEstimate(
            flops=4 * total * depth, bytes_accessed=2 * total * depth, transcendentals=0
        ),
    )(pltpu.with_memory_space_constraint(centers, pltpu.HBM), scale, local)


def kernel_block(
    held, slot_ref, points_ref, scale_ref, centers_ref, norm_ref, coef_ref, chosen_ref, extra_ref, *refs
):
    kernel_ref, value_ref, picked_ref, slots, sems, *stream = refs[2 * held :]
    steps = centers_ref.shape[0] // TILE
    loads = []
    if stream:
        for i in range(steps):
            rows = pl.ds(i * TILE, TILE)
            loads.append(
                pltpu.make_async_copy(centers_ref.at[rows, :], stream[0].at[i], stream[1].at[i])
            )
            loads[-1].start()
    samples = (points_ref[...].astype(F32) * scale_ref[...]).astype(BF)
    wide = samples.astype(F32)
    left = 0.5 * jnp.sum(wide * wide, axis=1, keepdims=True)

    def block(anchors, norm):
        products = lax.dot_general(
            samples, anchors, (((1,), (1,)), ((), ())), preferred_element_type=F32
        )
        return jnp.exp(products - left - norm).astype(BF)

    if held:
        value_ref[...] = refs[0][...]
        picked_ref[...] = refs[1][...]
    total = jnp.zeros(value_ref.shape[1:], F32)
    saves = []
    before = None
    for i in range(steps):
        rows = pl.ds(i * TILE, TILE)
        if stream and i in (0, EARLY):
            for load in loads[i : EARLY if i == 0 else steps]:
                load.wait()
        anchors = stream[0][i] if stream else centers_ref[rows, :]
        current = block(anchors, norm_ref[:, rows])
        slots[i] = current
        saves.append(pltpu.make_async_copy(slots.at[i], kernel_ref.at[:, rows], sems.at[i]))
        saves[-1].start()
        if before is not None:
            coef = coef_ref[pl.ds((i - 1) * TILE, TILE), :]
            total += jnp.dot(before, coef, preferred_element_type=F32)
        before = current
    coef = coef_ref[pl.ds((steps - 1) * TILE, TILE), :]
    total += jnp.dot(before, coef, preferred_element_type=F32)
    value_ref[slot_ref[0]] = total.astype(value_ref.dtype)
    picked_ref[slot_ref[0]] = block(chosen_ref[...], extra_ref[...])
    for save in saves:
        save.wait()


def kernel_and_value(slot, samples, scale, anchors, norms, coefficients, chosen, extra, *held):
    count, depth = samples.shape
    total, cols = coefficients.shape
    steps = total // TILE
    space = VMEM if held else pl.BlockSpec(memory_space=pltpu.HBM)
    loaded = [pltpu.VMEM((steps, TILE, depth), BF), pltpu.SemaphoreType.DMA((steps,))]
    args = [samples, scale, anchors if held else pltpu.with_memory_space_constraint(anchors, pltpu.HBM)]
    args += [norms, coefficients, chosen, extra, *held]
    return pl.pallas_call(
        functools.partial(kernel_block, bool(held)),
        out_shape=(
            pltpu.HBM((count, total), BF),
            jax.ShapeDtypeStruct((PLANES, count, cols), BF),
            jax.ShapeDtypeStruct((PLANES, count, chosen.shape[0]), BF),
        ),
        in_specs=[pl.BlockSpec(memory_space=pltpu.SMEM), VMEM, VMEM, space]
        + [VMEM] * (len(args) - 3),
        out_specs=[pl.BlockSpec(memory_space=pltpu.HBM), VMEM, VMEM],
        scratch_shapes=[pltpu.VMEM((steps, count, TILE), BF), pltpu.SemaphoreType.DMA((steps,))]
        + ([] if held else loaded),
        compiler_params=pltpu.CompilerParams(vmem_limit_bytes=24 * 1024 * 1024),
        cost_estimate=pl.CostEstimate(
            flops=2 * count * total * (depth + cols),
            bytes_accessed=2 * count * total,
            transcendentals=count * total,
        ),
    )(slot, *args)


def lane_block(shape, width, index):
    lane = lax.broadcasted_iota(jnp.int32, shape, len(shape) - 1)
    return (lane >= index * width) & (lane < (index + 1) * width)


def turned(x, lanes):
    lanes = lanes % LANES
    return pltpu.roll(x, lanes, 1) if lanes else x


def folded_sum(product, fold, strip, blocks):
    width = LANES // fold
    out = None
    for f in range(fold):
        total = None
        for r in blocks:
            row = (r * fold + f) * strip
            part = turned(product[row : row + strip, :], (f - r) * width)
            total = part if total is None else total + part
        out = total if out is None else jnp.where(lane_block(total.shape, width, f), total, out)
    return out


def first_step(matrix_ref, window_ref, sent_ref, low_ref, high_ref):
    strip = sent_ref.shape[1]
    fold = int(round((matrix_ref.shape[0] // strip) ** 0.5))
    product = jnp.dot(matrix_ref[...], window_ref[...], preferred_element_type=F32)
    low = folded_sum(product, fold, strip, range(fold // HALVES))
    high = folded_sum(product, fold, strip, range(fold // HALVES, fold))
    low_ref[...] = low
    high_ref[...] = high
    sent_ref[...] = jnp.broadcast_to(low.astype(BF)[None], sent_ref.shape)


def natural_product(matrix_ref, data_ref, rows_ref):
    parts, fold, strip, _ = rows_ref.shape
    data = data_ref[...].astype(F32).reshape(parts * strip, LANES)
    for f in range(fold):
        piece = turned(data, -f * (LANES // fold)).astype(BF)
        rows_ref[:, f] = piece.reshape(parts, strip, LANES)
    right = rows_ref[...].reshape(parts * fold * strip, LANES)
    return jnp.dot(matrix_ref[...].astype(BF), right, preferred_element_type=F32)


def middle_step(matrix_ref, data_ref, sent_ref, rows_ref):
    product = natural_product(matrix_ref, data_ref, rows_ref)
    _, fold, strip, _ = rows_ref.shape
    width = LANES // fold
    out = None
    for f in range(fold):
        part = turned(product[f * strip : (f + 1) * strip, :], f * width)
        out = part if out is None else jnp.where(lane_block(part.shape, width, f), part, out)
    sent_ref[...] = jnp.broadcast_to(out.astype(BF)[None], sent_ref.shape)


def last_step(panel_ref, matrix_ref, data_ref, low_ref, high_ref, out_ref, rows_ref):
    product = natural_product(matrix_ref, data_ref, rows_ref)
    _, fold, strip, _ = rows_ref.shape
    width = LANES // fold
    low = jnp.concatenate([turned(low_ref[...], -f * width) for f in range(fold)], axis=0)
    high = jnp.concatenate([turned(high_ref[...], -f * width) for f in range(fold)], axis=0)
    solved = jnp.where(panel_ref[0] == 0, low, high - product)
    out_ref[...] = solved.T[:width, :]


def panel_call(body, shape, matrix, parts, fold, data, *more, scalars=()):
    rows, depth = matrix.shape[0], parts * data.shape[0] // parts * fold
    strip = data.shape[0] // parts
    return pl.pallas_call(
        body,
        grid=(1,),
        out_shape=shape,
        in_specs=[pl.BlockSpec(memory_space=pltpu.SMEM)] * len(scalars)
        + [pl.BlockSpec((rows, depth), lambda i: (0, 0))]
        + [VMEM] * (1 + len(more)),
        out_specs=VMEM,
        scratch_shapes=[pltpu.VMEM((parts, fold, strip, LANES), BF)],
        compiler_params=pltpu.CompilerParams(vmem_limit_bytes=16 * 1024 * 1024),
    )(*scalars, matrix, data, *more)


def residual_step(shares_ref, targets_ref, weight_ref, sent_ref):
    predicted = jnp.sum(shares_ref[...].astype(F32), axis=0)
    residual = (weight_ref[...] * (predicted - targets_ref[...])).astype(BF)
    sent_ref[...] = jnp.broadcast_to(residual[None], sent_ref.shape)


def window_step(chosen_ref, residual_ref, window_ref):
    window = lax.dot_general(
        chosen_ref[...], residual_ref[...], (((0,), (0,)), ((), ())), preferred_element_type=F32
    )
    window_ref[...] = window.astype(window_ref.dtype)


def fold_step(group_ref, parts_ref, sent_ref):
    groups = parts_ref.shape[0]
    strip = sent_ref.shape[1]
    width = LANES // groups
    window = jnp.sum(parts_ref[...].astype(F32), axis=0)
    result = None
    for p in range(groups):
        out = None
        for r in range(window.shape[0] // strip):
            part = turned(window[r * strip : (r + 1) * strip, :], (r - p) * width)
            out = part if out is None else jnp.where(lane_block(part.shape, width, r), part, out)
        result = out if result is None else jnp.where(group_ref[0] == p, out, result)
    sent_ref[...] = jnp.broadcast_to(result.astype(BF)[None], sent_ref.shape)


def whole(body, shapes, *args, scalars=0):
    return pl.pallas_call(
        body,
        out_shape=shapes,
        in_specs=[pl.BlockSpec(memory_space=pltpu.SMEM)] * scalars + [VMEM] * (len(args) - scalars),
        out_specs=jax.tree.map(lambda _: VMEM, shapes),
        compiler_params=pltpu.CompilerParams(vmem_limit_bytes=16 * 1024 * 1024),
    )(*args)


def half_norm(rows):
    return 0.5 * jnp.sum(jnp.square(rows.astype(F32)), axis=-1)


def class_lookup(labels, table):
    classes = jnp.arange(table.shape[0], dtype=jnp.int32)
    return jnp.sum(jnp.where(labels[:, None] == classes[None, :], table[None, :], 0.0), axis=1)


def body(
    points,
    point_class,
    targets,
    class_weight,
    inv_scale,
    centers,
    coefficients,
    center_index,
    factor,
    panel_inverse,
):
    groups = lax.axis_size("pts")
    shards = lax.axis_size("ctr")
    shard = lax.axis_index("ctr")
    group = lax.axis_index("pts")
    own_points, depth = points.shape
    shard_rows = centers.shape[0]
    target_count = targets.shape[1]
    target_slice = target_count // groups
    own_rows = center_index.shape[0] // shards
    panel_rows = panel_inverse.shape[1]
    panel_shards = panel_rows // own_rows
    panel = shard // panel_shards
    fold = LANES // target_slice
    strip = own_rows // fold
    plane_size = shards // PLANES
    plane = shard // plane_size
    plane_points = plane_size * own_points

    plane_rows = exchanged(copies(points, plane_size), "ctr", PLANES)
    plane_rows = plane_rows.reshape(plane_points, depth)
    blocks = center_index.reshape(own_rows, shards)
    order = blocks[0] // shard_rows
    here = order == shard
    local = jnp.sum(jnp.where(here[None, :], blocks - shard * shard_rows, 0), axis=1)
    scale = inv_scale[None, :]
    scaled_centers, center_norm, chosen, extra = scaled_and_norm(centers, scale, local[:, None])
    plane_rows, extra = lax.optimization_barrier((plane_rows, extra))
    chunks = [plane_rows] + [None] * (PLANES - 1)
    for k in (2, 1, 3):
        chunks[k] = swapped(plane_rows, "ctr", k * plane_size)
    held = ()
    kernels = [None] * PLANES
    for k in (0, 1, 3, 2):
        slot = (plane ^ k).astype(jnp.int32).reshape(1)
        kernels[k], *held = kernel_and_value(
            slot, chunks[k], scale, scaled_centers, center_norm, coefficients, chosen, extra, *held
        )
    values, picked = held
    values, panel_inverse = lax.optimization_barrier((values, panel_inverse))

    place = (order[:, None] == jnp.arange(shards, dtype=jnp.int32)[None, :]).astype(BF)

    inverse = panel_inverse.astype(BF)
    count = panel_rows // (strip * shards)
    turned_inverse = jnp.einsum(
        "rhqj,js->hrsq", inverse.reshape(own_rows, count, strip, shards), place
    ).reshape(count * own_rows, shards * strip)

    weight = class_lookup(point_class, class_weight)[:, None]
    shares = exchanged(values.reshape(shards, own_points, target_count), "ctr")
    residual = whole(
        residual_step,
        jax.ShapeDtypeStruct((shards, own_points, target_count), BF),
        shares,
        targets,
        weight,
    )
    residual, turned_inverse = lax.optimization_barrier((residual, turned_inverse))
    other_inverse = swapped(turned_inverse, "ctr", panel_shards)
    residual = exchanged(residual, "ctr").reshape(shards * own_points, target_count)
    residual, other_inverse = lax.optimization_barrier((residual, other_inverse))

    index = group.astype(jnp.int32).reshape(1)
    window = whole(
        window_step,
        jax.ShapeDtypeStruct((own_rows, target_count), BF),
        picked.reshape(shards * own_points, own_rows),
        residual,
    )
    parts = lax.all_gather(window, "pts")
    sent = jax.ShapeDtypeStruct((shards, strip, LANES), BF)
    window = whole(fold_step, sent, index, parts, scalars=1)
    window, other_inverse = lax.optimization_barrier((window, other_inverse))
    other_inverse = swapped(other_inverse, "pts", 1)
    other_inverse, residual = lax.optimization_barrier((other_inverse, residual))
    solve_rows = jnp.concatenate(
        [
            jnp.where(panel == 0, turned_inverse, other_inverse),
            jnp.where(panel == 0, other_inverse, turned_inverse),
        ],
        axis=0,
    )
    window = exchanged(window, "ctr")
    window = window.reshape(shards * strip, LANES)

    planes = residual.reshape(PLANES, plane_points, target_count)
    backward = None
    for k in range(PLANES):
        part = lax.dot_general(
            pick(planes, plane ^ k), kernels[k], (((0,), (0,)), ((), ())), preferred_element_type=F32
        )
        backward = part if backward is None else backward + part
    backward = backward.reshape(groups, target_slice, shard_rows)
    near_pair = jnp.stack([pick(backward, group), pick(backward, group ^ 2)])
    far_pair = jnp.stack([pick(backward, group ^ 1), pick(backward, group ^ 3)]).astype(BF)
    near_pair = near_pair + swapped(far_pair, "pts", 1).astype(F32)
    gradient = near_pair[0] + swapped(near_pair[1].astype(BF), "pts", 2).astype(F32)
    gradient = gradient.T

    half = shards // HALVES
    sent = jax.ShapeDtypeStruct((half, strip, LANES), BF)
    packed = jax.ShapeDtypeStruct((strip, LANES), F32)
    first, low, high = whole(first_step, (sent, packed, packed), solve_rows, window)
    first = exchanged(first, "ctr", HALVES).reshape(half * strip, LANES)
    update = panel_call(middle_step, sent, factor, half, fold, first)
    update = exchanged(update, "ctr", HALVES).reshape(half * strip, LANES)
    solved = panel_call(
        last_step,
        jax.ShapeDtypeStruct((target_slice, own_rows), F32),
        panel_inverse,
        half,
        fold,
        update,
        low,
        high,
        scalars=(panel.astype(jnp.int32).reshape(1),),
    )
    return (gradient, solved.T)


def solution(mesh):
    placed = (
        P(("pts", "ctr"), None),
        P(("pts", "ctr")),
        P(("pts", "ctr"), None),
        P(),
        P(),
        P("ctr", None),
        P("ctr", None),
        P(),
        P("ctr", None),
        P("ctr", None),
    )
    return jax.shard_map(
        body,
        mesh=mesh,
        in_specs=placed,
        out_specs=(P("ctr", "pts"), P("ctr", "pts")),
        check_vma=False,
    )
```

```python
import functools

import jax
import jax.numpy as jnp
from jax import lax
from jax.experimental import pallas as pl
from jax.experimental.pallas import tpu as pltpu
from jax.sharding import PartitionSpec as P

BF = jnp.bfloat16
F32 = jnp.float32
LANES = 128
PLANES = 4
HALVES = 2
TILE = 512
EARLY = 2
VMEM = pl.BlockSpec(memory_space=pltpu.VMEM)


def exchanged(pieces, axis, parts=1):
    size = lax.axis_size(axis) // parts
    groups = [[part * size + i for i in range(size)] for part in range(parts)]
    return lax.all_to_all(
        pieces, axis, 0, 0, tiled=True, axis_index_groups=groups if parts > 1 else None
    )


def copies(x, count):
    return jnp.broadcast_to(x[None], (count, *x.shape))


def swapped(x, axis, bits):
    return lax.ppermute(x, axis, [(i, i ^ bits) for i in range(lax.axis_size(axis))])


def pick(x, index):
    return lax.dynamic_index_in_dim(x, index, 0, keepdims=False)


def scale_step(
    centers_ref, scale_ref, local_ref, scaled_ref, norm_ref, chosen_ref, extra_ref, slots, sems, outs
):
    loads = []
    for i in range(slots.shape[0]):
        rows = pl.ds(i * TILE, TILE)
        loads.append(pltpu.make_async_copy(centers_ref.at[rows, :], slots.at[i], sems.at[i]))
        loads[-1].start()
    count = chosen_ref.shape[0]
    chosen = jnp.zeros(chosen_ref.shape, F32)
    lane = lax.broadcasted_iota(jnp.int32, (count, TILE), 1)
    saves = []
    for i, load in enumerate(loads):
        rows = pl.ds(i * TILE, TILE)
        load.wait()
        scaled = (slots[i].astype(F32) * scale_ref[...]).astype(BF)
        slots[i] = scaled
        saves.append(pltpu.make_async_copy(slots.at[i], scaled_ref.at[rows, :], outs.at[i]))
        saves[-1].start()
        wide = scaled.astype(F32)
        norm = 0.5 * jnp.sum(wide * wide, axis=1, keepdims=True)
        norm_ref[:, rows] = jnp.broadcast_to(norm, (TILE, LANES)).T[0:1, :]
        pick_rows = (lane + i * TILE == local_ref[...]).astype(F32).astype(BF)
        chosen += jnp.dot(pick_rows, scaled, preferred_element_type=F32)
    chosen_ref[...] = chosen.astype(BF)
    norm = 0.5 * jnp.sum(chosen * chosen, axis=1, keepdims=True)
    extra_ref[...] = jnp.broadcast_to(norm, (count, LANES)).T[0:1, :]
    for save in saves:
        save.wait()


def scaled_and_norm(centers, scale, local):
    total, depth = centers.shape
    count = local.shape[0]
    steps = total // TILE
    return pl.pallas_call(
        scale_step,
        out_shape=(
            pltpu.HBM((total, depth), BF),
            jax.ShapeDtypeStruct((1, total), F32),
            jax.ShapeDtypeStruct((count, depth), BF),
            jax.ShapeDtypeStruct((1, count), F32),
        ),
        in_specs=[pl.BlockSpec(memory_space=pltpu.HBM), VMEM, VMEM],
        out_specs=[pl.BlockSpec(memory_space=pltpu.HBM)] + [VMEM] * 3,
        scratch_shapes=[pltpu.VMEM((steps, TILE, depth), BF)]
        + [pltpu.SemaphoreType.DMA((steps,))] * 2,
        compiler_params=pltpu.CompilerParams(vmem_limit_bytes=24 * 1024 * 1024),
        cost_estimate=pl.CostEstimate(
            flops=4 * total * depth, bytes_accessed=2 * total * depth, transcendentals=0
        ),
    )(pltpu.with_memory_space_constraint(centers, pltpu.HBM), scale, local)


def kernel_block(
    held, slot_ref, points_ref, scale_ref, centers_ref, norm_ref, coef_ref, chosen_ref, extra_ref, *refs
):
    kernel_ref, value_ref, picked_ref, slots, sems, *stream = refs[2 * held :]
    steps = centers_ref.shape[0] // TILE
    loads = []
    if stream:
        for i in range(steps):
            rows = pl.ds(i * TILE, TILE)
            loads.append(
                pltpu.make_async_copy(centers_ref.at[rows, :], stream[0].at[i], stream[1].at[i])
            )
            loads[-1].start()
    samples = (points_ref[...].astype(F32) * scale_ref[...]).astype(BF)
    wide = samples.astype(F32)
    left = 0.5 * jnp.sum(wide * wide, axis=1, keepdims=True)

    def block(anchors, norm):
        products = lax.dot_general(
            samples, anchors, (((1,), (1,)), ((), ())), preferred_element_type=F32
        )
        return jnp.exp(products - left - norm).astype(BF)

    if held:
        value_ref[...] = refs[0][...]
        picked_ref[...] = refs[1][...]
    total = jnp.zeros(value_ref.shape[1:], F32)
    saves = []
    before = None
    for i in range(steps):
        rows = pl.ds(i * TILE, TILE)
        if stream and i in (0, EARLY):
            for load in loads[i : EARLY if i == 0 else steps]:
                load.wait()
        anchors = stream[0][i] if stream else centers_ref[rows, :]
        current = block(anchors, norm_ref[:, rows])
        slots[i] = current
        saves.append(pltpu.make_async_copy(slots.at[i], kernel_ref.at[:, rows], sems.at[i]))
        saves[-1].start()
        if before is not None:
            coef = coef_ref[pl.ds((i - 1) * TILE, TILE), :]
            total += jnp.dot(before, coef, preferred_element_type=F32)
        before = current
    coef = coef_ref[pl.ds((steps - 1) * TILE, TILE), :]
    total += jnp.dot(before, coef, preferred_element_type=F32)
    value_ref[slot_ref[0]] = total.astype(value_ref.dtype)
    picked_ref[slot_ref[0]] = block(chosen_ref[...], extra_ref[...])
    for save in saves:
        save.wait()


def kernel_and_value(slot, samples, scale, anchors, norms, coefficients, chosen, extra, *held):
    count, depth = samples.shape
    total, cols = coefficients.shape
    steps = total // TILE
    space = VMEM if held else pl.BlockSpec(memory_space=pltpu.HBM)
    loaded = [pltpu.VMEM((steps, TILE, depth), BF), pltpu.SemaphoreType.DMA((steps,))]
    args = [samples, scale, anchors if held else pltpu.with_memory_space_constraint(anchors, pltpu.HBM)]
    args += [norms, coefficients, chosen, extra, *held]
    return pl.pallas_call(
        functools.partial(kernel_block, bool(held)),
        out_shape=(
            pltpu.HBM((count, total), BF),
            jax.ShapeDtypeStruct((PLANES, count, cols), BF),
            jax.ShapeDtypeStruct((PLANES, count, chosen.shape[0]), BF),
        ),
        in_specs=[pl.BlockSpec(memory_space=pltpu.SMEM), VMEM, VMEM, space]
        + [VMEM] * (len(args) - 3),
        out_specs=[pl.BlockSpec(memory_space=pltpu.HBM), VMEM, VMEM],
        scratch_shapes=[pltpu.VMEM((steps, count, TILE), BF), pltpu.SemaphoreType.DMA((steps,))]
        + ([] if held else loaded),
        compiler_params=pltpu.CompilerParams(vmem_limit_bytes=24 * 1024 * 1024),
        cost_estimate=pl.CostEstimate(
            flops=2 * count * total * (depth + cols),
            bytes_accessed=2 * count * total,
            transcendentals=count * total,
        ),
    )(slot, *args)


def lane_block(shape, width, index):
    lane = lax.broadcasted_iota(jnp.int32, shape, len(shape) - 1)
    return (lane >= index * width) & (lane < (index + 1) * width)


def turned(x, lanes):
    lanes = lanes % LANES
    return pltpu.roll(x, lanes, 1) if lanes else x


def folded_sum(product, fold, strip, blocks):
    width = LANES // fold
    out = None
    for f in range(fold):
        total = None
        for r in blocks:
            row = (r * fold + f) * strip
            part = turned(product[row : row + strip, :], (f - r) * width)
            total = part if total is None else total + part
        out = total if out is None else jnp.where(lane_block(total.shape, width, f), total, out)
    return out


def first_step(matrix_ref, window_ref, sent_ref, low_ref, high_ref):
    strip = sent_ref.shape[1]
    fold = int(round((matrix_ref.shape[0] // strip) ** 0.5))
    product = jnp.dot(matrix_ref[...], window_ref[...], preferred_element_type=F32)
    low = folded_sum(product, fold, strip, range(fold // HALVES))
    high = folded_sum(product, fold, strip, range(fold // HALVES, fold))
    low_ref[...] = low
    high_ref[...] = high
    sent_ref[...] = jnp.broadcast_to(low.astype(BF)[None], sent_ref.shape)


def natural_product(matrix_ref, data_ref, rows_ref):
    parts, fold, strip, _ = rows_ref.shape
    data = data_ref[...].astype(F32).reshape(parts * strip, LANES)
    for f in range(fold):
        piece = turned(data, -f * (LANES // fold)).astype(BF)
        rows_ref[:, f] = piece.reshape(parts, strip, LANES)
    right = rows_ref[...].reshape(parts * fold * strip, LANES)
    return jnp.dot(matrix_ref[...].astype(BF), right, preferred_element_type=F32)


def middle_step(matrix_ref, data_ref, sent_ref, rows_ref):
    product = natural_product(matrix_ref, data_ref, rows_ref)
    _, fold, strip, _ = rows_ref.shape
    width = LANES // fold
    out = None
    for f in range(fold):
        part = turned(product[f * strip : (f + 1) * strip, :], f * width)
        out = part if out is None else jnp.where(lane_block(part.shape, width, f), part, out)
    sent_ref[...] = jnp.broadcast_to(out.astype(BF)[None], sent_ref.shape)


def last_step(panel_ref, matrix_ref, data_ref, low_ref, high_ref, out_ref, rows_ref):
    product = natural_product(matrix_ref, data_ref, rows_ref)
    _, fold, strip, _ = rows_ref.shape
    width = LANES // fold
    low = jnp.concatenate([turned(low_ref[...], -f * width) for f in range(fold)], axis=0)
    high = jnp.concatenate([turned(high_ref[...], -f * width) for f in range(fold)], axis=0)
    solved = jnp.where(panel_ref[0] == 0, low, high - product)
    out_ref[...] = solved.T[:width, :]


def panel_call(body, shape, matrix, parts, fold, data, *more, scalars=()):
    rows, depth = matrix.shape[0], parts * data.shape[0] // parts * fold
    strip = data.shape[0] // parts
    return pl.pallas_call(
        body,
        grid=(1,),
        out_shape=shape,
        in_specs=[pl.BlockSpec(memory_space=pltpu.SMEM)] * len(scalars)
        + [pl.BlockSpec((rows, depth), lambda i: (0, 0))]
        + [VMEM] * (1 + len(more)),
        out_specs=VMEM,
        scratch_shapes=[pltpu.VMEM((parts, fold, strip, LANES), BF)],
        compiler_params=pltpu.CompilerParams(vmem_limit_bytes=16 * 1024 * 1024),
    )(*scalars, matrix, data, *more)


def residual_step(shares_ref, targets_ref, weight_ref, sent_ref):
    predicted = jnp.sum(shares_ref[...].astype(F32), axis=0)
    residual = (weight_ref[...] * (predicted - targets_ref[...])).astype(BF)
    sent_ref[...] = jnp.broadcast_to(residual[None], sent_ref.shape)


def window_step(chosen_ref, residual_ref, window_ref):
    window = lax.dot_general(
        chosen_ref[...], residual_ref[...], (((0,), (0,)), ((), ())), preferred_element_type=F32
    )
    window_ref[...] = window.astype(window_ref.dtype)


def fold_step(group_ref, parts_ref, sent_ref):
    groups = parts_ref.shape[0]
    strip = sent_ref.shape[1]
    width = LANES // groups
    window = jnp.sum(parts_ref[...].astype(F32), axis=0)
    result = None
    for p in range(groups):
        out = None
        for r in range(window.shape[0] // strip):
            part = turned(window[r * strip : (r + 1) * strip, :], (r - p) * width)
            out = part if out is None else jnp.where(lane_block(part.shape, width, r), part, out)
        result = out if result is None else jnp.where(group_ref[0] == p, out, result)
    sent_ref[...] = jnp.broadcast_to(result.astype(BF)[None], sent_ref.shape)


def whole(body, shapes, *args, scalars=0):
    return pl.pallas_call(
        body,
        out_shape=shapes,
        in_specs=[pl.BlockSpec(memory_space=pltpu.SMEM)] * scalars + [VMEM] * (len(args) - scalars),
        out_specs=jax.tree.map(lambda _: VMEM, shapes),
        compiler_params=pltpu.CompilerParams(vmem_limit_bytes=16 * 1024 * 1024),
    )(*args)


def half_norm(rows):
    return 0.5 * jnp.sum(jnp.square(rows.astype(F32)), axis=-1)


def class_lookup(labels, table):
    classes = jnp.arange(table.shape[0], dtype=jnp.int32)
    return jnp.sum(jnp.where(labels[:, None] == classes[None, :], table[None, :], 0.0), axis=1)


def body(
    points,
    point_class,
    targets,
    class_weight,
    inv_scale,
    centers,
    coefficients,
    center_index,
    factor,
    panel_inverse,
):
    groups = lax.axis_size("pts")
    shards = lax.axis_size("ctr")
    shard = lax.axis_index("ctr")
    group = lax.axis_index("pts")
    own_points, depth = points.shape
    shard_rows = centers.shape[0]
    target_count = targets.shape[1]
    target_slice = target_count // groups
    own_rows = center_index.shape[0] // shards
    panel_rows = panel_inverse.shape[1]
    panel_shards = panel_rows // own_rows
    panel = shard // panel_shards
    fold = LANES // target_slice
    strip = own_rows // fold
    plane_size = shards // PLANES
    plane = shard // plane_size
    plane_points = plane_size * own_points

    plane_rows = exchanged(copies(points, plane_size), "ctr", PLANES)
    plane_rows = plane_rows.reshape(plane_points, depth)
    blocks = center_index.reshape(own_rows, shards)
    order = blocks[0] // shard_rows
    here = order == shard
    local = jnp.sum(jnp.where(here[None, :], blocks - shard * shard_rows, 0), axis=1)
    scale = inv_scale[None, :]
    scaled_centers, center_norm, chosen, extra = scaled_and_norm(centers, scale, local[:, None])
    plane_rows, extra = lax.optimization_barrier((plane_rows, extra))
    chunks = [plane_rows] + [None] * (PLANES - 1)
    for k in (2, 1, 3):
        chunks[k] = swapped(plane_rows, "ctr", k * plane_size)
    held = ()
    kernels = [None] * PLANES
    for k in (0, 1, 2, 3):
        slot = (plane ^ k).astype(jnp.int32).reshape(1)
        kernels[k], *held = kernel_and_value(
            slot, chunks[k], scale, scaled_centers, center_norm, coefficients, chosen, extra, *held
        )
    values, picked = held
    values, panel_inverse = lax.optimization_barrier((values, panel_inverse))

    place = (order[:, None] == jnp.arange(shards, dtype=jnp.int32)[None, :]).astype(BF)

    inverse = panel_inverse.astype(BF)
    count = panel_rows // (strip * shards)
    turned_inverse = jnp.einsum(
        "rhqj,js->hrsq", inverse.reshape(own_rows, count, strip, shards), place
    ).reshape(count * own_rows, shards * strip)

    weight = class_lookup(point_class, class_weight)[:, None]
    shares = exchanged(values.reshape(shards, own_points, target_count), "ctr")
    residual = whole(
        residual_step,
        jax.ShapeDtypeStruct((shards, own_points, target_count), BF),
        shares,
        targets,
        weight,
    )
    residual = exchanged(residual, "ctr").reshape(shards * own_points, target_count)

    index = group.astype(jnp.int32).reshape(1)
    window = whole(
        window_step,
        jax.ShapeDtypeStruct((own_rows, target_count), BF),
        picked.reshape(shards * own_points, own_rows),
        residual,
    )
    parts = lax.all_gather(window, "pts")
    sent = jax.ShapeDtypeStruct((shards, strip, LANES), BF)
    window = whole(fold_step, sent, index, parts, scalars=1)
    window, turned_inverse = lax.optimization_barrier((window, turned_inverse))
    other_inverse = swapped(turned_inverse, "ctr", panel_shards)
    other_inverse, residual = lax.optimization_barrier((other_inverse, residual))
    solve_rows = jnp.concatenate(
        [
            jnp.where(panel == 0, turned_inverse, other_inverse),
            jnp.where(panel == 0, other_inverse, turned_inverse),
        ],
        axis=0,
    )
    window = exchanged(window, "ctr")
    window = window.reshape(shards * strip, LANES)

    planes = residual.reshape(PLANES, plane_points, target_count)
    backward = None
    for k in range(PLANES):
        part = lax.dot_general(
            pick(planes, plane ^ k), kernels[k], (((0,), (0,)), ((), ())), preferred_element_type=F32
        )
        backward = part if backward is None else backward + part
    backward = backward.reshape(groups, target_slice, shard_rows)
    near_pair = jnp.stack([pick(backward, group), pick(backward, group ^ 2)])
    far_pair = jnp.stack([pick(backward, group ^ 1), pick(backward, group ^ 3)]).astype(BF)
    near_pair = near_pair + swapped(far_pair, "pts", 1).astype(F32)
    gradient = near_pair[0] + swapped(near_pair[1].astype(BF), "pts", 2).astype(F32)
    gradient = gradient.T

    half = shards // HALVES
    sent = jax.ShapeDtypeStruct((half, strip, LANES), BF)
    packed = jax.ShapeDtypeStruct((strip, LANES), F32)
    first, low, high = whole(first_step, (sent, packed, packed), solve_rows, window)
    first = exchanged(first, "ctr", HALVES).reshape(half * strip, LANES)
    update = panel_call(middle_step, sent, factor, half, fold, first)
    update = exchanged(update, "ctr", HALVES).reshape(half * strip, LANES)
    solved = panel_call(
        last_step,
        jax.ShapeDtypeStruct((target_slice, own_rows), F32),
        panel_inverse,
        half,
        fold,
        update,
        low,
        high,
        scalars=(panel.astype(jnp.int32).reshape(1),),
    )
    return (gradient, solved.T)


def solution(mesh):
    placed = (
        P(("pts", "ctr"), None),
        P(("pts", "ctr")),
        P(("pts", "ctr"), None),
        P(),
        P(),
        P("ctr", None),
        P("ctr", None),
        P(),
        P("ctr", None),
        P("ctr", None),
    )
    return jax.shard_map(
        body,
        mesh=mesh,
        in_specs=placed,
        out_specs=(P("ctr", "pts"), P("ctr", "pts")),
        check_vma=False,
    )
```

```python
import functools

import jax
import jax.numpy as jnp
from jax import lax
from jax.experimental import pallas as pl
from jax.experimental.pallas import tpu as pltpu
from jax.sharding import PartitionSpec as P

BF = jnp.bfloat16
F32 = jnp.float32
LANES = 128
PLANES = 4
HALVES = 2
TILE = 512
EARLY = 2
VMEM = pl.BlockSpec(memory_space=pltpu.VMEM)


def exchanged(pieces, axis, parts=1):
    size = lax.axis_size(axis) // parts
    groups = [[part * size + i for i in range(size)] for part in range(parts)]
    return lax.all_to_all(
        pieces, axis, 0, 0, tiled=True, axis_index_groups=groups if parts > 1 else None
    )


def copies(x, count):
    return jnp.broadcast_to(x[None], (count, *x.shape))


def swapped(x, axis, bits):
    return lax.ppermute(x, axis, [(i, i ^ bits) for i in range(lax.axis_size(axis))])


def pick(x, index):
    return lax.dynamic_index_in_dim(x, index, 0, keepdims=False)


def scale_step(
    centers_ref, scale_ref, local_ref, scaled_ref, norm_ref, chosen_ref, extra_ref, slots, sems, outs
):
    loads = []
    for i in range(slots.shape[0]):
        rows = pl.ds(i * TILE, TILE)
        loads.append(pltpu.make_async_copy(centers_ref.at[rows, :], slots.at[i], sems.at[i]))
        loads[-1].start()
    count = chosen_ref.shape[0]
    chosen = jnp.zeros(chosen_ref.shape, F32)
    lane = lax.broadcasted_iota(jnp.int32, (count, TILE), 1)
    saves = []
    for i, load in enumerate(loads):
        rows = pl.ds(i * TILE, TILE)
        load.wait()
        scaled = (slots[i].astype(F32) * scale_ref[...]).astype(BF)
        slots[i] = scaled
        saves.append(pltpu.make_async_copy(slots.at[i], scaled_ref.at[rows, :], outs.at[i]))
        saves[-1].start()
        wide = scaled.astype(F32)
        norm = 0.5 * jnp.sum(wide * wide, axis=1, keepdims=True)
        norm_ref[:, rows] = jnp.broadcast_to(norm, (TILE, LANES)).T[0:1, :]
        pick_rows = (lane + i * TILE == local_ref[...]).astype(F32).astype(BF)
        chosen += jnp.dot(pick_rows, scaled, preferred_element_type=F32)
    chosen_ref[...] = chosen.astype(BF)
    norm = 0.5 * jnp.sum(chosen * chosen, axis=1, keepdims=True)
    extra_ref[...] = jnp.broadcast_to(norm, (count, LANES)).T[0:1, :]
    for save in saves:
        save.wait()


def scaled_and_norm(centers, scale, local):
    total, depth = centers.shape
    count = local.shape[0]
    steps = total // TILE
    return pl.pallas_call(
        scale_step,
        out_shape=(
            pltpu.HBM((total, depth), BF),
            jax.ShapeDtypeStruct((1, total), F32),
            jax.ShapeDtypeStruct((count, depth), BF),
            jax.ShapeDtypeStruct((1, count), F32),
        ),
        in_specs=[pl.BlockSpec(memory_space=pltpu.HBM), VMEM, VMEM],
        out_specs=[pl.BlockSpec(memory_space=pltpu.HBM)] + [VMEM] * 3,
        scratch_shapes=[pltpu.VMEM((steps, TILE, depth), BF)]
        + [pltpu.SemaphoreType.DMA((steps,))] * 2,
        compiler_params=pltpu.CompilerParams(vmem_limit_bytes=24 * 1024 * 1024),
        cost_estimate=pl.CostEstimate(
            flops=4 * total * depth, bytes_accessed=2 * total * depth, transcendentals=0
        ),
    )(pltpu.with_memory_space_constraint(centers, pltpu.HBM), scale, local)


def kernel_block(
    held, slot_ref, points_ref, scale_ref, centers_ref, norm_ref, coef_ref, chosen_ref, extra_ref, *refs
):
    kernel_ref, value_ref, picked_ref, slots, sems, *stream = refs[2 * held :]
    steps = centers_ref.shape[0] // TILE
    loads = []
    if stream:
        for i in range(steps):
            rows = pl.ds(i * TILE, TILE)
            loads.append(
                pltpu.make_async_copy(centers_ref.at[rows, :], stream[0].at[i], stream[1].at[i])
            )
            loads[-1].start()
    samples = (points_ref[...].astype(F32) * scale_ref[...]).astype(BF)
    wide = samples.astype(F32)
    left = 0.5 * jnp.sum(wide * wide, axis=1, keepdims=True)

    def block(anchors, norm):
        products = lax.dot_general(
            samples, anchors, (((1,), (1,)), ((), ())), preferred_element_type=F32
        )
        return jnp.exp(products - left - norm).astype(BF)

    if held:
        value_ref[...] = refs[0][...]
        picked_ref[...] = refs[1][...]
    total = jnp.zeros(value_ref.shape[1:], F32)
    saves = []
    before = None
    for i in range(steps):
        rows = pl.ds(i * TILE, TILE)
        if stream and i in (0, EARLY):
            for load in loads[i : EARLY if i == 0 else steps]:
                load.wait()
        anchors = stream[0][i] if stream else centers_ref[rows, :]
        current = block(anchors, norm_ref[:, rows])
        slots[i] = current
        saves.append(pltpu.make_async_copy(slots.at[i], kernel_ref.at[:, rows], sems.at[i]))
        saves[-1].start()
        if before is not None:
            coef = coef_ref[pl.ds((i - 1) * TILE, TILE), :]
            total += jnp.dot(before, coef, preferred_element_type=F32)
        before = current
    coef = coef_ref[pl.ds((steps - 1) * TILE, TILE), :]
    total += jnp.dot(before, coef, preferred_element_type=F32)
    value_ref[slot_ref[0]] = total.astype(value_ref.dtype)
    picked_ref[slot_ref[0]] = block(chosen_ref[...], extra_ref[...])
    for save in saves:
        save.wait()


def kernel_and_value(slot, samples, scale, anchors, norms, coefficients, chosen, extra, *held):
    count, depth = samples.shape
    total, cols = coefficients.shape
    steps = total // TILE
    space = VMEM if held else pl.BlockSpec(memory_space=pltpu.HBM)
    loaded = [pltpu.VMEM((steps, TILE, depth), BF), pltpu.SemaphoreType.DMA((steps,))]
    args = [samples, scale, anchors if held else pltpu.with_memory_space_constraint(anchors, pltpu.HBM)]
    args += [norms, coefficients, chosen, extra, *held]
    return pl.pallas_call(
        functools.partial(kernel_block, bool(held)),
        out_shape=(
            pltpu.HBM((count, total), BF),
            jax.ShapeDtypeStruct((PLANES, count, cols), BF),
            jax.ShapeDtypeStruct((PLANES, count, chosen.shape[0]), BF),
        ),
        in_specs=[pl.BlockSpec(memory_space=pltpu.SMEM), VMEM, VMEM, space]
        + [VMEM] * (len(args) - 3),
        out_specs=[pl.BlockSpec(memory_space=pltpu.HBM), VMEM, VMEM],
        scratch_shapes=[pltpu.VMEM((steps, count, TILE), BF), pltpu.SemaphoreType.DMA((steps,))]
        + ([] if held else loaded),
        compiler_params=pltpu.CompilerParams(vmem_limit_bytes=24 * 1024 * 1024),
        cost_estimate=pl.CostEstimate(
            flops=2 * count * total * (depth + cols),
            bytes_accessed=2 * count * total,
            transcendentals=count * total,
        ),
    )(slot, *args)


def lane_block(shape, width, index):
    lane = lax.broadcasted_iota(jnp.int32, shape, len(shape) - 1)
    return (lane >= index * width) & (lane < (index + 1) * width)


def turned(x, lanes):
    lanes = lanes % LANES
    return pltpu.roll(x, lanes, 1) if lanes else x


def folded_sum(product, fold, strip, blocks):
    width = LANES // fold
    out = None
    for f in range(fold):
        total = None
        for r in blocks:
            row = (r * fold + f) * strip
            part = turned(product[row : row + strip, :], (f - r) * width)
            total = part if total is None else total + part
        out = total if out is None else jnp.where(lane_block(total.shape, width, f), total, out)
    return out


def first_step(matrix_ref, window_ref, sent_ref, low_ref, high_ref):
    strip = sent_ref.shape[1]
    fold = int(round((matrix_ref.shape[0] // strip) ** 0.5))
    product = jnp.dot(matrix_ref[...], window_ref[...], preferred_element_type=F32)
    low = folded_sum(product, fold, strip, range(fold // HALVES))
    high = folded_sum(product, fold, strip, range(fold // HALVES, fold))
    low_ref[...] = low
    high_ref[...] = high
    sent_ref[...] = jnp.broadcast_to(low.astype(BF)[None], sent_ref.shape)


def natural_product(matrix_ref, data_ref, rows_ref):
    parts, fold, strip, _ = rows_ref.shape
    data = data_ref[...].astype(F32).reshape(parts * strip, LANES)
    for f in range(fold):
        piece = turned(data, -f * (LANES // fold)).astype(BF)
        rows_ref[:, f] = piece.reshape(parts, strip, LANES)
    right = rows_ref[...].reshape(parts * fold * strip, LANES)
    return jnp.dot(matrix_ref[...].astype(BF), right, preferred_element_type=F32)


def middle_step(matrix_ref, data_ref, sent_ref, rows_ref):
    product = natural_product(matrix_ref, data_ref, rows_ref)
    _, fold, strip, _ = rows_ref.shape
    width = LANES // fold
    out = None
    for f in range(fold):
        part = turned(product[f * strip : (f + 1) * strip, :], f * width)
        out = part if out is None else jnp.where(lane_block(part.shape, width, f), part, out)
    sent_ref[...] = jnp.broadcast_to(out.astype(BF)[None], sent_ref.shape)


def last_step(panel_ref, matrix_ref, data_ref, low_ref, high_ref, out_ref, rows_ref):
    product = natural_product(matrix_ref, data_ref, rows_ref)
    _, fold, strip, _ = rows_ref.shape
    width = LANES // fold
    low = jnp.concatenate([turned(low_ref[...], -f * width) for f in range(fold)], axis=0)
    high = jnp.concatenate([turned(high_ref[...], -f * width) for f in range(fold)], axis=0)
    solved = jnp.where(panel_ref[0] == 0, low, high - product)
    out_ref[...] = solved.T[:width, :]


def panel_call(body, shape, matrix, parts, fold, data, *more, scalars=()):
    rows, depth = matrix.shape[0], parts * data.shape[0] // parts * fold
    strip = data.shape[0] // parts
    return pl.pallas_call(
        body,
        grid=(1,),
        out_shape=shape,
        in_specs=[pl.BlockSpec(memory_space=pltpu.SMEM)] * len(scalars)
        + [pl.BlockSpec((rows, depth), lambda i: (0, 0))]
        + [VMEM] * (1 + len(more)),
        out_specs=VMEM,
        scratch_shapes=[pltpu.VMEM((parts, fold, strip, LANES), BF)],
        compiler_params=pltpu.CompilerParams(vmem_limit_bytes=16 * 1024 * 1024),
    )(*scalars, matrix, data, *more)


def residual_step(shares_ref, targets_ref, weight_ref, sent_ref):
    predicted = jnp.sum(shares_ref[...].astype(F32), axis=0)
    residual = (weight_ref[...] * (predicted - targets_ref[...])).astype(BF)
    sent_ref[...] = jnp.broadcast_to(residual[None], sent_ref.shape)


def window_step(chosen_ref, residual_ref, window_ref):
    window = lax.dot_general(
        chosen_ref[...], residual_ref[...], (((0,), (0,)), ((), ())), preferred_element_type=F32
    )
    window_ref[...] = window.astype(window_ref.dtype)


def fold_step(group_ref, parts_ref, sent_ref):
    groups = parts_ref.shape[0]
    strip = sent_ref.shape[1]
    width = LANES // groups
    window = jnp.sum(parts_ref[...].astype(F32), axis=0)
    result = None
    for p in range(groups):
        out = None
        for r in range(window.shape[0] // strip):
            part = turned(window[r * strip : (r + 1) * strip, :], (r - p) * width)
            out = part if out is None else jnp.where(lane_block(part.shape, width, r), part, out)
        result = out if result is None else jnp.where(group_ref[0] == p, out, result)
    sent_ref[...] = jnp.broadcast_to(result.astype(BF)[None], sent_ref.shape)


def whole(body, shapes, *args, scalars=0):
    return pl.pallas_call(
        body,
        out_shape=shapes,
        in_specs=[pl.BlockSpec(memory_space=pltpu.SMEM)] * scalars + [VMEM] * (len(args) - scalars),
        out_specs=jax.tree.map(lambda _: VMEM, shapes),
        compiler_params=pltpu.CompilerParams(vmem_limit_bytes=16 * 1024 * 1024),
    )(*args)


def half_norm(rows):
    return 0.5 * jnp.sum(jnp.square(rows.astype(F32)), axis=-1)


def class_lookup(labels, table):
    classes = jnp.arange(table.shape[0], dtype=jnp.int32)
    return jnp.sum(jnp.where(labels[:, None] == classes[None, :], table[None, :], 0.0), axis=1)


def body(
    points,
    point_class,
    targets,
    class_weight,
    inv_scale,
    centers,
    coefficients,
    center_index,
    factor,
    panel_inverse,
):
    groups = lax.axis_size("pts")
    shards = lax.axis_size("ctr")
    shard = lax.axis_index("ctr")
    group = lax.axis_index("pts")
    own_points, depth = points.shape
    shard_rows = centers.shape[0]
    target_count = targets.shape[1]
    target_slice = target_count // groups
    own_rows = center_index.shape[0] // shards
    panel_rows = panel_inverse.shape[1]
    panel_shards = panel_rows // own_rows
    panel = shard // panel_shards
    fold = LANES // target_slice
    strip = own_rows // fold
    plane_size = shards // PLANES
    plane = shard // plane_size
    plane_points = plane_size * own_points

    plane_rows = exchanged(copies(points, plane_size), "ctr", PLANES)
    plane_rows = plane_rows.reshape(plane_points, depth)
    blocks = center_index.reshape(own_rows, shards)
    order = blocks[0] // shard_rows
    here = order == shard
    local = jnp.sum(jnp.where(here[None, :], blocks - shard * shard_rows, 0), axis=1)
    scale = inv_scale[None, :]
    scaled_centers, center_norm, chosen, extra = scaled_and_norm(centers, scale, local[:, None])
    plane_rows, extra = lax.optimization_barrier((plane_rows, extra))
    chunks = [plane_rows] + [None] * (PLANES - 1)
    for k in (2, 1, 3):
        chunks[k] = swapped(plane_rows, "ctr", k * plane_size)
    held = ()
    kernels = [None] * PLANES
    for k in (0, 2, 1, 3):
        slot = (plane ^ k).astype(jnp.int32).reshape(1)
        kernels[k], *held = kernel_and_value(
            slot, chunks[k], scale, scaled_centers, center_norm, coefficients, chosen, extra, *held
        )
    values, picked = held
    values, panel_inverse = lax.optimization_barrier((values, panel_inverse))

    place = (order[:, None] == jnp.arange(shards, dtype=jnp.int32)[None, :]).astype(BF)

    inverse = panel_inverse.astype(BF)
    count = panel_rows // (strip * shards)
    turned_inverse = jnp.einsum(
        "rhqj,js->hrsq", inverse.reshape(own_rows, count, strip, shards), place
    ).reshape(count * own_rows, shards * strip)

    weight = class_lookup(point_class, class_weight)[:, None]
    shares = exchanged(values.reshape(shards, own_points, target_count), "ctr")
    residual = whole(
        residual_step,
        jax.ShapeDtypeStruct((shards, own_points, target_count), BF),
        shares,
        targets,
        weight,
    )
    residual = exchanged(residual, "ctr").reshape(shards * own_points, target_count)

    index = group.astype(jnp.int32).reshape(1)
    window = whole(
        window_step,
        jax.ShapeDtypeStruct((own_rows, target_count), BF),
        picked.reshape(shards * own_points, own_rows),
        residual,
    )
    parts = lax.all_gather(window, "pts")
    sent = jax.ShapeDtypeStruct((shards, strip, LANES), BF)
    window = whole(fold_step, sent, index, parts, scalars=1)
    window, turned_inverse = lax.optimization_barrier((window, turned_inverse))
    other_inverse = swapped(turned_inverse, "ctr", panel_shards)
    other_inverse, residual = lax.optimization_barrier((other_inverse, residual))
    solve_rows = jnp.concatenate(
        [
            jnp.where(panel == 0, turned_inverse, other_inverse),
            jnp.where(panel == 0, other_inverse, turned_inverse),
        ],
        axis=0,
    )
    window = exchanged(window, "ctr")
    window = window.reshape(shards * strip, LANES)

    planes = residual.reshape(PLANES, plane_points, target_count)
    backward = None
    for k in range(PLANES):
        part = lax.dot_general(
            pick(planes, plane ^ k), kernels[k], (((0,), (0,)), ((), ())), preferred_element_type=F32
        )
        backward = part if backward is None else backward + part
    backward = backward.reshape(groups, target_slice, shard_rows)
    near_pair = jnp.stack([pick(backward, group), pick(backward, group ^ 2)])
    far_pair = jnp.stack([pick(backward, group ^ 1), pick(backward, group ^ 3)]).astype(BF)
    near_pair = near_pair + swapped(far_pair, "pts", 1).astype(F32)
    gradient = near_pair[0] + swapped(near_pair[1].astype(BF), "pts", 2).astype(F32)
    gradient = gradient.T

    half = shards // HALVES
    sent = jax.ShapeDtypeStruct((half, strip, LANES), BF)
    packed = jax.ShapeDtypeStruct((strip, LANES), F32)
    first, low, high = whole(first_step, (sent, packed, packed), solve_rows, window)
    first = exchanged(first, "ctr", HALVES).reshape(half * strip, LANES)
    update = panel_call(middle_step, sent, factor, half, fold, first)
    update = exchanged(update, "ctr", HALVES).reshape(half * strip, LANES)
    solved = panel_call(
        last_step,
        jax.ShapeDtypeStruct((target_slice, own_rows), F32),
        panel_inverse,
        half,
        fold,
        update,
        low,
        high,
        scalars=(panel.astype(jnp.int32).reshape(1),),
    )
    return (gradient, solved.T)


def solution(mesh):
    placed = (
        P(("pts", "ctr"), None),
        P(("pts", "ctr")),
        P(("pts", "ctr"), None),
        P(),
        P(),
        P("ctr", None),
        P("ctr", None),
        P(),
        P("ctr", None),
        P("ctr", None),
    )
    return jax.shard_map(
        body,
        mesh=mesh,
        in_specs=placed,
        out_specs=(P("ctr", "pts"), P("ctr", "pts")),
        check_vma=False,
    )
```
